32 devices in a mesh: grp: 2 (over y), rows: 8 (over z, x), diam: 2 (over core).
Axes of the slice: x: 2, y: 2, z: 4, core: 2. Of those that a mesh axis runs over, the one named last changes fastest.
Arguments:
- phi: bfloat16 [8192, 3200], P('rows', 'diam'), may hold values from -0.4375 to 0.4375
- loads: bfloat16 [8192, 512], P('rows'), may hold values from -1 to 1
- harm_diam: int32 [16], replicated, may hold values from 0 to 15
- mistuning: float32 [3200, 3200], P('diam', 'rows'), may hold values from -0.109375 to 0.109375
- dyn_diag: float32 [6400], P('grp'), parts along dimension 0, may hold values from 0.8 to 3
- blade_order: int32 [16], replicated, may hold values from 0 to 15, each once
Outputs:
- blades: bfloat16 [16, 64, 8192], P('diam', 'grp', 'rows'), parts along dimension 1
The draws below stay inside these ranges and needn't reach their ends.
There are 2 independent parts, one for each index of `grp`. The reference program is written for one: setup_inputs(seed, part) draws one part's arguments, and reference() takes and returns one part's arrays. A program takes and returns all parts, laid end to end along the dimension named above; an argument that names none is the same for every part. Nothing has to cross between parts.
Inputs may be any that keep to these rules, and one draw needn't show every extreme that they name: `blade_order`: each blade once.
All inputs are finite; a program needn't handle non-finite values.
Results may differ from the reference program's by a relative error of at most 0.013.
Values may be sent and summed in bfloat16 or wider, within the bound.
No kernel may reach another device: no remote copies, remote signals or barrier semaphores. Data moves between devices by JAX's collectives and lax.ppermute only.
A program may use at most 64 MiB of HBM per device.

```python
import math
import jax
import jax.numpy as jnp
from jax import lax

NBLADE = 16
MODES = 200
NHARM = 16
NCOL = 32
ITERS = 4
DOF = 8192
MODES_ALL = 3200


def with_ends(result, key, low, high):
    index_at = [jax.random.randint(jax.random.fold_in(key, axis), (), 0, length) for axis, length in enumerate(result.shape)]
    widest = result.shape.index(max(result.shape))
    next_to = index_at[:widest] + [(index_at[widest] + 1) % result.shape[widest]] + index_at[widest + 1:]
    return result.at[tuple(index_at)].set(low).at[tuple(next_to)].set(high)


def shard_levels(rng, dims, shards, least, high):
    factor_of = 1.0
    for axis_at, parts in shards:
        steps = jax.random.uniform(jax.random.fold_in(jax.random.fold_in(rng, 6), axis_at), (parts,), jnp.float32, least / len(shards), high / len(shards))
        factor_of = factor_of * jnp.repeat(jnp.exp(steps), dims[axis_at] // parts).reshape((-1,) + (1,) * (len(dims) - 1 - axis_at))
    return factor_of


def bell_draw(stream_key, dims, scale, bound, shards=(), dtype=jnp.bfloat16):
    gain = shard_levels(stream_key, dims, shards, -0.22, 0.18) if shards else 1.0
    result = jax.random.normal(stream_key, dims, jnp.float32) * scale * gain
    return jnp.minimum(jnp.maximum(result, -bound), bound).astype(dtype)


def setup_inputs(seed: int = 0, part: int = 0) -> dict:
    streams_of = jax.random.split(jax.random.key(seed), 7)
    own_keys = jax.random.split(jax.random.fold_in(streams_of[6], part), 7)
    return {
        "phi": bell_draw(streams_of[0], (DOF, MODES_ALL), MODES ** -0.5, 0.4375, ((0, 8), (1, 2))),
        "loads": bell_draw(streams_of[1], (DOF, NHARM * NCOL), (DOF // MODES) ** -0.5, 1.0, ((0, 8),)),
        "harm_diam": with_ends(jax.random.randint(streams_of[2], (NHARM,), 0, NBLADE), jax.random.fold_in(streams_of[2], 1), 0, NBLADE - 1).astype(jnp.int32),
        "mistuning": bell_draw(streams_of[3], (MODES_ALL, MODES_ALL), MODES_ALL ** -0.5, 0.109375, ((0, 2), (1, 8)), jnp.float32),
        "dyn_diag": jnp.clip(jnp.exp(jax.random.uniform(own_keys[4], (MODES_ALL,), jnp.float32, math.log(0.8), math.log(3.0))), 0.8, 3.0),
        "blade_order": jax.random.permutation(streams_of[5], NBLADE).astype(jnp.int32),
    }


def cyclic_rows(blade_order):
    count = NBLADE
    blade_pos = jnp.arange(count).astype(jnp.float32)[:, None]
    harmonic = jnp.arange(count)[None, :]
    half_count = count // 2
    wave = jnp.where(harmonic > half_count, harmonic - half_count, harmonic).astype(jnp.float32)
    angle = 2.0 * math.pi * wave * blade_pos / count
    scale = jnp.where((harmonic == 0) | (harmonic == half_count), 1.0 / math.sqrt(count), math.sqrt(2.0 / count))
    cyclic_tab = jnp.where(harmonic > half_count, jnp.sin(angle), jnp.cos(angle)) * scale
    onehot = (blade_order[:, None] == jnp.arange(count)[None, :]).astype(jnp.float32)
    return jnp.dot(onehot, cyclic_tab.astype(jnp.float32), precision=lax.Precision.HIGHEST)

def reference(phi, loads, harm_diam, mistuning, dyn_diag, blade_order):
    dof_rows = phi.shape[0]
    select = (harm_diam[:, None] == jnp.arange(NBLADE)[None, :]).astype(jnp.float32)
    loads_three = loads.reshape(dof_rows, NHARM, NCOL).astype(jnp.float32)
    combined = jnp.einsum('rkc,kh->rhc', loads_three, select).astype(jnp.bfloat16)
    pieces = []
    for diam in range(NBLADE):
        shape_cols = phi[:, diam * MODES:(diam + 1) * MODES]
        pieces.append(jnp.dot(shape_cols.T, combined[:, diam, :], preferred_element_type=jnp.float32))
    force = jnp.concatenate(pieces, axis=0)
    stiff = dyn_diag[:, None]
    amp = force / stiff
    for sweep in range(ITERS):
        amp = (force - jnp.dot(mistuning, amp, precision=lax.Precision.HIGHEST, preferred_element_type=jnp.float32)) / stiff
    amp_low = amp.astype(jnp.bfloat16)
    sectors = []
    for diam in range(NBLADE):
        shape_cols = phi[:, diam * MODES:(diam + 1) * MODES]
        response = jnp.dot(shape_cols, amp_low[diam * MODES:(diam + 1) * MODES], preferred_element_type=jnp.float32)
        sectors.append(response.astype(jnp.bfloat16).T)
    sector = jnp.stack(sectors, axis=0)
    table = cyclic_rows(blade_order)
    blades = jnp.einsum('sh,hcr->scr', table, sector.astype(jnp.float32), precision=lax.Precision.HIGHEST)
    return blades.astype(jnp.bfloat16)
```

```python
import math

import jax
import jax.numpy as jnp
from jax import lax
from jax.sharding import PartitionSpec as P

NBLADE = 16
MODES = 200
NHARM = 16
ITERS = 4
SWAP = [(0, 1), (1, 0)]
F32 = jnp.float32
BF16 = jnp.bfloat16


def cyclic_rows(blade_order):
    count = NBLADE
    blade_pos = jnp.arange(count).astype(jnp.float32)[:, None]
    harmonic = jnp.arange(count)[None, :]
    half_count = count // 2
    wave = jnp.where(harmonic > half_count, harmonic - half_count, harmonic).astype(jnp.float32)
    angle = 2.0 * math.pi * wave * blade_pos / count
    scale = jnp.where(
        (harmonic == 0) | (harmonic == half_count), 1.0 / math.sqrt(count), math.sqrt(2.0 / count)
    )
    cyclic_tab = jnp.where(harmonic > half_count, jnp.sin(angle), jnp.cos(angle)) * scale
    onehot = (blade_order[:, None] == jnp.arange(count)[None, :]).astype(jnp.float32)
    return jnp.dot(onehot, cyclic_tab, precision=lax.Precision.HIGHEST)


def general_plan(phi, loads, harm_diam, mistuning, dyn_diag, blade_order):
    rows_dev = phi.shape[0]
    half_modes = phi.shape[1]
    local_diam = half_modes // MODES
    columns = loads.shape[1] // NHARM
    col_width = mistuning.shape[1]
    diam_index = lax.axis_index("diam")
    row_index = lax.axis_index("rows")
    first_diam = diam_index * local_diam
    diam_ids = first_diam + jnp.arange(local_diam, dtype=jnp.int32)
    select = (harm_diam[:, None] == diam_ids[None, :]).astype(jnp.bfloat16)
    combined = jnp.einsum(
        "rkc,kh->rhc",
        loads.reshape(rows_dev, NHARM, columns),
        select,
        preferred_element_type=jnp.float32,
    ).astype(jnp.bfloat16)
    shapes = phi.reshape(rows_dev, local_diam, MODES)
    force_part = jnp.einsum(
        "rhm,rhc->hmc", shapes, combined, preferred_element_type=jnp.float32
    ).reshape(half_modes, columns)
    half_start = diam_index * half_modes
    dyn_half = lax.dynamic_slice_in_dim(dyn_diag, half_start, half_modes, 0)[:, None]

    def row_total(partial_term):
        return lax.psum(partial_term, "rows")

    force_half = row_total(force_part)
    amp_half = force_half / dyn_half
    for sweep in range(ITERS):
        full_amp = lax.all_gather(amp_half, "diam", axis=0, tiled=True)
        col_part = lax.dynamic_slice_in_dim(full_amp, row_index * col_width, col_width, 0)
        amp_half = (
            force_half
            - row_total(
                jnp.dot(
                    mistuning,
                    col_part,
                    precision=lax.Precision.HIGHEST,
                    preferred_element_type=jnp.float32,
                )
            )
        ) / dyn_half
    amp_low = amp_half.astype(jnp.bfloat16).reshape(local_diam, MODES, columns)
    sector = jnp.einsum("rhm,hmc->hcr", shapes, amp_low, preferred_element_type=jnp.float32).astype(
        jnp.bfloat16
    )
    table = cyclic_rows(blade_order)
    table_cols = lax.dynamic_slice_in_dim(table, first_diam, local_diam, 1)
    partial_value = jnp.einsum(
        "sh,hcr->scr", table_cols, sector.astype(jnp.float32), precision=lax.Precision.HIGHEST
    )
    blades = lax.psum_scatter(
        partial_value.astype(jnp.bfloat16), "diam", scatter_dimension=0, tiled=True
    )
    return blades


def by_parity(arr, parity):
    pairs = arr.reshape((arr.shape[0] // 2, 2) + arr.shape[1:])
    return jnp.where(parity == 0, pairs[:, 0], pairs[:, 1])


def chunk_plan(phi, loads, harm_diam, mistuning, dyn_diag, blade_order):
    rows_dev, half_modes = phi.shape
    local_diam = half_modes // MODES
    columns = loads.shape[1] // NHARM
    core = lax.axis_index("diam")
    own_diam = 2 * lax.axis_index("rows") + core
    first_diam = core * local_diam

    def other_core(value):
        return lax.ppermute(value, "diam", SWAP)

    def in_half_order(own, received):
        return jnp.where(
            core == 0, jnp.concatenate([own, received]), jnp.concatenate([received, own])
        )

    shapes = phi.T.reshape(local_diam, MODES, rows_dev)
    shapes_received = other_core(shapes)

    stiff = mistuning.T.reshape(2 * MODES, local_diam, MODES).transpose(1, 0, 2).astype(BF16)
    coupling = in_half_order(by_parity(stiff, core), other_core(by_parity(stiff, 1 - core)))
    coupling_own = jnp.where(core == 0, coupling[:, :MODES], coupling[:, MODES:])
    coupling_other = jnp.where(core == 0, coupling[:, MODES:], coupling[:, :MODES])

    diam_ids = first_diam + jnp.arange(local_diam, dtype=jnp.int32)
    select = (harm_diam[None, :] == diam_ids[:, None]).astype(BF16)
    spread = jnp.einsum("hk,cd->hckd", select, jnp.eye(columns, dtype=BF16)).reshape(
        local_diam * columns, NHARM * columns
    )
    combined = (
        jnp.einsum("ak,rk->ar", spread, loads, preferred_element_type=F32)
        .astype(BF16)
        .reshape(local_diam, columns, rows_dev)
    )
    force_part = jnp.einsum(
        "hcr,hmr->hcm", combined, shapes, preferred_element_type=F32
    ).astype(BF16)
    force_slots = in_half_order(
        by_parity(force_part, core), other_core(by_parity(force_part, 1 - core))
    )

    def row_total(slots):
        got = lax.all_to_all(slots, "rows", 0, 0, tiled=True)
        return jnp.sum(got.astype(F32), axis=0)

    dyn_own = lax.dynamic_slice_in_dim(dyn_diag, own_diam * MODES, MODES, 0)[None, :]
    force = row_total(force_slots)
    amp = force / dyn_own
    for sweep in range(ITERS):
        amp_low = amp.astype(BF16)
        amp_other = other_core(amp_low)
        part = jnp.einsum("cj,sjm->scm", amp_low, coupling_own, preferred_element_type=F32)
        part = part + jnp.einsum(
            "cj,sjm->scm", amp_other, coupling_other, preferred_element_type=F32
        )
        amp = (force - row_total(part.astype(BF16))) / dyn_own
    amp_low = amp.astype(BF16)
    same = lax.all_to_all(
        jnp.broadcast_to(amp_low[None], (local_diam,) + amp_low.shape), "rows", 0, 0, tiled=True
    )
    crossed = other_core(same)
    even = jnp.where(core == 0, same, crossed)
    odd = jnp.where(core == 0, crossed, same)
    amps = jnp.stack([even, odd], axis=1).reshape(NBLADE, columns, MODES)

    table = lax.dynamic_slice_in_dim(cyclic_rows(blade_order), first_diam, local_diam, 0)
    weights = (table.T[:, :, None, None] * amps.astype(F32)[:, None]).astype(BF16)
    weights = weights.reshape(2, local_diam, local_diam * columns, MODES)
    mine = jnp.where(core == 0, weights[0], weights[1])
    theirs = jnp.where(core == 0, weights[1], weights[0])
    blades = jnp.einsum("ham,hmr->ar", mine, shapes, preferred_element_type=F32) + jnp.einsum(
        "ham,hmr->ar", theirs, shapes_received, preferred_element_type=F32
    )
    return blades.astype(BF16).reshape(local_diam, columns, rows_dev)


def solution(mesh):
    placed = (P("rows", "diam"), P("rows", None), P(), P("diam", "rows"), P("grp"), P())
    one_each = mesh.shape["rows"] * 2 == NBLADE and mesh.shape["diam"] == 2
    return jax.shard_map(
        chunk_plan if one_each else general_plan,
        mesh=mesh,
        in_specs=placed,
        out_specs=P("diam", "grp", "rows"),
        check_vma=False,
    )
```

```python
import functools
import math

import jax
import jax.numpy as jnp
from jax import lax
from jax.experimental import pallas as pl
from jax.experimental.pallas import tpu as pltpu
from jax.sharding import PartitionSpec as P

NBLADE = 16
MODES = 200
NHARM = 16
ITERS = 4
SWAP = [(0, 1), (1, 0)]
F32 = jnp.float32
BF16 = jnp.bfloat16


def cyclic_rows(blade_order):
    count = NBLADE
    blade_pos = jnp.arange(count).astype(jnp.float32)[:, None]
    harmonic = jnp.arange(count)[None, :]
    half_count = count // 2
    wave = jnp.where(harmonic > half_count, harmonic - half_count, harmonic).astype(jnp.float32)
    angle = 2.0 * math.pi * wave * blade_pos / count
    scale = jnp.where(
        (harmonic == 0) | (harmonic == half_count), 1.0 / math.sqrt(count), math.sqrt(2.0 / count)
    )
    cyclic_tab = jnp.where(harmonic > half_count, jnp.sin(angle), jnp.cos(angle)) * scale
    onehot = (blade_order[:, None] == jnp.arange(count)[None, :]).astype(jnp.float32)
    return jnp.dot(onehot, cyclic_tab, precision=lax.Precision.HIGHEST)


def general_plan(phi, loads, harm_diam, mistuning, dyn_diag, blade_order):
    rows_dev = phi.shape[0]
    half_modes = phi.shape[1]
    local_diam = half_modes // MODES
    columns = loads.shape[1] // NHARM
    col_width = mistuning.shape[1]
    diam_index = lax.axis_index("diam")
    row_index = lax.axis_index("rows")
    first_diam = diam_index * local_diam
    diam_ids = first_diam + jnp.arange(local_diam, dtype=jnp.int32)
    select = (harm_diam[:, None] == diam_ids[None, :]).astype(jnp.bfloat16)
    combined = jnp.einsum(
        "rkc,kh->rhc",
        loads.reshape(rows_dev, NHARM, columns),
        select,
        preferred_element_type=jnp.float32,
    ).astype(jnp.bfloat16)
    shapes = phi.reshape(rows_dev, local_diam, MODES)
    force_part = jnp.einsum(
        "rhm,rhc->hmc", shapes, combined, preferred_element_type=jnp.float32
    ).reshape(half_modes, columns)
    half_start = diam_index * half_modes
    dyn_half = lax.dynamic_slice_in_dim(dyn_diag, half_start, half_modes, 0)[:, None]

    def row_total(partial_term):
        return lax.psum(partial_term, "rows")

    force_half = row_total(force_part)
    amp_half = force_half / dyn_half
    for sweep in range(ITERS):
        full_amp = lax.all_gather(amp_half, "diam", axis=0, tiled=True)
        col_part = lax.dynamic_slice_in_dim(full_amp, row_index * col_width, col_width, 0)
        amp_half = (
            force_half
            - row_total(
                jnp.dot(
                    mistuning,
                    col_part,
                    precision=lax.Precision.HIGHEST,
                    preferred_element_type=jnp.float32,
                )
            )
        ) / dyn_half
    amp_low = amp_half.astype(jnp.bfloat16).reshape(local_diam, MODES, columns)
    sector = jnp.einsum("rhm,hmc->hcr", shapes, amp_low, preferred_element_type=jnp.float32).astype(
        jnp.bfloat16
    )
    table = cyclic_rows(blade_order)
    table_cols = lax.dynamic_slice_in_dim(table, first_diam, local_diam, 1)
    partial_value = jnp.einsum(
        "sh,hcr->scr", table_cols, sector.astype(jnp.float32), precision=lax.Precision.HIGHEST
    )
    blades = lax.psum_scatter(
        partial_value.astype(jnp.bfloat16), "diam", scatter_dimension=0, tiled=True
    )
    return blades


VMEM = pl.BlockSpec(memory_space=pltpu.VMEM)
SMEM = pl.BlockSpec(memory_space=pltpu.SMEM)
HBM = pl.BlockSpec(memory_space=pltpu.HBM)
LIMIT = pltpu.CompilerParams(vmem_limit_bytes=24 << 20)


def nt_dot(left, right):
    return lax.dot_general(left, right, (((1,), (1,)), ((), ())), preferred_element_type=F32)


def pick(core, even, odd):
    return jnp.where(core == 0, even, odd)


def force_kernel(columns, core_ref, harm_ref, loads_hbm, phi_hbm, mine_ref, send_ref, loads_ref, phi_ref, combined_ref, load_sem, phi_sem):
    core = core_ref[0]
    local_diam = phi_ref.shape[0]
    load_copy = pltpu.make_async_copy(loads_hbm, loads_ref, load_sem)
    load_copy.start()
    copies = [
        pltpu.make_async_copy(phi_hbm.at[k], phi_ref.at[k], phi_sem.at[k])
        for k in range(local_diam)
    ]
    for copy in copies:
        copy.start()
    shape = (local_diam * columns, loads_ref.shape[1])
    row = lax.broadcasted_iota(jnp.int32, shape, 0)
    col = lax.broadcasted_iota(jnp.int32, shape, 1)
    harmonic = col // columns
    excited = jnp.zeros(shape, jnp.int32)
    for k in range(NHARM):
        excited = jnp.where(harmonic == k, harm_ref[k], excited)
    hit = (row % columns == col % columns) & (excited == row // columns + core * local_diam)
    spread = jnp.where(hit, 1.0, 0.0).astype(BF16)
    load_copy.wait()
    combined_ref[...] = nt_dot(spread, loads_ref[...]).astype(BF16)
    for k in range(0, local_diam, 2):
        part = []
        for at in (k, k + 1):
            copies[at].wait()
            part.append(nt_dot(combined_ref[at * columns : (at + 1) * columns], phi_ref[at]))
        mine_ref[k // 2] = pick(core, part[0], part[1]).astype(BF16)
        send_ref[k // 2] = pick(core, part[1], part[0]).astype(BF16)


def regroup_kernel(core_ref, stiff_ref, keep_ref, send_ref):
    core = core_ref[0]
    for k in range(0, 2 * keep_ref.shape[1], 2):
        for chunk in range(2):
            pair = [
                stiff_ref[chunk * MODES : (chunk + 1) * MODES, (k + odd) * MODES : (k + odd + 1) * MODES]
                for odd in range(2)
            ]
            keep_ref[pick(core, chunk, 1 - chunk), k // 2] = pick(core, pair[0], pair[1]).astype(BF16)
            send_ref[pick(core, 1 - chunk, chunk), k // 2] = pick(core, pair[1], pair[0]).astype(BF16)


def product_kernel(source, core_ref, amp_ref, keep_ref, recv_ref, *rest):
    prev_ref, out_ref = rest if len(rest) == 2 else (None, rest[0])
    core = core_ref[0]
    slots = keep_ref.shape[1]
    for half, ref in ((core, keep_ref), (1 - core, recv_ref)):
        for k in range(slots):
            at = half * slots + k
            value = jnp.dot(amp_ref[...], ref[source, k], preferred_element_type=F32)
            if prev_ref is not None:
                value = value + prev_ref[at]
            out_ref[at] = value.astype(out_ref.dtype)


def blades_kernel(crossed, core_ref, table_ref, amp_ref, own_ref, recv_ref, *rest):
    prev_ref, out_ref = rest if len(rest) == 2 else (None, rest[0])
    core = core_ref[0]
    local_diam, columns, _ = amp_ref.shape
    half_count = local_diam // 2
    odd = 1 - core if crossed else core
    total = None
    for half, ref in ((core, own_ref), (1 - core, recv_ref)):
        for k in range(half_count):
            at = half * half_count + k
            amp = amp_ref[at].astype(F32)
            weights = jnp.concatenate(
                [(table_ref[s, 2 * at + odd] * amp).astype(BF16) for s in range(local_diam)]
            )
            value = jnp.dot(weights, ref[2 * k + odd], preferred_element_type=F32)
            total = value if total is None else total + value
    total = total.reshape(out_ref.shape)
    if prev_ref is not None:
        total = total + prev_ref[...]
    out_ref[...] = total.astype(out_ref.dtype)


def chunk_plan(phi, loads, harm_diam, mistuning, dyn_diag, blade_order):
    rows_dev, half_modes = phi.shape
    local_diam = half_modes // MODES
    columns = loads.shape[1] // NHARM
    core = lax.axis_index("diam")
    own_diam = 2 * lax.axis_index("rows") + core
    first_diam = core * local_diam
    core_arg = core.reshape(1).astype(jnp.int32)
    pairs = local_diam // 2

    def other_core(value):
        return lax.ppermute(value, "diam", SWAP)

    def in_half_order(own, received):
        return jnp.where(
            core == 0, jnp.concatenate([own, received]), jnp.concatenate([received, own])
        )

    def exchange(slots):
        return lax.all_to_all(slots, "rows", 0, 0, tiled=True)

    def row_total(got):
        return jnp.sum(got.astype(F32), axis=0)

    half_slots = jax.ShapeDtypeStruct((pairs, columns, MODES), BF16)
    shapes = phi.T.reshape(local_diam, MODES, rows_dev)
    mine, send = pl.pallas_call(
        functools.partial(force_kernel, columns),
        name="force",
        in_specs=[SMEM, SMEM, HBM, HBM],
        out_specs=[VMEM, VMEM],
        out_shape=[half_slots, half_slots],
        scratch_shapes=[
            pltpu.VMEM(loads.shape, BF16),
            pltpu.VMEM(shapes.shape, BF16),
            pltpu.VMEM((local_diam * columns, rows_dev), BF16),
            pltpu.SemaphoreType.DMA,
            pltpu.SemaphoreType.DMA((local_diam,)),
        ],
        compiler_params=pltpu.CompilerParams(vmem_limit_bytes=60 << 20),
    )(core_arg, harm_diam, loads, shapes)
    force_slots = in_half_order(mine, other_core(send))
    force_slots, stiff, order, shapes_sent = lax.optimization_barrier(
        (force_slots, mistuning.T, blade_order, shapes)
    )
    force_got = exchange(force_slots)

    group = jax.ShapeDtypeStruct((2, pairs, MODES, MODES), BF16)
    keep, sent = pl.pallas_call(
        regroup_kernel,
        name="regroup",
        in_specs=[SMEM, VMEM],
        out_specs=[VMEM, VMEM],
        out_shape=[group, group],
        compiler_params=LIMIT,
        cost_estimate=pl.CostEstimate(
            flops=2 * mistuning.size, bytes_accessed=8 * mistuning.size, transcendentals=0
        ),
    )(core_arg, stiff)
    recv = other_core(sent)
    shapes_received = other_core(shapes_sent)
    table = lax.dynamic_slice_in_dim(cyclic_rows(order), first_diam, local_diam, 0)
    dyn_own = lax.dynamic_slice_in_dim(dyn_diag, own_diam * MODES, MODES, 0)[None, :]
    force_got, keep, table, dyn_own = lax.optimization_barrier((force_got, keep, table, dyn_own))

    slots_shape = (local_diam, columns, MODES)

    def product(source, *operands):
        return pl.pallas_call(
            functools.partial(product_kernel, source),
            name="product",
            in_specs=[SMEM] + [VMEM] * len(operands),
            out_specs=VMEM,
            out_shape=jax.ShapeDtypeStruct(slots_shape, BF16 if source else F32),
            compiler_params=LIMIT,
        )(core_arg, *operands)

    force = row_total(force_got)
    amp = force / dyn_own
    for sweep in range(ITERS):
        amp_low = amp.astype(BF16)
        amp_other = other_core(amp_low)
        part = product(0, amp_low, keep, recv)
        part, amp_other = lax.optimization_barrier((part, amp_other))
        part = product(1, amp_other, keep, recv, part)
        amp = (force - row_total(exchange(part))) / dyn_own
        if sweep == 0:
            amp, shapes_received = lax.optimization_barrier((amp, shapes_received))
    same = exchange(jnp.broadcast_to(amp.astype(BF16)[None], slots_shape))
    crossed = other_core(same)

    def blades(is_crossed, amps, *prev):
        return pl.pallas_call(
            functools.partial(blades_kernel, is_crossed),
            name="blades",
            in_specs=[SMEM, SMEM] + [VMEM] * (3 + len(prev)),
            out_specs=VMEM,
            out_shape=jax.ShapeDtypeStruct(
                (local_diam, columns, rows_dev), BF16 if is_crossed else F32
            ),
            compiler_params=LIMIT,
            cost_estimate=pl.CostEstimate(
                flops=2 * local_diam * columns * phi.size,
                bytes_accessed=4 * phi.size,
                transcendentals=0,
            ),
        )(core_arg, table, amps, shapes, shapes_received, *prev)

    part = blades(False, same)
    part, crossed = lax.optimization_barrier((part, crossed))
    return blades(True, crossed, part)


def solution(mesh):
    placed = (P("rows", "diam"), P("rows", None), P(), P("diam", "rows"), P("grp"), P())
    one_each = mesh.shape["rows"] * 2 == NBLADE and mesh.shape["diam"] == 2
    return jax.shard_map(
        chunk_plan if one_each else general_plan,
        mesh=mesh,
        in_specs=placed,
        out_specs=P("diam", "grp", "rows"),
        check_vma=False,
    )
```

```python
import functools
import math

import jax
import jax.numpy as jnp
from jax import lax
from jax.experimental import pallas as pl
from jax.experimental.pallas import tpu as pltpu
from jax.sharding import PartitionSpec as P

NBLADE = 16
MODES = 200
NHARM = 16
ITERS = 4
SWAP = [(0, 1), (1, 0)]
F32 = jnp.float32
BF16 = jnp.bfloat16


def cyclic_rows(blade_order):
    count = NBLADE
    blade_pos = jnp.arange(count).astype(jnp.float32)[:, None]
    harmonic = jnp.arange(count)[None, :]
    half_count = count // 2
    wave = jnp.where(harmonic > half_count, harmonic - half_count, harmonic).astype(jnp.float32)
    angle = 2.0 * math.pi * wave * blade_pos / count
    scale = jnp.where(
        (harmonic == 0) | (harmonic == half_count), 1.0 / math.sqrt(count), math.sqrt(2.0 / count)
    )
    cyclic_tab = jnp.where(harmonic > half_count, jnp.sin(angle), jnp.cos(angle)) * scale
    onehot = (blade_order[:, None] == jnp.arange(count)[None, :]).astype(jnp.float32)
    return jnp.dot(onehot, cyclic_tab, precision=lax.Precision.HIGHEST)


def general_plan(phi, loads, harm_diam, mistuning, dyn_diag, blade_order):
    rows_dev = phi.shape[0]
    half_modes = phi.shape[1]
    local_diam = half_modes // MODES
    columns = loads.shape[1] // NHARM
    col_width = mistuning.shape[1]
    diam_index = lax.axis_index("diam")
    row_index = lax.axis_index("rows")
    first_diam = diam_index * local_diam
    diam_ids = first_diam + jnp.arange(local_diam, dtype=jnp.int32)
    select = (harm_diam[:, None] == diam_ids[None, :]).astype(jnp.bfloat16)
    combined = jnp.einsum(
        "rkc,kh->rhc",
        loads.reshape(rows_dev, NHARM, columns),
        select,
        preferred_element_type=jnp.float32,
    ).astype(jnp.bfloat16)
    shapes = phi.reshape(rows_dev, local_diam, MODES)
    force_part = jnp.einsum(
        "rhm,rhc->hmc", shapes, combined, preferred_element_type=jnp.float32
    ).reshape(half_modes, columns)
    half_start = diam_index * half_modes
    dyn_half = lax.dynamic_slice_in_dim(dyn_diag, half_start, half_modes, 0)[:, None]

    def row_total(partial_term):
        return lax.psum(partial_term, "rows")

    force_half = row_total(force_part)
    amp_half = force_half / dyn_half
    for sweep in range(ITERS):
        full_amp = lax.all_gather(amp_half, "diam", axis=0, tiled=True)
        col_part = lax.dynamic_slice_in_dim(full_amp, row_index * col_width, col_width, 0)
        amp_half = (
            force_half
            - row_total(
                jnp.dot(
                    mistuning,
                    col_part,
                    precision=lax.Precision.HIGHEST,
                    preferred_element_type=jnp.float32,
                )
            )
        ) / dyn_half
    amp_low = amp_half.astype(jnp.bfloat16).reshape(local_diam, MODES, columns)
    sector = jnp.einsum("rhm,hmc->hcr", shapes, amp_low, preferred_element_type=jnp.float32).astype(
        jnp.bfloat16
    )
    table = cyclic_rows(blade_order)
    table_cols = lax.dynamic_slice_in_dim(table, first_diam, local_diam, 1)
    partial_value = jnp.einsum(
        "sh,hcr->scr", table_cols, sector.astype(jnp.float32), precision=lax.Precision.HIGHEST
    )
    blades = lax.psum_scatter(
        partial_value.astype(jnp.bfloat16), "diam", scatter_dimension=0, tiled=True
    )
    return blades


def by_parity(arr, parity):
    pairs = arr.reshape((arr.shape[0] // 2, 2) + arr.shape[1:])
    return jnp.where(parity == 0, pairs[:, 0], pairs[:, 1])


VMEM = pl.BlockSpec(memory_space=pltpu.VMEM)
SMEM = pl.BlockSpec(memory_space=pltpu.SMEM)
HBM = pl.BlockSpec(memory_space=pltpu.HBM)
LIMIT = pltpu.CompilerParams(vmem_limit_bytes=8 << 20)


def pick(core, even, odd):
    return jnp.where(core == 0, even, odd)


def load_kernel(columns, core_ref, harm_ref, loads_ref, phi_hbm, combined_ref, phi_ref, phi_sem):
    local_diam = phi_ref.shape[0]
    phi_copy = pltpu.make_async_copy(phi_hbm, phi_ref, phi_sem)
    phi_copy.start()
    wide = loads_ref.shape[1]
    first_diam = core_ref[0] * local_diam
    col = lax.broadcasted_iota(jnp.int32, (8, wide), 1)
    key = jnp.zeros((8, wide), jnp.int32)
    for k in range(NHARM):
        inside = (col >= k * columns) & (col < (k + 1) * columns)
        key = jnp.where(inside, (harm_ref[k] - first_diam - k) * columns + col, key)
    shape = (local_diam * columns, wide)
    row = lax.broadcasted_iota(jnp.int32, shape, 0)
    spread = jnp.where(row == jnp.broadcast_to(key[0:1], shape), 1.0, 0.0).astype(BF16)
    combined = lax.dot_general(
        spread, loads_ref[...], (((1,), (1,)), ((), ())), preferred_element_type=F32
    )
    combined_ref[...] = combined.astype(BF16).reshape(combined_ref.shape)
    phi_copy.wait()


def fetch_kernel(own_hbm, recv_hbm, both_ref, sems):
    half = own_hbm.shape[0]
    copies = [
        pltpu.make_async_copy(own_hbm, both_ref.at[:half], sems.at[0]),
        pltpu.make_async_copy(recv_hbm, both_ref.at[half:], sems.at[1]),
    ]
    for copy in copies:
        copy.start()
    for copy in copies:
        copy.wait()


def regroup_kernel(core_ref, stiff_ref, keep_ref, send_ref):
    core = core_ref[0]
    for k in range(0, 2 * keep_ref.shape[1], 2):
        for chunk in range(2):
            pair = [
                stiff_ref[chunk * MODES : (chunk + 1) * MODES, (k + odd) * MODES : (k + odd + 1) * MODES]
                for odd in range(2)
            ]
            keep_ref[pick(core, chunk, 1 - chunk), k // 2] = pick(core, pair[0], pair[1]).astype(BF16)
            send_ref[pick(core, 1 - chunk, chunk), k // 2] = pick(core, pair[1], pair[0]).astype(BF16)


def product_kernel(source, core_ref, amp_ref, keep_ref, recv_ref, *rest):
    prev_ref, out_ref = rest if len(rest) == 2 else (None, rest[0])
    core = core_ref[0]
    slots = keep_ref.shape[1]
    for half, ref in ((core, keep_ref), (1 - core, recv_ref)):
        for k in range(slots):
            at = half * slots + k
            value = jnp.dot(amp_ref[...], ref[source, k], preferred_element_type=F32)
            if prev_ref is not None:
                value = value + prev_ref[at]
            out_ref[at] = value.astype(out_ref.dtype)


def weights_kernel(core_ref, table_ref, same_ref, crossed_ref, out_ref):
    core = core_ref[0]
    local_diam, columns, _ = same_ref.shape
    half_count = local_diam // 2
    for at_half, half in enumerate((core, 1 - core)):
        for k in range(half_count):
            at = half * half_count + k
            for odd, amp_ref in ((core, same_ref), (1 - core, crossed_ref)):
                amp = amp_ref[at].astype(F32)
                for s in range(local_diam):
                    value = table_ref[s, 2 * at + odd] * amp
                    place = at_half * local_diam + 2 * k + odd
                    out_ref[place, s * columns : (s + 1) * columns] = value.astype(BF16)


def chunk_plan(phi, loads, harm_diam, mistuning, dyn_diag, blade_order):
    rows_dev, half_modes = phi.shape
    local_diam = half_modes // MODES
    columns = loads.shape[1] // NHARM
    core = lax.axis_index("diam")
    own_diam = 2 * lax.axis_index("rows") + core
    first_diam = core * local_diam
    core_arg = core.reshape(1).astype(jnp.int32)
    pairs = local_diam // 2

    def other_core(value):
        return lax.ppermute(value, "diam", SWAP)

    def in_half_order(own, received):
        return jnp.where(
            core == 0, jnp.concatenate([own, received]), jnp.concatenate([received, own])
        )

    def exchange(slots):
        return lax.all_to_all(slots, "rows", 0, 0, tiled=True)

    def row_total(got):
        return jnp.sum(got.astype(F32), axis=0)

    shapes = phi.T.reshape(local_diam, MODES, rows_dev)
    shape_sized = jax.ShapeDtypeStruct(shapes.shape, BF16)
    combined, shapes_near = pl.pallas_call(
        functools.partial(load_kernel, columns),
        name="load",
        in_specs=[SMEM, SMEM, VMEM, HBM],
        out_specs=[VMEM, VMEM],
        out_shape=[
            jax.ShapeDtypeStruct((local_diam, columns, rows_dev), BF16),
            shape_sized,
        ],
        scratch_shapes=[pltpu.SemaphoreType.DMA],
        compiler_params=LIMIT,
    )(core_arg, harm_diam, loads, shapes)
    force_part = jnp.einsum(
        "hcr,hmr->hcm", combined, shapes_near, preferred_element_type=F32
    ).astype(BF16)
    force_slots = in_half_order(
        by_parity(force_part, core), other_core(by_parity(force_part, 1 - core))
    )
    force_slots, stiff, order, shapes_sent, dyn_diag = lax.optimization_barrier(
        (force_slots, mistuning.T, blade_order, shapes, dyn_diag)
    )
    force_got = exchange(force_slots)

    group = jax.ShapeDtypeStruct((2, pairs, MODES, MODES), BF16)
    keep, sent = pl.pallas_call(
        regroup_kernel,
        name="regroup",
        in_specs=[SMEM, VMEM],
        out_specs=[VMEM, VMEM],
        out_shape=[group, group],
        compiler_params=LIMIT,
        cost_estimate=pl.CostEstimate(
            flops=2 * mistuning.size, bytes_accessed=8 * mistuning.size, transcendentals=0
        ),
    )(core_arg, stiff)
    recv = other_core(sent)
    shapes_received = other_core(shapes_sent)
    table = lax.dynamic_slice_in_dim(cyclic_rows(order), first_diam, local_diam, 0)
    dyn_own = lax.dynamic_slice_in_dim(dyn_diag, own_diam * MODES, MODES, 0)[None, :]
    force_got, keep, table, dyn_own = lax.optimization_barrier((force_got, keep, table, dyn_own))

    slots_shape = (local_diam, columns, MODES)

    def product(source, *operands):
        return pl.pallas_call(
            functools.partial(product_kernel, source),
            name="product",
            in_specs=[SMEM] + [VMEM] * len(operands),
            out_specs=VMEM,
            out_shape=jax.ShapeDtypeStruct(slots_shape, BF16 if source else F32),
            compiler_params=LIMIT,
        )(core_arg, *operands)

    force = row_total(force_got)
    amp = force / dyn_own
    for sweep in range(ITERS):
        amp_low = amp.astype(BF16)
        amp_other = other_core(amp_low)
        part = product(0, amp_low, keep, recv)
        part, amp_other = lax.optimization_barrier((part, amp_other))
        part = product(1, amp_other, keep, recv, part)
        amp = (force - row_total(exchange(part))) / dyn_own
        if sweep == 0:
            amp, shapes_received = lax.optimization_barrier((amp, shapes_received))
    amp, own_hbm, recv_hbm = lax.optimization_barrier((amp, shapes, shapes_received))
    same = exchange(jnp.broadcast_to(amp.astype(BF16)[None], slots_shape))
    shapes_both = pl.pallas_call(
        fetch_kernel,
        name="fetch",
        in_specs=[HBM, HBM],
        out_specs=VMEM,
        out_shape=jax.ShapeDtypeStruct((NBLADE, MODES, rows_dev), BF16),
        scratch_shapes=[pltpu.SemaphoreType.DMA((2,))],
        compiler_params=LIMIT,
        cost_estimate=pl.CostEstimate(
            flops=0, bytes_accessed=8 * phi.size, transcendentals=0
        ),
    )(own_hbm, recv_hbm)
    same, shapes_both = lax.optimization_barrier((same, shapes_both))
    crossed = other_core(same)
    weights = pl.pallas_call(
        weights_kernel,
        name="weights",
        in_specs=[SMEM, SMEM, VMEM, VMEM],
        out_specs=VMEM,
        out_shape=jax.ShapeDtypeStruct((NBLADE, local_diam * columns, MODES), BF16),
        compiler_params=LIMIT,
    )(core_arg, table, same, crossed)
    blades = jnp.einsum("ham,hmr->ar", weights, shapes_both, preferred_element_type=F32)
    return blades.astype(BF16).reshape(local_diam, columns, rows_dev)


def solution(mesh):
    placed = (P("rows", "diam"), P("rows", None), P(), P("diam", "rows"), P("grp"), P())
    one_each = mesh.shape["rows"] * 2 == NBLADE and mesh.shape["diam"] == 2
    return jax.shard_map(
        chunk_plan if one_each else general_plan,
        mesh=mesh,
        in_specs=placed,
        out_specs=P("diam", "grp", "rows"),
        check_vma=False,
    )
```

```python
import functools
import math

import jax
import jax.numpy as jnp
from jax import lax
from jax.experimental import pallas as pl
from jax.experimental.pallas import tpu as pltpu
from jax.sharding import PartitionSpec as P

NBLADE = 16
MODES = 200
NHARM = 16
ITERS = 4
SWAP = [(0, 1), (1, 0)]
F32 = jnp.float32
BF16 = jnp.bfloat16


def cyclic_rows(blade_order):
    count = NBLADE
    blade_pos = jnp.arange(count).astype(jnp.float32)[:, None]
    harmonic = jnp.arange(count)[None, :]
    half_count = count // 2
    wave = jnp.where(harmonic > half_count, harmonic - half_count, harmonic).astype(jnp.float32)
    angle = 2.0 * math.pi * wave * blade_pos / count
    scale = jnp.where(
        (harmonic == 0) | (harmonic == half_count), 1.0 / math.sqrt(count), math.sqrt(2.0 / count)
    )
    cyclic_tab = jnp.where(harmonic > half_count, jnp.sin(angle), jnp.cos(angle)) * scale
    onehot = (blade_order[:, None] == jnp.arange(count)[None, :]).astype(jnp.float32)
    return jnp.dot(onehot, cyclic_tab, precision=lax.Precision.HIGHEST)


def general_plan(phi, loads, harm_diam, mistuning, dyn_diag, blade_order):
    rows_dev = phi.shape[0]
    half_modes = phi.shape[1]
    local_diam = half_modes // MODES
    columns = loads.shape[1] // NHARM
    col_width = mistuning.shape[1]
    diam_index = lax.axis_index("diam")
    row_index = lax.axis_index("rows")
    first_diam = diam_index * local_diam
    diam_ids = first_diam + jnp.arange(local_diam, dtype=jnp.int32)
    select = (harm_diam[:, None] == diam_ids[None, :]).astype(jnp.bfloat16)
    combined = jnp.einsum(
        "rkc,kh->rhc",
        loads.reshape(rows_dev, NHARM, columns),
        select,
        preferred_element_type=jnp.float32,
    ).astype(jnp.bfloat16)
    shapes = phi.reshape(rows_dev, local_diam, MODES)
    force_part = jnp.einsum(
        "rhm,rhc->hmc", shapes, combined, preferred_element_type=jnp.float32
    ).reshape(half_modes, columns)
    half_start = diam_index * half_modes
    dyn_half = lax.dynamic_slice_in_dim(dyn_diag, half_start, half_modes, 0)[:, None]

    def row_total(partial_term):
        return lax.psum(partial_term, "rows")

    force_half = row_total(force_part)
    amp_half = force_half / dyn_half
    for sweep in range(ITERS):
        full_amp = lax.all_gather(amp_half, "diam", axis=0, tiled=True)
        col_part = lax.dynamic_slice_in_dim(full_amp, row_index * col_width, col_width, 0)
        amp_half = (
            force_half
            - row_total(
                jnp.dot(
                    mistuning,
                    col_part,
                    precision=lax.Precision.HIGHEST,
                    preferred_element_type=jnp.float32,
                )
            )
        ) / dyn_half
    amp_low = amp_half.astype(jnp.bfloat16).reshape(local_diam, MODES, columns)
    sector = jnp.einsum("rhm,hmc->hcr", shapes, amp_low, preferred_element_type=jnp.float32).astype(
        jnp.bfloat16
    )
    table = cyclic_rows(blade_order)
    table_cols = lax.dynamic_slice_in_dim(table, first_diam, local_diam, 1)
    partial_value = jnp.einsum(
        "sh,hcr->scr", table_cols, sector.astype(jnp.float32), precision=lax.Precision.HIGHEST
    )
    blades = lax.psum_scatter(
        partial_value.astype(jnp.bfloat16), "diam", scatter_dimension=0, tiled=True
    )
    return blades


def by_parity(arr, parity):
    pairs = arr.reshape((arr.shape[0] // 2, 2) + arr.shape[1:])
    return jnp.where(parity == 0, pairs[:, 0], pairs[:, 1])


VMEM = pl.BlockSpec(memory_space=pltpu.VMEM)
SMEM = pl.BlockSpec(memory_space=pltpu.SMEM)
HBM = pl.BlockSpec(memory_space=pltpu.HBM)
WIDE = pltpu.CompilerParams(vmem_limit_bytes=16 << 20)
LIMIT = pltpu.CompilerParams(vmem_limit_bytes=8 << 20)


def in_hbm(*values):
    return [pltpu.with_memory_space_constraint(value, pltpu.HBM) for value in values]


def pick(core, even, odd):
    return jnp.where(core == 0, even, odd)


def load_kernel(columns, core_ref, harm_hbm, loads_hbm, phi_hbm, combined_ref, phi_ref, harm_ref, loads_ref, sems):
    local_diam = phi_ref.shape[0]
    harm_copy = pltpu.make_async_copy(harm_hbm, harm_ref, sems.at[0])
    harm_copy.start()
    load_copy = pltpu.make_async_copy(loads_hbm, loads_ref, sems.at[1])
    load_copy.start()
    phi_copy = pltpu.make_async_copy(phi_hbm, phi_ref, sems.at[2])
    phi_copy.start()
    harm_copy.wait()
    wide = loads_ref.shape[1]
    first_diam = core_ref[0] * local_diam
    col = lax.broadcasted_iota(jnp.int32, (8, wide), 1)
    key = jnp.zeros((8, wide), jnp.int32)
    for k in range(NHARM):
        inside = (col >= k * columns) & (col < (k + 1) * columns)
        key = jnp.where(inside, (harm_ref[k] - first_diam - k) * columns + col, key)
    shape = (local_diam * columns, wide)
    row = lax.broadcasted_iota(jnp.int32, shape, 0)
    spread = jnp.where(row == jnp.broadcast_to(key[0:1], shape), 1.0, 0.0).astype(BF16)
    load_copy.wait()
    combined = lax.dot_general(
        spread, loads_ref[...], (((1,), (1,)), ((), ())), preferred_element_type=F32
    )
    combined_ref[...] = combined.astype(BF16).reshape(combined_ref.shape)
    phi_copy.wait()


def parity_copies(odd, own_hbm, recv_hbm, near_ref, sems):
    pairs = own_hbm.shape[0] // 2
    return [
        pltpu.make_async_copy(
            ref.at[2 * k + odd], near_ref.at[at_half * pairs + k], sems.at[at_half * pairs + k]
        )
        for at_half, ref in enumerate((own_hbm, recv_hbm))
        for k in range(pairs)
    ]


def fetch_kernel(core_ref, own_hbm, recv_hbm, near_ref, sems):
    copies = parity_copies(core_ref[0], own_hbm, recv_hbm, near_ref, sems)
    for copy in copies:
        copy.start()
    for copy in copies:
        copy.wait()


def regroup_kernel(core_ref, stiff_hbm, keep_ref, send_ref, stiff_ref, sem):
    copy = pltpu.make_async_copy(stiff_hbm, stiff_ref, sem)
    copy.start()
    copy.wait()
    core = core_ref[0]
    for k in range(0, 2 * keep_ref.shape[1], 2):
        for chunk in range(2):
            pair = [
                stiff_ref[chunk * MODES : (chunk + 1) * MODES, (k + odd) * MODES : (k + odd + 1) * MODES]
                for odd in range(2)
            ]
            keep_ref[pick(core, chunk, 1 - chunk), k // 2] = pick(core, pair[0], pair[1]).astype(BF16)
            send_ref[pick(core, 1 - chunk, chunk), k // 2] = pick(core, pair[1], pair[0]).astype(BF16)


def product_kernel(source, core_ref, amp_ref, keep_ref, recv_ref, *rest):
    prev_ref, out_ref = rest if len(rest) == 2 else (None, rest[0])
    core = core_ref[0]
    slots = keep_ref.shape[1]
    for half, ref in ((core, keep_ref), (1 - core, recv_ref)):
        for k in range(slots):
            at = half * slots + k
            value = jnp.dot(amp_ref[...], ref[source, k], preferred_element_type=F32)
            if prev_ref is not None:
                value = value + prev_ref[at]
            out_ref[at] = value.astype(out_ref.dtype)


def parity_product(odd, core, table_ref, amp_ref, near_ref, copies):
    local_diam, columns, _ = amp_ref.shape
    pairs = local_diam // 2
    total = None
    for at_half, half in enumerate((core, 1 - core)):
        for k in range(pairs):
            at = half * pairs + k
            amp = amp_ref[at].astype(F32)
            weights = jnp.concatenate(
                [(table_ref[s, 2 * at + odd] * amp).astype(BF16) for s in range(local_diam)]
            )
            if copies:
                copies[at_half * pairs + k].wait()
            shape = near_ref[at_half * pairs + k]
            value = jnp.dot(weights, shape, preferred_element_type=F32)
            total = value if total is None else total + value
    return total.reshape(local_diam, columns, near_ref.shape[2])


def same_kernel(core_ref, table_ref, amp_ref, near_ref, out_ref):
    core = core_ref[0]
    out_ref[...] = parity_product(core, core, table_ref, amp_ref, near_ref, None)


def crossed_kernel(core_ref, table_ref, amp_ref, own_hbm, recv_hbm, prev_ref, out_ref, near_ref, sems):
    core = core_ref[0]
    copies = parity_copies(1 - core, own_hbm, recv_hbm, near_ref, sems)
    for copy in copies:
        copy.start()
    total = parity_product(1 - core, core, table_ref, amp_ref, near_ref, copies)
    out_ref[...] = (total + prev_ref[...]).astype(out_ref.dtype)


def chunk_plan(phi, loads, harm_diam, mistuning, dyn_diag, blade_order):
    rows_dev, half_modes = phi.shape
    local_diam = half_modes // MODES
    columns = loads.shape[1] // NHARM
    core = lax.axis_index("diam")
    own_diam = 2 * lax.axis_index("rows") + core
    first_diam = core * local_diam
    core_arg = core.reshape(1).astype(jnp.int32)
    pairs = local_diam // 2

    def other_core(value):
        return lax.ppermute(value, "diam", SWAP)

    def in_half_order(own, received):
        return jnp.where(
            core == 0, jnp.concatenate([own, received]), jnp.concatenate([received, own])
        )

    def exchange(slots):
        return lax.all_to_all(slots, "rows", 0, 0, tiled=True)

    def row_total(got):
        return jnp.sum(got.astype(F32), axis=0)

    shapes = phi.T.reshape(local_diam, MODES, rows_dev)
    shape_sized = jax.ShapeDtypeStruct(shapes.shape, BF16)
    combined, shapes_near = pl.pallas_call(
        functools.partial(load_kernel, columns),
        name="load",
        in_specs=[SMEM, HBM, HBM, HBM],
        out_specs=[VMEM, VMEM],
        out_shape=[
            jax.ShapeDtypeStruct((local_diam, columns, rows_dev), BF16),
            shape_sized,
        ],
        scratch_shapes=[
            pltpu.SMEM(harm_diam.shape, jnp.int32),
            pltpu.VMEM(loads.shape, BF16),
            pltpu.SemaphoreType.DMA((3,)),
        ],
        compiler_params=LIMIT,
    )(core_arg, *in_hbm(harm_diam, loads, shapes))
    force_part = jnp.einsum(
        "hcr,hmr->hcm", combined, shapes_near, preferred_element_type=F32
    ).astype(BF16)
    force_slots = in_half_order(
        by_parity(force_part, core), other_core(by_parity(force_part, 1 - core))
    )
    force_slots, stiff, order, shapes_sent, dyn_diag = lax.optimization_barrier(
        (force_slots, mistuning.T, blade_order, shapes, dyn_diag)
    )
    force_got = exchange(force_slots)

    group = jax.ShapeDtypeStruct((2, pairs, MODES, MODES), BF16)
    keep, sent = pl.pallas_call(
        regroup_kernel,
        name="regroup",
        in_specs=[SMEM, HBM],
        out_specs=[VMEM, VMEM],
        out_shape=[group, group],
        scratch_shapes=[pltpu.VMEM(stiff.shape, F32), pltpu.SemaphoreType.DMA],
        compiler_params=WIDE,
        cost_estimate=pl.CostEstimate(
            flops=2 * mistuning.size, bytes_accessed=8 * mistuning.size, transcendentals=0
        ),
    )(core_arg, *in_hbm(stiff))
    recv = other_core(sent)
    shapes_received = other_core(shapes_sent)
    table = lax.dynamic_slice_in_dim(cyclic_rows(order), first_diam, local_diam, 0)
    dyn_own = lax.dynamic_slice_in_dim(dyn_diag, own_diam * MODES, MODES, 0)[None, :]
    force_got, keep, table, dyn_own = lax.optimization_barrier((force_got, keep, table, dyn_own))

    slots_shape = (local_diam, columns, MODES)

    def product(source, *operands):
        return pl.pallas_call(
            functools.partial(product_kernel, source),
            name="product",
            in_specs=[SMEM] + [VMEM] * len(operands),
            out_specs=VMEM,
            out_shape=jax.ShapeDtypeStruct(slots_shape, BF16 if source else F32),
            compiler_params=LIMIT,
        )(core_arg, *operands)

    force = row_total(force_got)
    amp = force / dyn_own
    for sweep in range(ITERS):
        amp_low = amp.astype(BF16)
        amp_other = other_core(amp_low)
        part = product(0, amp_low, keep, recv)
        part, amp_other = lax.optimization_barrier((part, amp_other))
        part = product(1, amp_other, keep, recv, part)
        amp = (force - row_total(exchange(part))) / dyn_own
        if sweep == 0:
            amp, shapes_received = lax.optimization_barrier((amp, shapes_received))
    amp, own_hbm, recv_hbm = lax.optimization_barrier((amp, shapes, shapes_received))
    same = exchange(jnp.broadcast_to(amp.astype(BF16)[None], slots_shape))
    near = pl.pallas_call(
        fetch_kernel,
        name="fetch",
        in_specs=[SMEM, HBM, HBM],
        out_specs=VMEM,
        out_shape=shape_sized,
        scratch_shapes=[pltpu.SemaphoreType.DMA((local_diam,))],
        compiler_params=LIMIT,
        cost_estimate=pl.CostEstimate(
            flops=0, bytes_accessed=4 * phi.size, transcendentals=0
        ),
    )(core_arg, own_hbm, recv_hbm)
    same, near = lax.optimization_barrier((same, near))
    crossed = other_core(same)
    half_cost = pl.CostEstimate(
        flops=2 * local_diam * columns * phi.size, bytes_accessed=2 * phi.size, transcendentals=0
    )
    out_shape = (local_diam, columns, rows_dev)
    part = pl.pallas_call(
        same_kernel,
        name="blades_same",
        in_specs=[SMEM, SMEM, VMEM, VMEM],
        out_specs=VMEM,
        out_shape=jax.ShapeDtypeStruct(out_shape, F32),
        compiler_params=LIMIT,
        cost_estimate=half_cost,
    )(core_arg, table, same, near)
    part, crossed = lax.optimization_barrier((part, crossed))
    return pl.pallas_call(
        crossed_kernel,
        name="blades_crossed",
        in_specs=[SMEM, SMEM, VMEM, HBM, HBM, VMEM],
        out_specs=VMEM,
        out_shape=jax.ShapeDtypeStruct(out_shape, BF16),
        scratch_shapes=[
            pltpu.VMEM(shapes.shape, BF16),
            pltpu.SemaphoreType.DMA((local_diam,)),
        ],
        compiler_params=WIDE,
        cost_estimate=half_cost,
    )(core_arg, table, crossed, own_hbm, recv_hbm, part)


def solution(mesh):
    placed = (P("rows", "diam"), P("rows", None), P(), P("diam", "rows"), P("grp"), P())
    one_each = mesh.shape["rows"] * 2 == NBLADE and mesh.shape["diam"] == 2
    return jax.shard_map(
        chunk_plan if one_each else general_plan,
        mesh=mesh,
        in_specs=placed,
        out_specs=P("diam", "grp", "rows"),
        check_vma=False,
    )
```

```python
import functools
import math

import jax
import jax.numpy as jnp
from jax import lax
from jax.experimental import pallas as pl
from jax.experimental.pallas import tpu as pltpu
from jax.sharding import PartitionSpec as P

NBLADE = 16
MODES = 200
NHARM = 16
ITERS = 4
SWAP = [(0, 1), (1, 0)]
F32 = jnp.float32
BF16 = jnp.bfloat16


def cyclic_rows(blade_order):
    count = NBLADE
    blade_pos = jnp.arange(count).astype(jnp.float32)[:, None]
    harmonic = jnp.arange(count)[None, :]
    half_count = count // 2
    wave = jnp.where(harmonic > half_count, harmonic - half_count, harmonic).astype(jnp.float32)
    angle = 2.0 * math.pi * wave * blade_pos / count
    scale = jnp.where(
        (harmonic == 0) | (harmonic == half_count), 1.0 / math.sqrt(count), math.sqrt(2.0 / count)
    )
    cyclic_tab = jnp.where(harmonic > half_count, jnp.sin(angle), jnp.cos(angle)) * scale
    onehot = (blade_order[:, None] == jnp.arange(count)[None, :]).astype(jnp.float32)
    return jnp.dot(onehot, cyclic_tab, precision=lax.Precision.HIGHEST)


def general_plan(phi, loads, harm_diam, mistuning, dyn_diag, blade_order):
    rows_dev = phi.shape[0]
    half_modes = phi.shape[1]
    local_diam = half_modes // MODES
    columns = loads.shape[1] // NHARM
    col_width = mistuning.shape[1]
    diam_index = lax.axis_index("diam")
    row_index = lax.axis_index("rows")
    first_diam = diam_index * local_diam
    diam_ids = first_diam + jnp.arange(local_diam, dtype=jnp.int32)
    select = (harm_diam[:, None] == diam_ids[None, :]).astype(jnp.bfloat16)
    combined = jnp.einsum(
        "rkc,kh->rhc",
        loads.reshape(rows_dev, NHARM, columns),
        select,
        preferred_element_type=jnp.float32,
    ).astype(jnp.bfloat16)
    shapes = phi.reshape(rows_dev, local_diam, MODES)
    force_part = jnp.einsum(
        "rhm,rhc->hmc", shapes, combined, preferred_element_type=jnp.float32
    ).reshape(half_modes, columns)
    half_start = diam_index * half_modes
    dyn_half = lax.dynamic_slice_in_dim(dyn_diag, half_start, half_modes, 0)[:, None]

    def row_total(partial_term):
        return lax.psum(partial_term, "rows")

    force_half = row_total(force_part)
    amp_half = force_half / dyn_half
    for sweep in range(ITERS):
        full_amp = lax.all_gather(amp_half, "diam", axis=0, tiled=True)
        col_part = lax.dynamic_slice_in_dim(full_amp, row_index * col_width, col_width, 0)
        amp_half = (
            force_half
            - row_total(
                jnp.dot(
                    mistuning,
                    col_part,
                    precision=lax.Precision.HIGHEST,
                    preferred_element_type=jnp.float32,
                )
            )
        ) / dyn_half
    amp_low = amp_half.astype(jnp.bfloat16).reshape(local_diam, MODES, columns)
    sector = jnp.einsum("rhm,hmc->hcr", shapes, amp_low, preferred_element_type=jnp.float32).astype(
        jnp.bfloat16
    )
    table = cyclic_rows(blade_order)
    table_cols = lax.dynamic_slice_in_dim(table, first_diam, local_diam, 1)
    partial_value = jnp.einsum(
        "sh,hcr->scr", table_cols, sector.astype(jnp.float32), precision=lax.Precision.HIGHEST
    )
    blades = lax.psum_scatter(
        partial_value.astype(jnp.bfloat16), "diam", scatter_dimension=0, tiled=True
    )
    return blades


def by_parity(arr, parity):
    pairs = arr.reshape((arr.shape[0] // 2, 2) + arr.shape[1:])
    return jnp.where(parity == 0, pairs[:, 0], pairs[:, 1])


VMEM = pl.BlockSpec(memory_space=pltpu.VMEM)
SMEM = pl.BlockSpec(memory_space=pltpu.SMEM)
HBM = pl.BlockSpec(memory_space=pltpu.HBM)
WIDE = pltpu.CompilerParams(vmem_limit_bytes=16 << 20)
LIMIT = pltpu.CompilerParams(vmem_limit_bytes=8 << 20)


def in_hbm(*values):
    return [pltpu.with_memory_space_constraint(value, pltpu.HBM) for value in values]


def pick(core, even, odd):
    return jnp.where(core == 0, even, odd)


def load_kernel(columns, core_ref, harm_hbm, loads_hbm, phi_hbm, combined_ref, phi_ref, harm_ref, loads_ref, sems):
    local_diam = phi_ref.shape[0]
    harm_copy = pltpu.make_async_copy(harm_hbm, harm_ref, sems.at[0])
    harm_copy.start()
    load_copy = pltpu.make_async_copy(loads_hbm, loads_ref, sems.at[1])
    load_copy.start()
    phi_copy = pltpu.make_async_copy(phi_hbm, phi_ref, sems.at[2])
    phi_copy.start()
    harm_copy.wait()
    wide = loads_ref.shape[1]
    first_diam = core_ref[0] * local_diam
    col = lax.broadcasted_iota(jnp.int32, (8, wide), 1)
    key = jnp.zeros((8, wide), jnp.int32)
    for k in range(NHARM):
        inside = (col >= k * columns) & (col < (k + 1) * columns)
        key = jnp.where(inside, (harm_ref[k] - first_diam - k) * columns + col, key)
    shape = (local_diam * columns, wide)
    row = lax.broadcasted_iota(jnp.int32, shape, 0)
    spread = jnp.where(row == jnp.broadcast_to(key[0:1], shape), 1.0, 0.0).astype(BF16)
    load_copy.wait()
    combined = lax.dot_general(
        spread, loads_ref[...], (((1,), (1,)), ((), ())), preferred_element_type=F32
    )
    combined_ref[...] = combined.astype(BF16).reshape(combined_ref.shape)
    phi_copy.wait()


def parity_copies(odd, source, near_ref, first, sems):
    return [
        pltpu.make_async_copy(source.at[2 * k + odd], near_ref.at[first + k], sems.at[first + k])
        for k in range(source.shape[0] // 2)
    ]


def assemble_kernel(core_ref, part_ref, recv_ref, out_ref):
    core = core_ref[0]
    pairs = recv_ref.shape[0]
    for k in range(pairs):
        out_ref[core * pairs + k] = part_ref[2 * k + core]
        out_ref[(1 - core) * pairs + k] = recv_ref[k]


def regroup_kernel(core_ref, stiff_hbm, own_hbm, keep_ref, send_ref, near_ref, stiff_ref, sem, near_sems):
    core = core_ref[0]
    copy = pltpu.make_async_copy(stiff_hbm, stiff_ref, sem)
    copy.start()
    near_copies = parity_copies(core, own_hbm, near_ref, 0, near_sems)
    for near_copy in near_copies:
        near_copy.start()
    copy.wait()
    for k in range(0, 2 * keep_ref.shape[1], 2):
        for chunk in range(2):
            pair = [
                stiff_ref[chunk * MODES : (chunk + 1) * MODES, (k + odd) * MODES : (k + odd + 1) * MODES]
                for odd in range(2)
            ]
            keep_ref[pick(core, chunk, 1 - chunk), k // 2] = pick(core, pair[0], pair[1]).astype(BF16)
            send_ref[pick(core, 1 - chunk, chunk), k // 2] = pick(core, pair[1], pair[0]).astype(BF16)
    for near_copy in near_copies:
        near_copy.wait()


def product_kernel(source, core_ref, amp_ref, keep_ref, recv_ref, *rest):
    prev_ref, out_ref = rest if len(rest) == 2 else (None, rest[0])
    core = core_ref[0]
    slots = keep_ref.shape[1]
    for half, ref in ((core, keep_ref), (1 - core, recv_ref)):
        for k in range(slots):
            at = half * slots + k
            value = jnp.dot(amp_ref[...], ref[source, k], preferred_element_type=F32)
            if prev_ref is not None:
                value = value + prev_ref[at]
            out_ref[at] = value.astype(out_ref.dtype)


def diameter_product(odd, core, at_half, k, table_ref, amp_ref, shape):
    local_diam = amp_ref.shape[0]
    half = 1 - core if at_half else core
    at = half * (local_diam // 2) + k
    amp = amp_ref[at].astype(F32)
    weights = jnp.concatenate(
        [(table_ref[s, 2 * at + odd] * amp).astype(BF16) for s in range(local_diam)]
    )
    return jnp.dot(weights, shape, preferred_element_type=F32)


def same_kernel(core_ref, table_ref, amp_ref, near_ref, own_hbm, recv_hbm, out_ref, far_ref, rest_ref, rest_sems, far_sems):
    core = core_ref[0]
    pairs = near_ref.shape[0]
    rest = parity_copies(core, recv_hbm, rest_ref, 0, rest_sems)
    far = parity_copies(1 - core, own_hbm, far_ref, 0, far_sems)
    far += parity_copies(1 - core, recv_hbm, far_ref, pairs, far_sems)
    for copy in rest + far:
        copy.start()
    total = 0.0
    for k in range(pairs):
        total = total + diameter_product(core, core, 0, k, table_ref, amp_ref, near_ref[k])
    for k in range(pairs):
        rest[k].wait()
        total = total + diameter_product(core, core, 1, k, table_ref, amp_ref, rest_ref[k])
    out_ref[...] = total.reshape(out_ref.shape)
    for copy in far:
        copy.wait()


def crossed_kernel(core_ref, table_ref, amp_ref, far_ref, prev_ref, out_ref):
    core = core_ref[0]
    pairs = far_ref.shape[0] // 2
    total = 0.0
    for at_half in range(2):
        for k in range(pairs):
            total = total + diameter_product(
                1 - core, core, at_half, k, table_ref, amp_ref, far_ref[at_half * pairs + k]
            )
    out_ref[...] = (total.reshape(out_ref.shape) + prev_ref[...]).astype(out_ref.dtype)


def chunk_plan(phi, loads, harm_diam, mistuning, dyn_diag, blade_order):
    rows_dev, half_modes = phi.shape
    local_diam = half_modes // MODES
    columns = loads.shape[1] // NHARM
    core = lax.axis_index("diam")
    own_diam = 2 * lax.axis_index("rows") + core
    first_diam = core * local_diam
    core_arg = core.reshape(1).astype(jnp.int32)
    pairs = local_diam // 2

    def other_core(value):
        return lax.ppermute(value, "diam", SWAP)

    def exchange(slots):
        return lax.all_to_all(slots, "rows", 0, 0, tiled=True)

    def row_total(got):
        return jnp.sum(got.astype(F32), axis=0)

    shapes = phi.T.reshape(local_diam, MODES, rows_dev)
    combined, shapes_near = pl.pallas_call(
        functools.partial(load_kernel, columns),
        name="load",
        in_specs=[SMEM, HBM, HBM, HBM],
        out_specs=[VMEM, VMEM],
        out_shape=[
            jax.ShapeDtypeStruct((local_diam, columns, rows_dev), BF16),
            jax.ShapeDtypeStruct(shapes.shape, BF16),
        ],
        scratch_shapes=[
            pltpu.SMEM(harm_diam.shape, jnp.int32),
            pltpu.VMEM(loads.shape, BF16),
            pltpu.SemaphoreType.DMA((3,)),
        ],
        compiler_params=LIMIT,
    )(core_arg, *in_hbm(harm_diam, loads, shapes))
    force_part = jnp.einsum(
        "hcr,hmr->hcm", combined, shapes_near, preferred_element_type=F32
    ).astype(BF16)
    slots_shape = (local_diam, columns, MODES)
    force_slots = pl.pallas_call(
        assemble_kernel,
        name="assemble",
        in_specs=[SMEM, VMEM, VMEM],
        out_specs=VMEM,
        out_shape=jax.ShapeDtypeStruct(slots_shape, BF16),
        compiler_params=LIMIT,
    )(core_arg, force_part, other_core(by_parity(force_part, 1 - core)))
    force_slots, stiff, order, dyn_diag, shapes_sent = lax.optimization_barrier(
        (force_slots, mistuning.T, blade_order, dyn_diag, shapes)
    )
    force_got = exchange(force_slots)

    group = jax.ShapeDtypeStruct((2, pairs, MODES, MODES), BF16)
    near_sized = jax.ShapeDtypeStruct((pairs, MODES, rows_dev), BF16)
    keep, sent, near = pl.pallas_call(
        regroup_kernel,
        name="regroup",
        in_specs=[SMEM, HBM, HBM],
        out_specs=[VMEM, VMEM, VMEM],
        out_shape=[group, group, near_sized],
        scratch_shapes=[
            pltpu.VMEM(stiff.shape, F32),
            pltpu.SemaphoreType.DMA,
            pltpu.SemaphoreType.DMA((pairs,)),
        ],
        compiler_params=WIDE,
        cost_estimate=pl.CostEstimate(
            flops=2 * mistuning.size, bytes_accessed=8 * mistuning.size, transcendentals=0
        ),
    )(core_arg, *in_hbm(stiff, shapes))
    recv = other_core(sent)
    shapes_received = other_core(shapes_sent)
    table = lax.dynamic_slice_in_dim(cyclic_rows(order), first_diam, local_diam, 0)
    dyn_own = lax.dynamic_slice_in_dim(dyn_diag, own_diam * MODES, MODES, 0)[None, :]
    force_got, keep, table, dyn_own = lax.optimization_barrier((force_got, keep, table, dyn_own))

    def product(source, *operands):
        return pl.pallas_call(
            functools.partial(product_kernel, source),
            name="product",
            in_specs=[SMEM] + [VMEM] * len(operands),
            out_specs=VMEM,
            out_shape=jax.ShapeDtypeStruct(slots_shape, BF16 if source else F32),
            compiler_params=LIMIT,
        )(core_arg, *operands)

    force = row_total(force_got)
    amp = force / dyn_own
    for sweep in range(ITERS):
        amp_low = amp.astype(BF16)
        amp_other = other_core(amp_low)
        part = product(0, amp_low, keep, recv)
        part, amp_other = lax.optimization_barrier((part, amp_other))
        part = product(1, amp_other, keep, recv, part)
        amp = (force - row_total(exchange(part))) / dyn_own
        if sweep == 0:
            amp, shapes_received = lax.optimization_barrier((amp, shapes_received))
    same = exchange(jnp.broadcast_to(amp.astype(BF16)[None], slots_shape))
    crossed = other_core(same)
    half_cost = pl.CostEstimate(
        flops=2 * local_diam * columns * phi.size, bytes_accessed=2 * phi.size, transcendentals=0
    )
    out_shape = (local_diam, columns, rows_dev)
    part, far = pl.pallas_call(
        same_kernel,
        name="blades_same",
        in_specs=[SMEM, SMEM, VMEM, VMEM, HBM, HBM],
        out_specs=[VMEM, VMEM],
        out_shape=[
            jax.ShapeDtypeStruct(out_shape, F32),
            jax.ShapeDtypeStruct(shapes.shape, BF16),
        ],
        scratch_shapes=[
            pltpu.VMEM(near.shape, BF16),
            pltpu.SemaphoreType.DMA((pairs,)),
            pltpu.SemaphoreType.DMA((local_diam,)),
        ],
        compiler_params=WIDE,
        cost_estimate=half_cost,
    )(core_arg, table, same, near, *in_hbm(shapes, shapes_received))
    part, far, crossed = lax.optimization_barrier((part, far, crossed))
    return pl.pallas_call(
        crossed_kernel,
        name="blades_crossed",
        in_specs=[SMEM, SMEM, VMEM, VMEM, VMEM],
        out_specs=VMEM,
        out_shape=jax.ShapeDtypeStruct(out_shape, BF16),
        compiler_params=WIDE,
        cost_estimate=half_cost,
    )(core_arg, table, crossed, far, part)


def solution(mesh):
    placed = (P("rows", "diam"), P("rows", None), P(), P("diam", "rows"), P("grp"), P())
    one_each = mesh.shape["rows"] * 2 == NBLADE and mesh.shape["diam"] == 2
    return jax.shard_map(
        chunk_plan if one_each else general_plan,
        mesh=mesh,
        in_specs=placed,
        out_specs=P("diam", "grp", "rows"),
        check_vma=False,
    )
```

```python
import functools
import math

import jax
import jax.numpy as jnp
from jax import lax
from jax.experimental import pallas as pl
from jax.experimental.pallas import tpu as pltpu
from jax.sharding import PartitionSpec as P

NBLADE = 16
MODES = 200
NHARM = 16
ITERS = 4
SWAP = [(0, 1), (1, 0)]
F32 = jnp.float32
BF16 = jnp.bfloat16


def cyclic_rows(blade_order):
    count = NBLADE
    blade_pos = jnp.arange(count).astype(jnp.float32)[:, None]
    harmonic = jnp.arange(count)[None, :]
    half_count = count // 2
    wave = jnp.where(harmonic > half_count, harmonic - half_count, harmonic).astype(jnp.float32)
    angle = 2.0 * math.pi * wave * blade_pos / count
    scale = jnp.where(
        (harmonic == 0) | (harmonic == half_count), 1.0 / math.sqrt(count), math.sqrt(2.0 / count)
    )
    cyclic_tab = jnp.where(harmonic > half_count, jnp.sin(angle), jnp.cos(angle)) * scale
    onehot = (blade_order[:, None] == jnp.arange(count)[None, :]).astype(jnp.float32)
    return jnp.dot(onehot, cyclic_tab, precision=lax.Precision.HIGHEST)


def general_plan(phi, loads, harm_diam, mistuning, dyn_diag, blade_order):
    rows_dev = phi.shape[0]
    half_modes = phi.shape[1]
    local_diam = half_modes // MODES
    columns = loads.shape[1] // NHARM
    col_width = mistuning.shape[1]
    diam_index = lax.axis_index("diam")
    row_index = lax.axis_index("rows")
    first_diam = diam_index * local_diam
    diam_ids = first_diam + jnp.arange(local_diam, dtype=jnp.int32)
    select = (harm_diam[:, None] == diam_ids[None, :]).astype(jnp.bfloat16)
    combined = jnp.einsum(
        "rkc,kh->rhc",
        loads.reshape(rows_dev, NHARM, columns),
        select,
        preferred_element_type=jnp.float32,
    ).astype(jnp.bfloat16)
    shapes = phi.reshape(rows_dev, local_diam, MODES)
    force_part = jnp.einsum(
        "rhm,rhc->hmc", shapes, combined, preferred_element_type=jnp.float32
    ).reshape(half_modes, columns)
    half_start = diam_index * half_modes
    dyn_half = lax.dynamic_slice_in_dim(dyn_diag, half_start, half_modes, 0)[:, None]

    def row_total(partial_term):
        return lax.psum(partial_term, "rows")

    force_half = row_total(force_part)
    amp_half = force_half / dyn_half
    for sweep in range(ITERS):
        full_amp = lax.all_gather(amp_half, "diam", axis=0, tiled=True)
        col_part = lax.dynamic_slice_in_dim(full_amp, row_index * col_width, col_width, 0)
        amp_half = (
            force_half
            - row_total(
                jnp.dot(
                    mistuning,
                    col_part,
                    precision=lax.Precision.HIGHEST,
                    preferred_element_type=jnp.float32,
                )
            )
        ) / dyn_half
    amp_low = amp_half.astype(jnp.bfloat16).reshape(local_diam, MODES, columns)
    sector = jnp.einsum("rhm,hmc->hcr", shapes, amp_low, preferred_element_type=jnp.float32).astype(
        jnp.bfloat16
    )
    table = cyclic_rows(blade_order)
    table_cols = lax.dynamic_slice_in_dim(table, first_diam, local_diam, 1)
    partial_value = jnp.einsum(
        "sh,hcr->scr", table_cols, sector.astype(jnp.float32), precision=lax.Precision.HIGHEST
    )
    blades = lax.psum_scatter(
        partial_value.astype(jnp.bfloat16), "diam", scatter_dimension=0, tiled=True
    )
    return blades


def by_parity(arr, parity):
    pairs = arr.reshape((arr.shape[0] // 2, 2) + arr.shape[1:])
    return jnp.where(parity == 0, pairs[:, 0], pairs[:, 1])


VMEM = pl.BlockSpec(memory_space=pltpu.VMEM)
SMEM = pl.BlockSpec(memory_space=pltpu.SMEM)
HBM = pl.BlockSpec(memory_space=pltpu.HBM)
WIDE = pltpu.CompilerParams(vmem_limit_bytes=16 << 20)
LIMIT = pltpu.CompilerParams(vmem_limit_bytes=8 << 20)


def in_hbm(*values):
    return [pltpu.with_memory_space_constraint(value, pltpu.HBM) for value in values]


def pick(core, even, odd):
    return jnp.where(core == 0, even, odd)


def load_kernel(columns, core_ref, harm_hbm, loads_hbm, phi_hbm, combined_ref, phi_ref, harm_ref, loads_ref, sems):
    local_diam = phi_ref.shape[0]
    harm_copy = pltpu.make_async_copy(harm_hbm, harm_ref, sems.at[0])
    harm_copy.start()
    load_copy = pltpu.make_async_copy(loads_hbm, loads_ref, sems.at[1])
    load_copy.start()
    phi_copy = pltpu.make_async_copy(phi_hbm, phi_ref, sems.at[2])
    phi_copy.start()
    harm_copy.wait()
    wide = loads_ref.shape[1]
    first_diam = core_ref[0] * local_diam
    col = lax.broadcasted_iota(jnp.int32, (8, wide), 1)
    key = jnp.zeros((8, wide), jnp.int32)
    for k in range(NHARM):
        inside = (col >= k * columns) & (col < (k + 1) * columns)
        key = jnp.where(inside, (harm_ref[k] - first_diam - k) * columns + col, key)
    shape = (local_diam * columns, wide)
    row = lax.broadcasted_iota(jnp.int32, shape, 0)
    spread = jnp.where(row == jnp.broadcast_to(key[0:1], shape), 1.0, 0.0).astype(BF16)
    load_copy.wait()
    combined = lax.dot_general(
        spread, loads_ref[...], (((1,), (1,)), ((), ())), preferred_element_type=F32
    )
    combined_ref[...] = combined.astype(BF16).reshape(combined_ref.shape)
    phi_copy.wait()


def parity_copies(odd, source, near_ref, first, sems):
    return [
        pltpu.make_async_copy(source.at[2 * k + odd], near_ref.at[first + k], sems.at[first + k])
        for k in range(source.shape[0] // 2)
    ]


def assemble_kernel(core_ref, part_ref, recv_ref, out_ref):
    core = core_ref[0]
    pairs = recv_ref.shape[0]
    for k in range(pairs):
        out_ref[core * pairs + k] = part_ref[2 * k + core]
        out_ref[(1 - core) * pairs + k] = recv_ref[k]


def regroup_kernel(core_ref, stiff_hbm, own_hbm, keep_ref, send_ref, near_ref, stiff_ref, sems, near_sems):
    core = core_ref[0]
    chunks = [slice(0, MODES), slice(MODES, 2 * MODES)]
    copies = [
        pltpu.make_async_copy(stiff_hbm.at[rows], stiff_ref.at[rows], sems.at[chunk])
        for chunk, rows in enumerate(chunks)
    ]
    for copy in copies:
        copy.start()
    near_copies = parity_copies(core, own_hbm, near_ref, 0, near_sems)
    for near_copy in near_copies:
        near_copy.start()
    for chunk, rows in enumerate(chunks):
        copies[chunk].wait()
        stiff = stiff_ref[rows].astype(BF16)
        for k in range(keep_ref.shape[1]):
            even = stiff[:, 2 * k * MODES : (2 * k + 1) * MODES]
            odd = stiff[:, (2 * k + 1) * MODES : (2 * k + 2) * MODES]
            keep_ref[pick(core, chunk, 1 - chunk), k] = pick(core, even, odd)
            send_ref[pick(core, 1 - chunk, chunk), k] = pick(core, odd, even)
    for near_copy in near_copies:
        near_copy.wait()


def product_kernel(source, core_ref, amp_ref, keep_ref, recv_ref, *rest):
    prev_ref, out_ref = rest if len(rest) == 2 else (None, rest[0])
    core = core_ref[0]
    slots = keep_ref.shape[1]
    for half, ref in ((core, keep_ref), (1 - core, recv_ref)):
        for k in range(slots):
            at = half * slots + k
            value = jnp.dot(amp_ref[...], ref[source, k], preferred_element_type=F32)
            if prev_ref is not None:
                value = value + prev_ref[at]
            out_ref[at] = value.astype(out_ref.dtype)


def blades_kernel(core_ref, table_ref, same_ref, crossed_ref, near_ref, own_hbm, recv_hbm, out_hbm, far_ref, weights_ref, total_ref, out_ref, sems, out_sems):
    core = core_ref[0]
    local_diam, columns, _ = same_ref.shape
    pairs = local_diam // 2
    copies = parity_copies(core, recv_hbm, far_ref, 0, sems)
    copies += parity_copies(1 - core, own_hbm, far_ref, pairs, sems)
    copies += parity_copies(1 - core, recv_hbm, far_ref, 2 * pairs, sems)
    for copy in copies:
        copy.start()
    groups = [(core, core, same_ref), (1 - core, core, same_ref)]
    groups += [(core, 1 - core, crossed_ref), (1 - core, 1 - core, crossed_ref)]
    for g, (half, odd, amp_ref) in enumerate(groups):
        for k in range(pairs):
            at = half * pairs + k
            amp = amp_ref[at].astype(F32)
            for s in range(local_diam):
                value = table_ref[s, 2 * at + odd] * amp
                weights_ref[g * pairs + k, s * columns : (s + 1) * columns] = value.astype(BF16)
        if g:
            for copy in copies[(g - 1) * pairs : g * pairs]:
                copy.wait()
        last = g + 1 == len(groups)
        wide = total_ref.shape[1] // 4 if last else total_ref.shape[1]
        for tile in range(total_ref.shape[1] // wide):
            lanes = slice(tile * wide, (tile + 1) * wide)
            total = total_ref[:, lanes] if g else 0.0
            for k in range(pairs):
                shape = near_ref[k] if g == 0 else far_ref[(g - 1) * pairs + k, :, lanes]
                total = total + jnp.dot(
                    weights_ref[g * pairs + k], shape, preferred_element_type=F32
                )
            if last:
                out_ref[:, :, lanes] = total.reshape(local_diam, columns, wide).astype(BF16)
                pltpu.make_async_copy(
                    out_ref.at[:, :, lanes], out_hbm.at[:, :, lanes], out_sems.at[tile]
                ).start()
            else:
                total_ref[...] = total
    for tile in range(4):
        lanes = slice(tile * wide, (tile + 1) * wide)
        pltpu.make_async_copy(
            out_ref.at[:, :, lanes], out_hbm.at[:, :, lanes], out_sems.at[tile]
        ).wait()


def chunk_plan(phi, loads, harm_diam, mistuning, dyn_diag, blade_order):
    rows_dev, half_modes = phi.shape
    local_diam = half_modes // MODES
    columns = loads.shape[1] // NHARM
    core = lax.axis_index("diam")
    own_diam = 2 * lax.axis_index("rows") + core
    first_diam = core * local_diam
    core_arg = core.reshape(1).astype(jnp.int32)
    pairs = local_diam // 2

    def other_core(value):
        return lax.ppermute(value, "diam", SWAP)

    def exchange(slots):
        return lax.all_to_all(slots, "rows", 0, 0, tiled=True)

    def row_total(got):
        return jnp.sum(got.astype(F32), axis=0)

    shapes = phi.T.reshape(local_diam, MODES, rows_dev)
    combined, shapes_near = pl.pallas_call(
        functools.partial(load_kernel, columns),
        name="load",
        in_specs=[SMEM, HBM, HBM, HBM],
        out_specs=[VMEM, VMEM],
        out_shape=[
            jax.ShapeDtypeStruct((local_diam, columns, rows_dev), BF16),
            jax.ShapeDtypeStruct(shapes.shape, BF16),
        ],
        scratch_shapes=[
            pltpu.SMEM(harm_diam.shape, jnp.int32),
            pltpu.VMEM(loads.shape, BF16),
            pltpu.SemaphoreType.DMA((3,)),
        ],
        compiler_params=LIMIT,
    )(core_arg, *in_hbm(harm_diam, loads, shapes))
    force_part = jnp.einsum(
        "hcr,hmr->hcm", combined, shapes_near, preferred_element_type=F32
    ).astype(BF16)
    slots_shape = (local_diam, columns, MODES)
    force_recv = other_core(by_parity(force_part, 1 - core))
    force_slots = pl.pallas_call(
        assemble_kernel,
        name="assemble",
        in_specs=[SMEM, VMEM, VMEM],
        out_specs=VMEM,
        out_shape=jax.ShapeDtypeStruct(slots_shape, BF16),
        compiler_params=LIMIT,
    )(core_arg, force_part, force_recv)
    force_slots, stiff, order, dyn_diag, shapes_sent = lax.optimization_barrier(
        (force_slots, mistuning.T, blade_order, dyn_diag, shapes)
    )
    force_got = exchange(force_slots)

    group = jax.ShapeDtypeStruct((2, pairs, MODES, MODES), BF16)
    near_sized = jax.ShapeDtypeStruct((pairs, MODES, rows_dev), BF16)
    keep, sent, near = pl.pallas_call(
        regroup_kernel,
        name="regroup",
        in_specs=[SMEM, HBM, HBM],
        out_specs=[VMEM, VMEM, VMEM],
        out_shape=[group, group, near_sized],
        scratch_shapes=[
            pltpu.VMEM(stiff.shape, F32),
            pltpu.SemaphoreType.DMA((2,)),
            pltpu.SemaphoreType.DMA((pairs,)),
        ],
        compiler_params=WIDE,
        cost_estimate=pl.CostEstimate(
            flops=2 * mistuning.size, bytes_accessed=8 * mistuning.size, transcendentals=0
        ),
    )(core_arg, *in_hbm(stiff, shapes))
    recv = other_core(sent)
    shapes_received = other_core(shapes_sent)
    table = lax.dynamic_slice_in_dim(cyclic_rows(order), first_diam, local_diam, 0)
    dyn_own = lax.dynamic_slice_in_dim(dyn_diag, own_diam * MODES, MODES, 0)[None, :]
    force_got, keep, table, dyn_own = lax.optimization_barrier((force_got, keep, table, dyn_own))

    def product(source, *operands):
        return pl.pallas_call(
            functools.partial(product_kernel, source),
            name="product",
            in_specs=[SMEM] + [VMEM] * len(operands),
            out_specs=VMEM,
            out_shape=jax.ShapeDtypeStruct(slots_shape, BF16 if source else F32),
            compiler_params=LIMIT,
        )(core_arg, *operands)

    force = row_total(force_got)
    amp = force / dyn_own
    for sweep in range(ITERS):
        amp_low = amp.astype(BF16)
        amp_other = other_core(amp_low)
        part = product(0, amp_low, keep, recv)
        part, amp_other = lax.optimization_barrier((part, amp_other))
        part = product(1, amp_other, keep, recv, part)
        amp = (force - row_total(exchange(part))) / dyn_own
        if sweep == 0:
            amp, shapes_received = lax.optimization_barrier((amp, shapes_received))
    same = exchange(jnp.broadcast_to(amp.astype(BF16)[None], slots_shape))
    crossed = other_core(same)
    out_shape = (local_diam, columns, rows_dev)
    return pl.pallas_call(
        blades_kernel,
        name="blades",
        in_specs=[SMEM, SMEM, VMEM, VMEM, VMEM, HBM, HBM],
        out_specs=HBM,
        out_shape=jax.ShapeDtypeStruct(out_shape, BF16),
        scratch_shapes=[
            pltpu.VMEM((3 * pairs, MODES, rows_dev), BF16),
            pltpu.VMEM((NBLADE, local_diam * columns, MODES), BF16),
            pltpu.VMEM((local_diam * columns, rows_dev), F32),
            pltpu.VMEM(out_shape, BF16),
            pltpu.SemaphoreType.DMA((3 * pairs,)),
            pltpu.SemaphoreType.DMA((4,)),
        ],
        compiler_params=WIDE,
        cost_estimate=pl.CostEstimate(
            flops=4 * local_diam * columns * phi.size,
            bytes_accessed=4 * phi.size,
            transcendentals=0,
        ),
    )(core_arg, table, same, crossed, near, *in_hbm(shapes, shapes_received))


def solution(mesh):
    placed = (P("rows", "diam"), P("rows", None), P(), P("diam", "rows"), P("grp"), P())
    one_each = mesh.shape["rows"] * 2 == NBLADE and mesh.shape["diam"] == 2
    return jax.shard_map(
        chunk_plan if one_each else general_plan,
        mesh=mesh,
        in_specs=placed,
        out_specs=P("diam", "grp", "rows"),
        check_vma=False,
    )
```

```python
import functools
import math

import jax
import jax.numpy as jnp
from jax import lax
from jax.experimental import pallas as pl
from jax.experimental.pallas import tpu as pltpu
from jax.sharding import PartitionSpec as P

NBLADE = 16
MODES = 200
NHARM = 16
ITERS = 4
SWAP = [(0, 1), (1, 0)]
F32 = jnp.float32
BF16 = jnp.bfloat16


def cyclic_rows(blade_order):
    count = NBLADE
    blade_pos = jnp.arange(count).astype(jnp.float32)[:, None]
    harmonic = jnp.arange(count)[None, :]
    half_count = count // 2
    wave = jnp.where(harmonic > half_count, harmonic - half_count, harmonic).astype(jnp.float32)
    angle = 2.0 * math.pi * wave * blade_pos / count
    scale = jnp.where(
        (harmonic == 0) | (harmonic == half_count), 1.0 / math.sqrt(count), math.sqrt(2.0 / count)
    )
    cyclic_tab = jnp.where(harmonic > half_count, jnp.sin(angle), jnp.cos(angle)) * scale
    onehot = (blade_order[:, None] == jnp.arange(count)[None, :]).astype(jnp.float32)
    return jnp.dot(onehot, cyclic_tab, precision=lax.Precision.HIGHEST)


def general_plan(phi, loads, harm_diam, mistuning, dyn_diag, blade_order):
    rows_dev = phi.shape[0]
    half_modes = phi.shape[1]
    local_diam = half_modes // MODES
    columns = loads.shape[1] // NHARM
    col_width = mistuning.shape[1]
    diam_index = lax.axis_index("diam")
    row_index = lax.axis_index("rows")
    first_diam = diam_index * local_diam
    diam_ids = first_diam + jnp.arange(local_diam, dtype=jnp.int32)
    select = (harm_diam[:, None] == diam_ids[None, :]).astype(jnp.bfloat16)
    combined = jnp.einsum(
        "rkc,kh->rhc",
        loads.reshape(rows_dev, NHARM, columns),
        select,
        preferred_element_type=jnp.float32,
    ).astype(jnp.bfloat16)
    shapes = phi.reshape(rows_dev, local_diam, MODES)
    force_part = jnp.einsum(
        "rhm,rhc->hmc", shapes, combined, preferred_element_type=jnp.float32
    ).reshape(half_modes, columns)
    half_start = diam_index * half_modes
    dyn_half = lax.dynamic_slice_in_dim(dyn_diag, half_start, half_modes, 0)[:, None]

    def row_total(partial_term):
        return lax.psum(partial_term, "rows")

    force_half = row_total(force_part)
    amp_half = force_half / dyn_half
    for sweep in range(ITERS):
        full_amp = lax.all_gather(amp_half, "diam", axis=0, tiled=True)
        col_part = lax.dynamic_slice_in_dim(full_amp, row_index * col_width, col_width, 0)
        amp_half = (
            force_half
            - row_total(
                jnp.dot(
                    mistuning,
                    col_part,
                    precision=lax.Precision.HIGHEST,
                    preferred_element_type=jnp.float32,
                )
            )
        ) / dyn_half
    amp_low = amp_half.astype(jnp.bfloat16).reshape(local_diam, MODES, columns)
    sector = jnp.einsum("rhm,hmc->hcr", shapes, amp_low, preferred_element_type=jnp.float32).astype(
        jnp.bfloat16
    )
    table = cyclic_rows(blade_order)
    table_cols = lax.dynamic_slice_in_dim(table, first_diam, local_diam, 1)
    partial_value = jnp.einsum(
        "sh,hcr->scr", table_cols, sector.astype(jnp.float32), precision=lax.Precision.HIGHEST
    )
    blades = lax.psum_scatter(
        partial_value.astype(jnp.bfloat16), "diam", scatter_dimension=0, tiled=True
    )
    return blades


def by_parity(arr, parity):
    pairs = arr.reshape((arr.shape[0] // 2, 2) + arr.shape[1:])
    return jnp.where(parity == 0, pairs[:, 0], pairs[:, 1])


VMEM = pl.BlockSpec(memory_space=pltpu.VMEM)
SMEM = pl.BlockSpec(memory_space=pltpu.SMEM)
HBM = pl.BlockSpec(memory_space=pltpu.HBM)
WIDE = pltpu.CompilerParams(vmem_limit_bytes=16 << 20)
LIMIT = pltpu.CompilerParams(vmem_limit_bytes=8 << 20)


def in_hbm(*values):
    return [pltpu.with_memory_space_constraint(value, pltpu.HBM) for value in values]


def pick(core, even, odd):
    return jnp.where(core == 0, even, odd)


def load_kernel(columns, core_ref, harm_hbm, loads_hbm, phi_hbm, combined_ref, phi_ref, harm_ref, loads_ref, sems):
    local_diam = phi_ref.shape[0]
    harm_copy = pltpu.make_async_copy(harm_hbm, harm_ref, sems.at[0])
    harm_copy.start()
    load_copy = pltpu.make_async_copy(loads_hbm, loads_ref, sems.at[1])
    load_copy.start()
    phi_copy = pltpu.make_async_copy(phi_hbm, phi_ref, sems.at[2])
    phi_copy.start()
    harm_copy.wait()
    wide = loads_ref.shape[1]
    first_diam = core_ref[0] * local_diam
    col = lax.broadcasted_iota(jnp.int32, (8, wide), 1)
    key = jnp.zeros((8, wide), jnp.int32)
    for k in range(NHARM):
        inside = (col >= k * columns) & (col < (k + 1) * columns)
        key = jnp.where(inside, (harm_ref[k] - first_diam - k) * columns + col, key)
    shape = (local_diam * columns, wide)
    row = lax.broadcasted_iota(jnp.int32, shape, 0)
    spread = jnp.where(row == jnp.broadcast_to(key[0:1], shape), 1.0, 0.0).astype(BF16)
    load_copy.wait()
    combined = lax.dot_general(
        spread, loads_ref[...], (((1,), (1,)), ((), ())), preferred_element_type=F32
    )
    combined_ref[...] = combined.astype(BF16).reshape(combined_ref.shape)
    phi_copy.wait()


def assemble_kernel(core_ref, part_ref, recv_ref, out_ref):
    core = core_ref[0]
    pairs = recv_ref.shape[0]
    for k in range(pairs):
        out_ref[core * pairs + k] = part_ref[2 * k + core]
        out_ref[(1 - core) * pairs + k] = recv_ref[k]


def regroup_kernel(core_ref, stiff_hbm, keep_ref, send_ref, stiff_ref, sems):
    core = core_ref[0]
    chunks = [slice(0, MODES), slice(MODES, 2 * MODES)]
    copies = [
        pltpu.make_async_copy(stiff_hbm.at[rows], stiff_ref.at[rows], sems.at[chunk])
        for chunk, rows in enumerate(chunks)
    ]
    for copy in copies:
        copy.start()
    for chunk, rows in enumerate(chunks):
        copies[chunk].wait()
        stiff = stiff_ref[rows].astype(BF16)
        for k in range(keep_ref.shape[1]):
            even = stiff[:, 2 * k * MODES : (2 * k + 1) * MODES]
            odd = stiff[:, (2 * k + 1) * MODES : (2 * k + 2) * MODES]
            keep_ref[pick(core, chunk, 1 - chunk), k] = pick(core, even, odd)
            send_ref[pick(core, 1 - chunk, chunk), k] = pick(core, odd, even)


def product_kernel(source, core_ref, amp_ref, keep_ref, recv_ref, *rest):
    prev_ref, out_ref = rest if len(rest) == 2 else (None, rest[0])
    core = core_ref[0]
    slots = keep_ref.shape[1]
    for half, ref in ((core, keep_ref), (1 - core, recv_ref)):
        for k in range(slots):
            at = half * slots + k
            value = jnp.dot(amp_ref[...], ref[source, k], preferred_element_type=F32)
            if prev_ref is not None:
                value = value + prev_ref[at]
            out_ref[at] = value.astype(out_ref.dtype)


def blades_kernel(crossed, core_ref, table_ref, amp_ref, own_ref, recv_ref, *rest):
    *prev_ref, out_ref, weights_ref = rest
    core = core_ref[0]
    local_diam, columns, _ = amp_ref.shape
    pairs = local_diam // 2
    odd = 1 - core if crossed else core
    total = prev_ref[0][...] if crossed else 0.0
    for at_half, (half, phi_ref) in enumerate(((core, own_ref), (1 - core, recv_ref))):
        for k in range(pairs):
            at = half * pairs + k
            place = at_half * pairs + k
            amp = amp_ref[at].astype(F32)
            for s in range(local_diam):
                value = table_ref[s, 2 * at + odd] * amp
                weights_ref[place, s * columns : (s + 1) * columns] = value.astype(BF16)
            total = total + jnp.dot(
                weights_ref[place], phi_ref[2 * k + odd], preferred_element_type=F32
            )
    out_ref[...] = total.astype(out_ref.dtype).reshape(out_ref.shape)


def chunk_plan(phi, loads, harm_diam, mistuning, dyn_diag, blade_order):
    rows_dev, half_modes = phi.shape
    local_diam = half_modes // MODES
    columns = loads.shape[1] // NHARM
    core = lax.axis_index("diam")
    own_diam = 2 * lax.axis_index("rows") + core
    first_diam = core * local_diam
    core_arg = core.reshape(1).astype(jnp.int32)
    pairs = local_diam // 2

    def other_core(value):
        return lax.ppermute(value, "diam", SWAP)

    def exchange(slots):
        return lax.all_to_all(slots, "rows", 0, 0, tiled=True)

    def row_total(got):
        return jnp.sum(got.astype(F32), axis=0)

    shapes = phi.T.reshape(local_diam, MODES, rows_dev)
    combined, shapes_near = pl.pallas_call(
        functools.partial(load_kernel, columns),
        name="load",
        in_specs=[SMEM, HBM, HBM, HBM],
        out_specs=[VMEM, VMEM],
        out_shape=[
            jax.ShapeDtypeStruct((local_diam, columns, rows_dev), BF16),
            jax.ShapeDtypeStruct(shapes.shape, BF16),
        ],
        scratch_shapes=[
            pltpu.SMEM(harm_diam.shape, jnp.int32),
            pltpu.VMEM(loads.shape, BF16),
            pltpu.SemaphoreType.DMA((3,)),
        ],
        compiler_params=LIMIT,
    )(core_arg, *in_hbm(harm_diam, loads, shapes))
    force_part = jnp.einsum(
        "hcr,hmr->hcm", combined, shapes_near, preferred_element_type=F32
    ).astype(BF16)
    slots_shape = (local_diam, columns, MODES)
    force_recv = other_core(by_parity(force_part, 1 - core))
    force_slots = pl.pallas_call(
        assemble_kernel,
        name="assemble",
        in_specs=[SMEM, VMEM, VMEM],
        out_specs=VMEM,
        out_shape=jax.ShapeDtypeStruct(slots_shape, BF16),
        compiler_params=LIMIT,
    )(core_arg, force_part, force_recv)
    force_slots, stiff, order, dyn_diag = lax.optimization_barrier(
        (force_slots, mistuning.T, blade_order, dyn_diag)
    )
    force_got = exchange(force_slots)

    group = jax.ShapeDtypeStruct((2, pairs, MODES, MODES), BF16)
    keep, sent = pl.pallas_call(
        regroup_kernel,
        name="regroup",
        in_specs=[SMEM, HBM],
        out_specs=[VMEM, VMEM],
        out_shape=[group, group],
        scratch_shapes=[
            pltpu.VMEM(stiff.shape, F32),
            pltpu.SemaphoreType.DMA((2,)),
        ],
        compiler_params=WIDE,
        cost_estimate=pl.CostEstimate(
            flops=2 * mistuning.size, bytes_accessed=8 * mistuning.size, transcendentals=0
        ),
    )(core_arg, *in_hbm(stiff))
    recv = other_core(sent)
    table = lax.dynamic_slice_in_dim(cyclic_rows(order), first_diam, local_diam, 0)
    dyn_own = lax.dynamic_slice_in_dim(dyn_diag, own_diam * MODES, MODES, 0)[None, :]
    force_got, keep, table, dyn_own = lax.optimization_barrier((force_got, keep, table, dyn_own))

    def product(source, *operands):
        return pl.pallas_call(
            functools.partial(product_kernel, source),
            name="product",
            in_specs=[SMEM] + [VMEM] * len(operands),
            out_specs=VMEM,
            out_shape=jax.ShapeDtypeStruct(slots_shape, BF16 if source else F32),
            compiler_params=LIMIT,
        )(core_arg, *operands)

    force = row_total(force_got)
    amp = force / dyn_own
    for sweep in range(ITERS):
        amp_low = amp.astype(BF16)
        amp_other = other_core(amp_low)
        part = product(0, amp_low, keep, recv)
        part, amp_other = lax.optimization_barrier((part, amp_other))
        if sweep == ITERS - 1:
            part, shapes_sent = lax.optimization_barrier((part, shapes))
            shapes_received = other_core(shapes_sent)
        part = product(1, amp_other, keep, recv, part)
        amp = (force - row_total(exchange(part))) / dyn_own
    same = exchange(jnp.broadcast_to(amp.astype(BF16)[None], slots_shape))
    crossed = other_core(same)

    def blades(crossed, amps, out_shape, *prev):
        return pl.pallas_call(
            functools.partial(blades_kernel, crossed),
            name="blades",
            in_specs=[SMEM, SMEM] + [VMEM] * (3 + len(prev)),
            out_specs=VMEM,
            out_shape=out_shape,
            scratch_shapes=[pltpu.VMEM((local_diam, local_diam * columns, MODES), BF16)],
            compiler_params=WIDE,
            cost_estimate=pl.CostEstimate(
                flops=2 * local_diam * columns * phi.size,
                bytes_accessed=2 * phi.size,
                transcendentals=0,
            ),
        )(core_arg, table, amps, shapes_sent, shapes_received, *prev)

    part = blades(False, same, jax.ShapeDtypeStruct((local_diam * columns, rows_dev), F32))
    part, crossed = lax.optimization_barrier((part, crossed))
    out_shape = jax.ShapeDtypeStruct((local_diam, columns, rows_dev), BF16)
    return blades(True, crossed, out_shape, part)


def solution(mesh):
    placed = (P("rows", "diam"), P("rows", None), P(), P("diam", "rows"), P("grp"), P())
    one_each = mesh.shape["rows"] * 2 == NBLADE and mesh.shape["diam"] == 2
    return jax.shard_map(
        chunk_plan if one_each else general_plan,
        mesh=mesh,
        in_specs=placed,
        out_specs=P("diam", "grp", "rows"),
        check_vma=False,
    )
```

```python
import functools
import math

import jax
import jax.numpy as jnp
from jax import lax
from jax.experimental import pallas as pl
from jax.experimental.pallas import tpu as pltpu
from jax.sharding import PartitionSpec as P

NBLADE = 16
MODES = 200
NHARM = 16
ITERS = 4
SWAP = [(0, 1), (1, 0)]
LANES = 128
HALF = 64
PACKED = (56, LANES)
F32 = jnp.float32
BF16 = jnp.bfloat16


def cyclic_rows(blade_order):
    count = NBLADE
    blade_pos = jnp.arange(count).astype(jnp.float32)[:, None]
    harmonic = jnp.arange(count)[None, :]
    half_count = count // 2
    wave = jnp.where(harmonic > half_count, harmonic - half_count, harmonic).astype(jnp.float32)
    angle = 2.0 * math.pi * wave * blade_pos / count
    scale = jnp.where(
        (harmonic == 0) | (harmonic == half_count), 1.0 / math.sqrt(count), math.sqrt(2.0 / count)
    )
    cyclic_tab = jnp.where(harmonic > half_count, jnp.sin(angle), jnp.cos(angle)) * scale
    onehot = (blade_order[:, None] == jnp.arange(count)[None, :]).astype(jnp.float32)
    return jnp.dot(onehot, cyclic_tab, precision=lax.Precision.HIGHEST)


def general_plan(phi, loads, harm_diam, mistuning, dyn_diag, blade_order):
    rows_dev = phi.shape[0]
    half_modes = phi.shape[1]
    local_diam = half_modes // MODES
    columns = loads.shape[1] // NHARM
    col_width = mistuning.shape[1]
    diam_index = lax.axis_index("diam")
    row_index = lax.axis_index("rows")
    first_diam = diam_index * local_diam
    diam_ids = first_diam + jnp.arange(local_diam, dtype=jnp.int32)
    select = (harm_diam[:, None] == diam_ids[None, :]).astype(jnp.bfloat16)
    combined = jnp.einsum(
        "rkc,kh->rhc",
        loads.reshape(rows_dev, NHARM, columns),
        select,
        preferred_element_type=jnp.float32,
    ).astype(jnp.bfloat16)
    shapes = phi.reshape(rows_dev, local_diam, MODES)
    force_part = jnp.einsum(
        "rhm,rhc->hmc", shapes, combined, preferred_element_type=jnp.float32
    ).reshape(half_modes, columns)
    half_start = diam_index * half_modes
    dyn_half = lax.dynamic_slice_in_dim(dyn_diag, half_start, half_modes, 0)[:, None]

    def row_total(partial_term):
        return lax.psum(partial_term, "rows")

    force_half = row_total(force_part)
    amp_half = force_half / dyn_half
    for sweep in range(ITERS):
        full_amp = lax.all_gather(amp_half, "diam", axis=0, tiled=True)
        col_part = lax.dynamic_slice_in_dim(full_amp, row_index * col_width, col_width, 0)
        amp_half = (
            force_half
            - row_total(
                jnp.dot(
                    mistuning,
                    col_part,
                    precision=lax.Precision.HIGHEST,
                    preferred_element_type=jnp.float32,
                )
            )
        ) / dyn_half
    amp_low = amp_half.astype(jnp.bfloat16).reshape(local_diam, MODES, columns)
    sector = jnp.einsum("rhm,hmc->hcr", shapes, amp_low, preferred_element_type=jnp.float32).astype(
        jnp.bfloat16
    )
    table = cyclic_rows(blade_order)
    table_cols = lax.dynamic_slice_in_dim(table, first_diam, local_diam, 1)
    partial_value = jnp.einsum(
        "sh,hcr->scr", table_cols, sector.astype(jnp.float32), precision=lax.Precision.HIGHEST
    )
    blades = lax.psum_scatter(
        partial_value.astype(jnp.bfloat16), "diam", scatter_dimension=0, tiled=True
    )
    return blades


VMEM = pl.BlockSpec(memory_space=pltpu.VMEM)
SMEM = pl.BlockSpec(memory_space=pltpu.SMEM)
HBM = pl.BlockSpec(memory_space=pltpu.HBM)
WIDE = pltpu.CompilerParams(vmem_limit_bytes=16 << 20)
LIMIT = pltpu.CompilerParams(vmem_limit_bytes=8 << 20)


def in_hbm(*values):
    return [pltpu.with_memory_space_constraint(value, pltpu.HBM) for value in values]


def pack(value):
    spare = jnp.zeros((value.shape[0], 2 * LANES - MODES), F32)
    tail = jnp.concatenate([value[:, LANES:], spare], axis=1)
    lane = lax.broadcasted_iota(jnp.int32, (8, LANES), 1)
    middle = []
    for row in (0, 8):
        late = pltpu.roll(tail[row + 16 : row + 24], HALF, 1)
        middle.append(jnp.where(lane < HALF, tail[row : row + 8], late))
    last = jnp.zeros((8, LANES), F32)
    for g in range(4):
        moved = pltpu.roll(tail[8 * g : 8 * g + 8], HALF + 8 * g, 1)
        last = jnp.where((lane >= 8 * g) & (lane < 8 * g + 8), moved, last)
    return jnp.concatenate([value[:, :LANES], *middle, last])


def unpack(packed):
    lane = lax.broadcasted_iota(jnp.int32, (8, LANES), 1)
    tail = []
    for g in range(4):
        row = 32 + 8 * (g % 2)
        middle = packed[row : row + 8]
        if g >= 2:
            middle = pltpu.roll(middle, HALF, 1)
        last = pltpu.roll(packed[48:56], HALF - 8 * g, 1)
        tail.append(jnp.where(lane < HALF, middle, last))
    return jnp.concatenate([packed[:32], jnp.concatenate(tail)], axis=1)[:, :MODES]


def pick(core, even, odd):
    return jnp.where(core == 0, even, odd)


def load_kernel(columns, core_ref, harm_hbm, loads_hbm, phi_hbm, send_ref, mine_ref, phi_send_ref, phi_mine_ref, harm_ref, loads_ref, sems, phi_sems):
    core = core_ref[0]
    pairs = phi_mine_ref.shape[0]
    harm_copy = pltpu.make_async_copy(harm_hbm, harm_ref, sems.at[0])
    harm_copy.start()
    load_copy = pltpu.make_async_copy(loads_hbm, loads_ref, sems.at[1])
    load_copy.start()
    copies = []
    for k in range(pairs):
        for at, ref, odd in ((0, phi_send_ref, 1 - core), (pairs, phi_mine_ref, core)):
            copies.append(
                pltpu.make_async_copy(phi_hbm.at[2 * k + odd], ref.at[k], phi_sems.at[at + k])
            )
    for copy in copies:
        copy.start()
    harm_copy.wait()
    wide = loads_ref.shape[1]
    col = lax.broadcasted_iota(jnp.int32, (8, wide), 1)
    key = jnp.full((8, wide), -1, jnp.int32)
    for k in range(NHARM):
        diam = harm_ref[k] - 2 * pairs * core
        place = pick((diam & 1) - core, pairs, 0) + (diam >> 1)
        place = jnp.where((diam >= 0) & (diam < 2 * pairs), place, 2 * pairs)
        inside = (col >= k * columns) & (col < (k + 1) * columns)
        key = jnp.where(inside, (place - k) * columns + col, key)
    shape = (2 * pairs * columns, wide)
    row = lax.broadcasted_iota(jnp.int32, shape, 0)
    spread = jnp.where(row == jnp.broadcast_to(key[0:1], shape), 1.0, 0.0).astype(BF16)
    load_copy.wait()
    combined = lax.dot_general(
        spread, loads_ref[...], (((1,), (1,)), ((), ())), preferred_element_type=F32
    ).astype(BF16)
    send_ref[...] = combined[: pairs * columns].reshape(send_ref.shape)
    mine_ref[...] = combined[pairs * columns :].reshape(mine_ref.shape)
    for copy in copies:
        copy.wait()


def assemble_kernel(core_ref, mine_ref, recv_ref, out_ref):
    core = core_ref[0]
    pairs = recv_ref.shape[0]
    for half, ref in ((core, mine_ref), (1 - core, recv_ref)):
        for k in range(pairs):
            out_ref[half * pairs + k] = pack(ref[k].astype(F32)).astype(BF16)


def pack_kernel(columns, row_ref, out_ref):
    row = jnp.broadcast_to(row_ref[...], (columns, MODES))
    out = pack(row)
    out_ref[...] = jnp.where(out == 0.0, 1.0, out)


def regroup_kernel(core_ref, stiff_hbm, keep_ref, send_ref, stiff_ref, sems):
    core = core_ref[0]
    chunks = [slice(0, MODES), slice(MODES, 2 * MODES)]
    copies = [
        pltpu.make_async_copy(stiff_hbm.at[rows], stiff_ref.at[rows], sems.at[chunk])
        for chunk, rows in enumerate(chunks)
    ]
    for copy in copies:
        copy.start()
    for chunk, rows in enumerate(chunks):
        copies[chunk].wait()
        stiff = stiff_ref[rows].astype(BF16)
        for k in range(keep_ref.shape[1]):
            even = stiff[:, 2 * k * MODES : (2 * k + 1) * MODES]
            odd = stiff[:, (2 * k + 1) * MODES : (2 * k + 2) * MODES]
            keep_ref[pick(core, chunk, 1 - chunk), k] = pick(core, even, odd)
            send_ref[pick(core, 1 - chunk, chunk), k] = pick(core, odd, even)


def product_kernel(source, core_ref, amp_ref, keep_ref, recv_ref, *rest):
    prev_ref, out_ref = rest if len(rest) == 2 else (None, rest[0])
    core = core_ref[0]
    slots = keep_ref.shape[1]
    amp = unpack(amp_ref[...].astype(F32)).astype(BF16)
    for half, ref in ((core, keep_ref), (1 - core, recv_ref)):
        for k in range(slots):
            at = half * slots + k
            value = jnp.dot(amp, ref[source, k], preferred_element_type=F32)
            if prev_ref is None:
                out_ref[at] = value
            else:
                out_ref[at] = pack(value + prev_ref[at]).astype(BF16)


def blades_kernel(crossed, core_ref, table_ref, amp_ref, own_ref, recv_ref, *rest):
    *prev_ref, out_ref, weights_ref = rest
    core = core_ref[0]
    local_diam = amp_ref.shape[0]
    columns = weights_ref.shape[1] // local_diam
    pairs = local_diam // 2
    odd = 1 - core if crossed else core
    total = prev_ref[0][...] if crossed else 0.0
    for at_half, (half, phi_ref) in enumerate(((core, own_ref), (1 - core, recv_ref))):
        for k in range(pairs):
            at = half * pairs + k
            place = at_half * pairs + k
            amp = unpack(amp_ref[at].astype(F32))
            for s in range(local_diam):
                value = table_ref[s, 2 * at + odd] * amp
                weights_ref[place, s * columns : (s + 1) * columns] = value.astype(BF16)
            total = total + jnp.dot(
                weights_ref[place], phi_ref[2 * k + odd], preferred_element_type=F32
            )
    out_ref[...] = total.astype(out_ref.dtype).reshape(out_ref.shape)


def chunk_plan(phi, loads, harm_diam, mistuning, dyn_diag, blade_order):
    rows_dev, half_modes = phi.shape
    local_diam = half_modes // MODES
    columns = loads.shape[1] // NHARM
    core = lax.axis_index("diam")
    own_diam = 2 * lax.axis_index("rows") + core
    first_diam = core * local_diam
    core_arg = core.reshape(1).astype(jnp.int32)
    pairs = local_diam // 2

    def other_core(value):
        return lax.ppermute(value, "diam", SWAP)

    def exchange(slots):
        return lax.all_to_all(slots, "rows", 0, 0, tiled=True)

    def row_total(got):
        return jnp.sum(got.astype(F32), axis=0)

    shapes = phi.T.reshape(local_diam, MODES, rows_dev)
    half_combined = jax.ShapeDtypeStruct((pairs, columns, rows_dev), BF16)
    half_shapes = jax.ShapeDtypeStruct((pairs, MODES, rows_dev), BF16)
    combined_send, combined_mine, shapes_send, shapes_mine = pl.pallas_call(
        functools.partial(load_kernel, columns),
        name="load",
        in_specs=[SMEM, HBM, HBM, HBM],
        out_specs=[VMEM] * 4,
        out_shape=[half_combined, half_combined, half_shapes, half_shapes],
        scratch_shapes=[
            pltpu.SMEM(harm_diam.shape, jnp.int32),
            pltpu.VMEM(loads.shape, BF16),
            pltpu.SemaphoreType.DMA((2,)),
            pltpu.SemaphoreType.DMA((local_diam,)),
        ],
        compiler_params=LIMIT,
    )(core_arg, *in_hbm(harm_diam, loads, shapes))

    def force_part(combined, near):
        return jnp.einsum("hcr,hmr->hcm", combined, near, preferred_element_type=F32).astype(BF16)

    force_recv = other_core(force_part(combined_send, shapes_send))
    slots_shape = (local_diam,) + PACKED
    force_slots = pl.pallas_call(
        assemble_kernel,
        name="assemble",
        in_specs=[SMEM, VMEM, VMEM],
        out_specs=VMEM,
        out_shape=jax.ShapeDtypeStruct(slots_shape, BF16),
        compiler_params=LIMIT,
    )(core_arg, force_part(combined_mine, shapes_mine), force_recv)
    force_slots, stiff, order, dyn_diag = lax.optimization_barrier(
        (force_slots, mistuning.T, blade_order, dyn_diag)
    )
    force_got = exchange(force_slots)

    group = jax.ShapeDtypeStruct((2, pairs, MODES, MODES), BF16)
    keep, sent = pl.pallas_call(
        regroup_kernel,
        name="regroup",
        in_specs=[SMEM, HBM],
        out_specs=[VMEM, VMEM],
        out_shape=[group, group],
        scratch_shapes=[
            pltpu.VMEM(stiff.shape, F32),
            pltpu.SemaphoreType.DMA((2,)),
        ],
        compiler_params=WIDE,
        cost_estimate=pl.CostEstimate(
            flops=2 * mistuning.size, bytes_accessed=8 * mistuning.size, transcendentals=0
        ),
    )(core_arg, *in_hbm(stiff))
    recv = other_core(sent)
    table = lax.dynamic_slice_in_dim(cyclic_rows(order), first_diam, local_diam, 0)
    dyn_own = pl.pallas_call(
        functools.partial(pack_kernel, columns),
        name="pack",
        in_specs=[VMEM],
        out_specs=VMEM,
        out_shape=jax.ShapeDtypeStruct(PACKED, F32),
        compiler_params=LIMIT,
        cost_estimate=pl.CostEstimate(flops=1, bytes_accessed=1, transcendentals=0),
    )(lax.dynamic_slice_in_dim(dyn_diag, own_diam * MODES, MODES, 0)[None, :])
    force_got, keep, table, dyn_own = lax.optimization_barrier((force_got, keep, table, dyn_own))

    def product(source, *operands):
        return pl.pallas_call(
            functools.partial(product_kernel, source),
            name="product",
            in_specs=[SMEM] + [VMEM] * len(operands),
            out_specs=VMEM,
            out_shape=(
                jax.ShapeDtypeStruct(slots_shape, BF16)
                if source
                else jax.ShapeDtypeStruct((local_diam, columns, MODES), F32)
            ),
            compiler_params=LIMIT,
        )(core_arg, *operands)

    force = row_total(force_got)
    amp = force / dyn_own
    for sweep in range(ITERS):
        amp_low = amp.astype(BF16)
        amp_other = other_core(amp_low)
        part = product(0, amp_low, keep, recv)
        part, amp_other = lax.optimization_barrier((part, amp_other))
        if sweep == ITERS - 1:
            part, shapes_sent = lax.optimization_barrier((part, shapes))
            shapes_received = other_core(shapes_sent)
        part = product(1, amp_other, keep, recv, part)
        amp = (force - row_total(exchange(part))) / dyn_own
    same = exchange(jnp.broadcast_to(amp.astype(BF16)[None], slots_shape))
    crossed = other_core(same)

    def blades(crossed, amps, out_shape, *prev):
        return pl.pallas_call(
            functools.partial(blades_kernel, crossed),
            name="blades",
            in_specs=[SMEM, SMEM] + [VMEM] * (3 + len(prev)),
            out_specs=VMEM,
            out_shape=out_shape,
            scratch_shapes=[pltpu.VMEM((local_diam, local_diam * columns, MODES), BF16)],
            compiler_params=WIDE,
            cost_estimate=pl.CostEstimate(
                flops=2 * local_diam * columns * phi.size,
                bytes_accessed=2 * phi.size,
                transcendentals=0,
            ),
        )(core_arg, table, amps, shapes_sent, shapes_received, *prev)

    part = blades(False, same, jax.ShapeDtypeStruct((local_diam * columns, rows_dev), F32))
    part, crossed = lax.optimization_barrier((part, crossed))
    out_shape = jax.ShapeDtypeStruct((local_diam, columns, rows_dev), BF16)
    return blades(True, crossed, out_shape, part)


def solution(mesh):
    placed = (P("rows", "diam"), P("rows", None), P(), P("diam", "rows"), P("grp"), P())
    one_each = mesh.shape["rows"] * 2 == NBLADE and mesh.shape["diam"] == 2
    return jax.shard_map(
        chunk_plan if one_each else general_plan,
        mesh=mesh,
        in_specs=placed,
        out_specs=P("diam", "grp", "rows"),
        check_vma=False,
    )
```

```python
import functools
import math

import jax
import jax.numpy as jnp
from jax import lax
from jax.experimental import pallas as pl
from jax.experimental.pallas import tpu as pltpu
from jax.sharding import PartitionSpec as P

NBLADE = 16
MODES = 200
NHARM = 16
ITERS = 4
SWAP = [(0, 1), (1, 0)]
F32 = jnp.float32
BF16 = jnp.bfloat16


def cyclic_rows(blade_order):
    count = NBLADE
    blade_pos = jnp.arange(count).astype(jnp.float32)[:, None]
    harmonic = jnp.arange(count)[None, :]
    half_count = count // 2
    wave = jnp.where(harmonic > half_count, harmonic - half_count, harmonic).astype(jnp.float32)
    angle = 2.0 * math.pi * wave * blade_pos / count
    scale = jnp.where(
        (harmonic == 0) | (harmonic == half_count), 1.0 / math.sqrt(count), math.sqrt(2.0 / count)
    )
    cyclic_tab = jnp.where(harmonic > half_count, jnp.sin(angle), jnp.cos(angle)) * scale
    onehot = (blade_order[:, None] == jnp.arange(count)[None, :]).astype(jnp.float32)
    return jnp.dot(onehot, cyclic_tab, precision=lax.Precision.HIGHEST)


def general_plan(phi, loads, harm_diam, mistuning, dyn_diag, blade_order):
    rows_dev = phi.shape[0]
    half_modes = phi.shape[1]
    local_diam = half_modes // MODES
    columns = loads.shape[1] // NHARM
    col_width = mistuning.shape[1]
    diam_index = lax.axis_index("diam")
    row_index = lax.axis_index("rows")
    first_diam = diam_index * local_diam
    diam_ids = first_diam + jnp.arange(local_diam, dtype=jnp.int32)
    select = (harm_diam[:, None] == diam_ids[None, :]).astype(jnp.bfloat16)
    combined = jnp.einsum(
        "rkc,kh->rhc",
        loads.reshape(rows_dev, NHARM, columns),
        select,
        preferred_element_type=jnp.float32,
    ).astype(jnp.bfloat16)
    shapes = phi.reshape(rows_dev, local_diam, MODES)
    force_part = jnp.einsum(
        "rhm,rhc->hmc", shapes, combined, preferred_element_type=jnp.float32
    ).reshape(half_modes, columns)
    half_start = diam_index * half_modes
    dyn_half = lax.dynamic_slice_in_dim(dyn_diag, half_start, half_modes, 0)[:, None]

    def row_total(partial_term):
        return lax.psum(partial_term, "rows")

    force_half = row_total(force_part)
    amp_half = force_half / dyn_half
    for sweep in range(ITERS):
        full_amp = lax.all_gather(amp_half, "diam", axis=0, tiled=True)
        col_part = lax.dynamic_slice_in_dim(full_amp, row_index * col_width, col_width, 0)
        amp_half = (
            force_half
            - row_total(
                jnp.dot(
                    mistuning,
                    col_part,
                    precision=lax.Precision.HIGHEST,
                    preferred_element_type=jnp.float32,
                )
            )
        ) / dyn_half
    amp_low = amp_half.astype(jnp.bfloat16).reshape(local_diam, MODES, columns)
    sector = jnp.einsum("rhm,hmc->hcr", shapes, amp_low, preferred_element_type=jnp.float32).astype(
        jnp.bfloat16
    )
    table = cyclic_rows(blade_order)
    table_cols = lax.dynamic_slice_in_dim(table, first_diam, local_diam, 1)
    partial_value = jnp.einsum(
        "sh,hcr->scr", table_cols, sector.astype(jnp.float32), precision=lax.Precision.HIGHEST
    )
    blades = lax.psum_scatter(
        partial_value.astype(jnp.bfloat16), "diam", scatter_dimension=0, tiled=True
    )
    return blades


VMEM = pl.BlockSpec(memory_space=pltpu.VMEM)
SMEM = pl.BlockSpec(memory_space=pltpu.SMEM)
HBM = pl.BlockSpec(memory_space=pltpu.HBM)
WIDE = pltpu.CompilerParams(vmem_limit_bytes=16 << 20)
LIMIT = pltpu.CompilerParams(vmem_limit_bytes=8 << 20)


def in_hbm(*values):
    return [pltpu.with_memory_space_constraint(value, pltpu.HBM) for value in values]


def pick(core, even, odd):
    return jnp.where(core == 0, even, odd)


def load_kernel(columns, core_ref, harm_hbm, loads_hbm, phi_hbm, send_ref, mine_ref, phi_send_ref, phi_mine_ref, harm_ref, loads_ref, sems):
    core = core_ref[0]
    pairs = phi_mine_ref.shape[0]
    harm_copy = pltpu.make_async_copy(harm_hbm, harm_ref, sems.at[0])
    harm_copy.start()
    load_copy = pltpu.make_async_copy(loads_hbm, loads_ref, sems.at[1])
    load_copy.start()
    copies = [
        pltpu.make_async_copy(phi_hbm.at[:, 1 - core], phi_send_ref, sems.at[2]),
        pltpu.make_async_copy(phi_hbm.at[:, core], phi_mine_ref, sems.at[3]),
    ]
    for copy in copies:
        copy.start()
    harm_copy.wait()
    wide = loads_ref.shape[1]
    col = lax.broadcasted_iota(jnp.int32, (8, wide), 1)
    key = jnp.full((8, wide), -1, jnp.int32)
    for k in range(NHARM):
        diam = harm_ref[k] - 2 * pairs * core
        place = pick((diam & 1) - core, pairs, 0) + (diam >> 1)
        place = jnp.where((diam >= 0) & (diam < 2 * pairs), place, 2 * pairs)
        inside = (col >= k * columns) & (col < (k + 1) * columns)
        key = jnp.where(inside, (place - k) * columns + col, key)
    shape = (2 * pairs * columns, wide)
    row = lax.broadcasted_iota(jnp.int32, shape, 0)
    spread = jnp.where(row == jnp.broadcast_to(key[0:1], shape), 1.0, 0.0).astype(BF16)
    load_copy.wait()
    combined = lax.dot_general(
        spread, loads_ref[...], (((1,), (1,)), ((), ())), preferred_element_type=F32
    ).astype(BF16)
    send_ref[...] = combined[: pairs * columns].reshape(send_ref.shape)
    mine_ref[...] = combined[pairs * columns :].reshape(mine_ref.shape)
    for copy in copies:
        copy.wait()


def assemble_kernel(core_ref, mine_ref, recv_ref, out_ref):
    core = core_ref[0]
    pairs = recv_ref.shape[0]
    for half, ref in ((core, mine_ref), (1 - core, recv_ref)):
        for k in range(pairs):
            out_ref[half * pairs + k] = ref[k]


def regroup_kernel(core_ref, stiff_hbm, keep_ref, send_ref, stiff_ref, sems):
    core = core_ref[0]
    pieces = [(chunk, first, last) for chunk in range(2) for first, last in ((0, 112), (112, MODES))]
    copies = []
    for at, (chunk, first, last) in enumerate(pieces):
        rows = pl.ds(chunk * MODES + first, last - first)
        copies.append(
            pltpu.make_async_copy(stiff_hbm.at[rows], stiff_ref.at[rows], sems.at[at])
        )
        copies[at].start()

    def split(parity, refs, chunk, first, last):
        stiff = stiff_ref[chunk * MODES + first : chunk * MODES + last].astype(BF16)
        for k in range(2 * keep_ref.shape[1]):
            odd = k % 2
            owner = parity if odd == parity else 1 - parity
            at = chunk if owner == 0 else 1 - chunk
            refs[odd][at, k // 2, first:last] = stiff[:, k * MODES : (k + 1) * MODES]

    for at, piece in enumerate(pieces):
        copies[at].wait()

        @pl.when(core == 0)
        def _():
            split(0, (keep_ref, send_ref), *piece)

        @pl.when(core == 1)
        def _():
            split(1, (send_ref, keep_ref), *piece)


def product_kernel(source, core_ref, amp_ref, keep_ref, recv_ref, *rest):
    prev_ref, out_ref = rest if len(rest) == 2 else (None, rest[0])
    core = core_ref[0]
    slots = keep_ref.shape[1]
    for half, ref in ((core, keep_ref), (1 - core, recv_ref)):
        for k in range(slots):
            at = half * slots + k
            value = jnp.dot(amp_ref[...], ref[source, k], preferred_element_type=F32)
            if prev_ref is not None:
                value = value + prev_ref[at]
            out_ref[at] = value.astype(out_ref.dtype)


def parity_weights(odd, core, table_ref, amp_ref, weights_ref):
    local_diam, columns, _ = amp_ref.shape
    pairs = local_diam // 2
    for at_half, half in enumerate((core, 1 - core)):
        for k in range(pairs):
            at = half * pairs + k
            amp = amp_ref[at].astype(F32)
            for s in range(local_diam):
                value = table_ref[s, 2 * at + odd] * amp
                weights_ref[at_half * pairs + k, s * columns : (s + 1) * columns] = value.astype(BF16)


def parity_product(odd, weights_ref, own_ref, recv_ref, total, lanes):
    pairs = own_ref.shape[0] // 2
    for at_half, phi_ref in enumerate((own_ref, recv_ref)):
        for k in range(pairs):
            total = total + jnp.dot(
                weights_ref[at_half * pairs + k],
                phi_ref[2 * k + odd, :, lanes],
                preferred_element_type=F32,
            )
    return total


def same_kernel(core_ref, table_ref, amp_ref, own_ref, recv_ref, out_ref, weights_ref):
    core = core_ref[0]
    parity_weights(core, core, table_ref, amp_ref, weights_ref)
    out_ref[...] = parity_product(core, weights_ref, own_ref, recv_ref, 0.0, slice(None))


def crossed_kernel(core_ref, table_ref, amp_ref, own_ref, recv_ref, prev_ref, out_hbm, weights_ref, out_ref, sems):
    core = core_ref[0]
    parity_weights(1 - core, core, table_ref, amp_ref, weights_ref)
    tiles = sems.shape[0]
    wide = out_ref.shape[2] // tiles
    copies = []
    for tile in range(tiles):
        lanes = slice(tile * wide, (tile + 1) * wide)
        total = prev_ref[:, lanes]
        total = parity_product(1 - core, weights_ref, own_ref, recv_ref, total, lanes)
        out_ref[:, :, lanes] = total.astype(BF16).reshape(out_ref.shape[:2] + (wide,))
        copies.append(
            pltpu.make_async_copy(out_ref.at[:, :, lanes], out_hbm.at[:, :, lanes], sems.at[tile])
        )
        copies[tile].start()
    for copy in copies:
        copy.wait()


def chunk_plan(phi, loads, harm_diam, mistuning, dyn_diag, blade_order):
    rows_dev, half_modes = phi.shape
    local_diam = half_modes // MODES
    columns = loads.shape[1] // NHARM
    core = lax.axis_index("diam")
    own_diam = 2 * lax.axis_index("rows") + core
    first_diam = core * local_diam
    core_arg = core.reshape(1).astype(jnp.int32)
    pairs = local_diam // 2

    def other_core(value):
        return lax.ppermute(value, "diam", SWAP)

    def exchange(slots):
        return lax.all_to_all(slots, "rows", 0, 0, tiled=True)

    def row_total(got):
        return jnp.sum(got.astype(F32), axis=0)

    shapes = phi.T.reshape(local_diam, MODES, rows_dev)
    half_combined = jax.ShapeDtypeStruct((pairs, columns, rows_dev), BF16)
    half_shapes = jax.ShapeDtypeStruct((pairs, MODES, rows_dev), BF16)
    combined_send, combined_mine, shapes_send, shapes_mine = pl.pallas_call(
        functools.partial(load_kernel, columns),
        name="load",
        in_specs=[SMEM, HBM, HBM, HBM],
        out_specs=[VMEM] * 4,
        out_shape=[half_combined, half_combined, half_shapes, half_shapes],
        scratch_shapes=[
            pltpu.SMEM(harm_diam.shape, jnp.int32),
            pltpu.VMEM(loads.shape, BF16),
            pltpu.SemaphoreType.DMA((4,)),
        ],
        compiler_params=LIMIT,
    )(core_arg, *in_hbm(harm_diam, loads, shapes.reshape(pairs, 2, MODES, rows_dev)))

    def force_part(combined, near):
        return jnp.einsum("hcr,hmr->hcm", combined, near, preferred_element_type=F32).astype(BF16)

    force_recv = other_core(force_part(combined_send, shapes_send))
    slots_shape = (local_diam, columns, MODES)
    force_slots = pl.pallas_call(
        assemble_kernel,
        name="assemble",
        in_specs=[SMEM, VMEM, VMEM],
        out_specs=VMEM,
        out_shape=jax.ShapeDtypeStruct(slots_shape, BF16),
        compiler_params=LIMIT,
    )(core_arg, force_part(combined_mine, shapes_mine), force_recv)
    force_slots, stiff, order, dyn_diag = lax.optimization_barrier(
        (force_slots, mistuning.T, blade_order, dyn_diag)
    )
    force_got = exchange(force_slots)

    group = jax.ShapeDtypeStruct((2, pairs, MODES, MODES), BF16)
    keep, sent = pl.pallas_call(
        regroup_kernel,
        name="regroup",
        in_specs=[SMEM, HBM],
        out_specs=[VMEM, VMEM],
        out_shape=[group, group],
        scratch_shapes=[
            pltpu.VMEM(stiff.shape, F32),
            pltpu.SemaphoreType.DMA((4,)),
        ],
        compiler_params=WIDE,
        cost_estimate=pl.CostEstimate(
            flops=2 * mistuning.size, bytes_accessed=8 * mistuning.size, transcendentals=0
        ),
    )(core_arg, *in_hbm(stiff))
    recv = other_core(sent)
    table = lax.dynamic_slice_in_dim(cyclic_rows(order), first_diam, local_diam, 0)
    dyn_own = lax.dynamic_slice_in_dim(dyn_diag, own_diam * MODES, MODES, 0)[None, :]
    force_got, keep, table, dyn_own = lax.optimization_barrier((force_got, keep, table, dyn_own))

    def product(source, *operands):
        return pl.pallas_call(
            functools.partial(product_kernel, source),
            name="product",
            in_specs=[SMEM] + [VMEM] * len(operands),
            out_specs=VMEM,
            out_shape=jax.ShapeDtypeStruct(slots_shape, BF16 if source else F32),
            compiler_params=LIMIT,
        )(core_arg, *operands)

    force = row_total(force_got)
    amp = force / dyn_own
    for sweep in range(ITERS):
        amp_low = amp.astype(BF16)
        amp_other = other_core(amp_low)
        part = product(0, amp_low, keep, recv)
        part, amp_other = lax.optimization_barrier((part, amp_other))
        if sweep == ITERS - 1:
            part, shapes_sent = lax.optimization_barrier((part, shapes))
            shapes_received = other_core(shapes_sent)
        part = product(1, amp_other, keep, recv, part)
        amp = (force - row_total(exchange(part))) / dyn_own
    same = exchange(jnp.broadcast_to(amp.astype(BF16)[None], slots_shape))
    crossed = other_core(same)

    half_cost = pl.CostEstimate(
        flops=2 * local_diam * columns * phi.size, bytes_accessed=2 * phi.size, transcendentals=0
    )
    weights = pltpu.VMEM((local_diam, local_diam * columns, MODES), BF16)
    part = pl.pallas_call(
        same_kernel,
        name="blades_same",
        in_specs=[SMEM, SMEM] + [VMEM] * 3,
        out_specs=VMEM,
        out_shape=jax.ShapeDtypeStruct((local_diam * columns, rows_dev), F32),
        scratch_shapes=[weights],
        compiler_params=WIDE,
        cost_estimate=half_cost,
    )(core_arg, table, same, shapes_sent, shapes_received)
    part, crossed = lax.optimization_barrier((part, crossed))
    out_shape = (local_diam, columns, rows_dev)
    return pl.pallas_call(
        crossed_kernel,
        name="blades_crossed",
        in_specs=[SMEM, SMEM] + [VMEM] * 4,
        out_specs=HBM,
        out_shape=jax.ShapeDtypeStruct(out_shape, BF16),
        scratch_shapes=[weights, pltpu.VMEM(out_shape, BF16), pltpu.SemaphoreType.DMA((4,))],
        compiler_params=WIDE,
        cost_estimate=half_cost,
    )(core_arg, table, crossed, shapes_sent, shapes_received, part)


def solution(mesh):
    placed = (P("rows", "diam"), P("rows", None), P(), P("diam", "rows"), P("grp"), P())
    one_each = mesh.shape["rows"] * 2 == NBLADE and mesh.shape["diam"] == 2
    return jax.shard_map(
        chunk_plan if one_each else general_plan,
        mesh=mesh,
        in_specs=placed,
        out_specs=P("diam", "grp", "rows"),
        check_vma=False,
    )
```

```python
import functools
import math

import jax
import jax.numpy as jnp
from jax import lax
from jax.experimental import pallas as pl
from jax.experimental.pallas import tpu as pltpu
from jax.sharding import PartitionSpec as P

NBLADE = 16
MODES = 200
NHARM = 16
ITERS = 4
SWAP = [(0, 1), (1, 0)]
F32 = jnp.float32
BF16 = jnp.bfloat16


def cyclic_rows(blade_order):
    count = NBLADE
    blade_pos = jnp.arange(count).astype(jnp.float32)[:, None]
    harmonic = jnp.arange(count)[None, :]
    half_count = count // 2
    wave = jnp.where(harmonic > half_count, harmonic - half_count, harmonic).astype(jnp.float32)
    angle = 2.0 * math.pi * wave * blade_pos / count
    scale = jnp.where(
        (harmonic == 0) | (harmonic == half_count), 1.0 / math.sqrt(count), math.sqrt(2.0 / count)
    )
    cyclic_tab = jnp.where(harmonic > half_count, jnp.sin(angle), jnp.cos(angle)) * scale
    onehot = (blade_order[:, None] == jnp.arange(count)[None, :]).astype(jnp.float32)
    return jnp.dot(onehot, cyclic_tab, precision=lax.Precision.HIGHEST)


def general_plan(phi, loads, harm_diam, mistuning, dyn_diag, blade_order):
    rows_dev = phi.shape[0]
    half_modes = phi.shape[1]
    local_diam = half_modes // MODES
    columns = loads.shape[1] // NHARM
    col_width = mistuning.shape[1]
    diam_index = lax.axis_index("diam")
    row_index = lax.axis_index("rows")
    first_diam = diam_index * local_diam
    diam_ids = first_diam + jnp.arange(local_diam, dtype=jnp.int32)
    select = (harm_diam[:, None] == diam_ids[None, :]).astype(jnp.bfloat16)
    combined = jnp.einsum(
        "rkc,kh->rhc",
        loads.reshape(rows_dev, NHARM, columns),
        select,
        preferred_element_type=jnp.float32,
    ).astype(jnp.bfloat16)
    shapes = phi.reshape(rows_dev, local_diam, MODES)
    force_part = jnp.einsum(
        "rhm,rhc->hmc", shapes, combined, preferred_element_type=jnp.float32
    ).reshape(half_modes, columns)
    half_start = diam_index * half_modes
    dyn_half = lax.dynamic_slice_in_dim(dyn_diag, half_start, half_modes, 0)[:, None]

    def row_total(partial_term):
        return lax.psum(partial_term, "rows")

    force_half = row_total(force_part)
    amp_half = force_half / dyn_half
    for sweep in range(ITERS):
        full_amp = lax.all_gather(amp_half, "diam", axis=0, tiled=True)
        col_part = lax.dynamic_slice_in_dim(full_amp, row_index * col_width, col_width, 0)
        amp_half = (
            force_half
            - row_total(
                jnp.dot(
                    mistuning,
                    col_part,
                    precision=lax.Precision.HIGHEST,
                    preferred_element_type=jnp.float32,
                )
            )
        ) / dyn_half
    amp_low = amp_half.astype(jnp.bfloat16).reshape(local_diam, MODES, columns)
    sector = jnp.einsum("rhm,hmc->hcr", shapes, amp_low, preferred_element_type=jnp.float32).astype(
        jnp.bfloat16
    )
    table = cyclic_rows(blade_order)
    table_cols = lax.dynamic_slice_in_dim(table, first_diam, local_diam, 1)
    partial_value = jnp.einsum(
        "sh,hcr->scr", table_cols, sector.astype(jnp.float32), precision=lax.Precision.HIGHEST
    )
    blades = lax.psum_scatter(
        partial_value.astype(jnp.bfloat16), "diam", scatter_dimension=0, tiled=True
    )
    return blades


VMEM = pl.BlockSpec(memory_space=pltpu.VMEM)
SMEM = pl.BlockSpec(memory_space=pltpu.SMEM)
HBM = pl.BlockSpec(memory_space=pltpu.HBM)
WIDE = pltpu.CompilerParams(vmem_limit_bytes=16 << 20)
LIMIT = pltpu.CompilerParams(vmem_limit_bytes=8 << 20)


def in_hbm(*values):
    return [pltpu.with_memory_space_constraint(value, pltpu.HBM) for value in values]


def pick(core, even, odd):
    return jnp.where(core == 0, even, odd)


def load_kernel(columns, core_ref, harm_hbm, loads_hbm, phi_hbm, send_ref, mine_ref, phi_send_ref, phi_mine_ref, harm_ref, loads_ref, sems):
    core = core_ref[0]
    pairs = phi_mine_ref.shape[0]
    harm_copy = pltpu.make_async_copy(harm_hbm, harm_ref, sems.at[0])
    harm_copy.start()
    load_copy = pltpu.make_async_copy(loads_hbm, loads_ref, sems.at[1])
    load_copy.start()
    copies = [
        pltpu.make_async_copy(phi_hbm.at[:, 1 - core], phi_send_ref, sems.at[2]),
        pltpu.make_async_copy(phi_hbm.at[:, core], phi_mine_ref, sems.at[3]),
    ]
    for copy in copies:
        copy.start()
    harm_copy.wait()
    wide = loads_ref.shape[1]
    col = lax.broadcasted_iota(jnp.int32, (8, wide), 1)
    key = jnp.full((8, wide), -1, jnp.int32)
    for k in range(NHARM):
        diam = harm_ref[k] - 2 * pairs * core
        place = pick((diam & 1) - core, pairs, 0) + (diam >> 1)
        place = jnp.where((diam >= 0) & (diam < 2 * pairs), place, 2 * pairs)
        inside = (col >= k * columns) & (col < (k + 1) * columns)
        key = jnp.where(inside, (place - k) * columns + col, key)
    shape = (2 * pairs * columns, wide)
    row = lax.broadcasted_iota(jnp.int32, shape, 0)
    spread = jnp.where(row == jnp.broadcast_to(key[0:1], shape), 1.0, 0.0).astype(BF16)
    load_copy.wait()
    combined = lax.dot_general(
        spread, loads_ref[...], (((1,), (1,)), ((), ())), preferred_element_type=F32
    ).astype(BF16)
    send_ref[...] = combined[: pairs * columns].reshape(send_ref.shape)
    mine_ref[...] = combined[pairs * columns :].reshape(mine_ref.shape)
    for copy in copies:
        copy.wait()


def assemble_kernel(core_ref, mine_ref, recv_ref, out_ref):
    core = core_ref[0]
    pairs = recv_ref.shape[0]
    for half, ref in ((core, mine_ref), (1 - core, recv_ref)):
        for k in range(pairs):
            out_ref[half * pairs + k] = ref[k]


def regroup_kernel(core_ref, stiff_hbm, keep_ref, send_ref, stiff_ref, sems):
    core = core_ref[0]
    pieces = [(chunk, first, last) for chunk in range(2) for first, last in ((0, 112), (112, MODES))]
    copies = []
    for at, (chunk, first, last) in enumerate(pieces):
        rows = pl.ds(chunk * MODES + first, last - first)
        copies.append(
            pltpu.make_async_copy(stiff_hbm.at[rows], stiff_ref.at[rows], sems.at[at])
        )
        copies[at].start()

    def split(parity, refs, chunk, first, last):
        stiff = stiff_ref[chunk * MODES + first : chunk * MODES + last].astype(BF16)
        for k in range(2 * keep_ref.shape[1]):
            odd = k % 2
            owner = parity if odd == parity else 1 - parity
            at = chunk if owner == 0 else 1 - chunk
            refs[odd][at, k // 2, first:last] = stiff[:, k * MODES : (k + 1) * MODES]

    for at, piece in enumerate(pieces):
        copies[at].wait()

        @pl.when(core == 0)
        def _():
            split(0, (keep_ref, send_ref), *piece)

        @pl.when(core == 1)
        def _():
            split(1, (send_ref, keep_ref), *piece)


def product_kernel(source, core_ref, amp_ref, keep_ref, recv_ref, *rest):
    prev_ref, out_ref = rest if len(rest) == 2 else (None, rest[0])
    core = core_ref[0]
    slots = keep_ref.shape[1]
    for half, ref in ((core, keep_ref), (1 - core, recv_ref)):
        for k in range(slots):
            at = half * slots + k
            value = jnp.dot(amp_ref[...], ref[source, k], preferred_element_type=F32)
            if prev_ref is not None:
                value = value + prev_ref[at]
            out_ref[at] = value.astype(out_ref.dtype)


def parity_weights(odd, core, table_ref, amp_ref, weights_ref):
    local_diam, columns, _ = amp_ref.shape
    pairs = local_diam // 2
    for at_half, half in enumerate((core, 1 - core)):
        for k in range(pairs):
            at = half * pairs + k
            amp = amp_ref[at].astype(F32)
            for s in range(local_diam):
                value = table_ref[2 * at + odd, s : s + 1] * amp
                weights_ref[at_half * pairs + k, s * columns : (s + 1) * columns] = value.astype(BF16)


def parity_product(odd, weights_ref, own_ref, recv_ref, total, lanes):
    pairs = own_ref.shape[0] // 2
    for at_half, phi_ref in enumerate((own_ref, recv_ref)):
        for k in range(pairs):
            total = total + jnp.dot(
                weights_ref[at_half * pairs + k],
                phi_ref[2 * k + odd, :, lanes],
                preferred_element_type=F32,
            )
    return total


def same_kernel(core_ref, table_ref, amp_ref, own_ref, recv_ref, out_ref, weights_ref):
    core = core_ref[0]
    parity_weights(core, core, table_ref, amp_ref, weights_ref)
    out_ref[...] = parity_product(core, weights_ref, own_ref, recv_ref, 0.0, slice(None))


def crossed_kernel(core_ref, table_ref, amp_ref, own_ref, recv_ref, prev_ref, out_hbm, weights_ref, out_ref, sems):
    core = core_ref[0]
    parity_weights(1 - core, core, table_ref, amp_ref, weights_ref)
    tiles = sems.shape[0]
    wide = out_ref.shape[2] // tiles
    copies = []
    for tile in range(tiles):
        lanes = slice(tile * wide, (tile + 1) * wide)
        total = prev_ref[:, lanes]
        total = parity_product(1 - core, weights_ref, own_ref, recv_ref, total, lanes)
        out_ref[:, :, lanes] = total.astype(BF16).reshape(out_ref.shape[:2] + (wide,))
        copies.append(
            pltpu.make_async_copy(out_ref.at[:, :, lanes], out_hbm.at[:, :, lanes], sems.at[tile])
        )
        copies[tile].start()
    for copy in copies:
        copy.wait()


def chunk_plan(phi, loads, harm_diam, mistuning, dyn_diag, blade_order):
    rows_dev, half_modes = phi.shape
    local_diam = half_modes // MODES
    columns = loads.shape[1] // NHARM
    core = lax.axis_index("diam")
    own_diam = 2 * lax.axis_index("rows") + core
    first_diam = core * local_diam
    core_arg = core.reshape(1).astype(jnp.int32)
    pairs = local_diam // 2

    def other_core(value):
        return lax.ppermute(value, "diam", SWAP)

    def exchange(slots):
        return lax.all_to_all(slots, "rows", 0, 0, tiled=True)

    def row_total(got):
        return jnp.sum(got.astype(F32), axis=0)

    shapes = phi.T.reshape(local_diam, MODES, rows_dev)
    half_combined = jax.ShapeDtypeStruct((pairs, columns, rows_dev), BF16)
    half_shapes = jax.ShapeDtypeStruct((pairs, MODES, rows_dev), BF16)
    combined_send, combined_mine, shapes_send, shapes_mine = pl.pallas_call(
        functools.partial(load_kernel, columns),
        name="load",
        in_specs=[SMEM, HBM, HBM, HBM],
        out_specs=[VMEM] * 4,
        out_shape=[half_combined, half_combined, half_shapes, half_shapes],
        scratch_shapes=[
            pltpu.SMEM(harm_diam.shape, jnp.int32),
            pltpu.VMEM(loads.shape, BF16),
            pltpu.SemaphoreType.DMA((4,)),
        ],
        compiler_params=LIMIT,
    )(core_arg, *in_hbm(harm_diam, loads, shapes.reshape(pairs, 2, MODES, rows_dev)))

    def force_part(combined, near):
        return jnp.einsum("hcr,hmr->hcm", combined, near, preferred_element_type=F32).astype(BF16)

    force_recv = other_core(force_part(combined_send, shapes_send))
    slots_shape = (local_diam, columns, MODES)
    force_slots = pl.pallas_call(
        assemble_kernel,
        name="assemble",
        in_specs=[SMEM, VMEM, VMEM],
        out_specs=VMEM,
        out_shape=jax.ShapeDtypeStruct(slots_shape, BF16),
        compiler_params=LIMIT,
    )(core_arg, force_part(combined_mine, shapes_mine), force_recv)
    force_slots, stiff, order, dyn_diag = lax.optimization_barrier(
        (force_slots, mistuning.T, blade_order, dyn_diag)
    )
    force_got = exchange(force_slots)

    group = jax.ShapeDtypeStruct((2, pairs, MODES, MODES), BF16)
    keep, sent = pl.pallas_call(
        regroup_kernel,
        name="regroup",
        in_specs=[SMEM, HBM],
        out_specs=[VMEM, VMEM],
        out_shape=[group, group],
        scratch_shapes=[
            pltpu.VMEM(stiff.shape, F32),
            pltpu.SemaphoreType.DMA((4,)),
        ],
        compiler_params=WIDE,
        cost_estimate=pl.CostEstimate(
            flops=2 * mistuning.size, bytes_accessed=8 * mistuning.size, transcendentals=0
        ),
    )(core_arg, *in_hbm(stiff))
    recv = other_core(sent)
    table = lax.dynamic_slice_in_dim(cyclic_rows(order), first_diam, local_diam, 0)
    table = jnp.broadcast_to(table.T[:, :, None], (NBLADE, local_diam, MODES))
    dyn_own = lax.dynamic_slice_in_dim(dyn_diag, own_diam * MODES, MODES, 0)[None, :]
    force_got, keep, table, dyn_own = lax.optimization_barrier((force_got, keep, table, dyn_own))

    def product(source, *operands):
        return pl.pallas_call(
            functools.partial(product_kernel, source),
            name="product",
            in_specs=[SMEM] + [VMEM] * len(operands),
            out_specs=VMEM,
            out_shape=jax.ShapeDtypeStruct(slots_shape, BF16 if source else F32),
            compiler_params=LIMIT,
        )(core_arg, *operands)

    force = row_total(force_got)
    amp = force / dyn_own
    for sweep in range(ITERS):
        amp_low = amp.astype(BF16)
        amp_other = other_core(amp_low)
        part = product(0, amp_low, keep, recv)
        part, amp_other = lax.optimization_barrier((part, amp_other))
        if sweep == ITERS - 1:
            part, shapes_sent = lax.optimization_barrier((part, shapes))
            shapes_received = other_core(shapes_sent)
        part = product(1, amp_other, keep, recv, part)
        amp = (force - row_total(exchange(part))) / dyn_own
    same = exchange(jnp.broadcast_to(amp.astype(BF16)[None], slots_shape))
    crossed = other_core(same)

    half_cost = pl.CostEstimate(
        flops=2 * local_diam * columns * phi.size, bytes_accessed=2 * phi.size, transcendentals=0
    )
    weights = pltpu.VMEM((local_diam, local_diam * columns, MODES), BF16)
    part = pl.pallas_call(
        same_kernel,
        name="blades_same",
        in_specs=[SMEM] + [VMEM] * 4,
        out_specs=VMEM,
        out_shape=jax.ShapeDtypeStruct((local_diam * columns, rows_dev), F32),
        scratch_shapes=[weights],
        compiler_params=WIDE,
        cost_estimate=half_cost,
    )(core_arg, table, same, shapes_sent, shapes_received)
    part, crossed = lax.optimization_barrier((part, crossed))
    out_shape = (local_diam, columns, rows_dev)
    return pl.pallas_call(
        crossed_kernel,
        name="blades_crossed",
        in_specs=[SMEM] + [VMEM] * 5,
        out_specs=HBM,
        out_shape=jax.ShapeDtypeStruct(out_shape, BF16),
        scratch_shapes=[weights, pltpu.VMEM(out_shape, BF16), pltpu.SemaphoreType.DMA((4,))],
        compiler_params=WIDE,
        cost_estimate=half_cost,
    )(core_arg, table, crossed, shapes_sent, shapes_received, part)


def solution(mesh):
    placed = (P("rows", "diam"), P("rows", None), P(), P("diam", "rows"), P("grp"), P())
    one_each = mesh.shape["rows"] * 2 == NBLADE and mesh.shape["diam"] == 2
    return jax.shard_map(
        chunk_plan if one_each else general_plan,
        mesh=mesh,
        in_specs=placed,
        out_specs=P("diam", "grp", "rows"),
        check_vma=False,
    )
```

```python
import functools
import math

import jax
import jax.numpy as jnp
from jax import lax
from jax.experimental import pallas as pl
from jax.experimental.pallas import tpu as pltpu
from jax.sharding import PartitionSpec as P

NBLADE = 16
MODES = 200
NHARM = 16
ITERS = 4
SWAP = [(0, 1), (1, 0)]
LANES = 128
HALF = 64
PACKED = (56, LANES)
F32 = jnp.float32
BF16 = jnp.bfloat16


def cyclic_rows(blade_order):
    count = NBLADE
    blade_pos = jnp.arange(count).astype(jnp.float32)[:, None]
    harmonic = jnp.arange(count)[None, :]
    half_count = count // 2
    wave = jnp.where(harmonic > half_count, harmonic - half_count, harmonic).astype(jnp.float32)
    angle = 2.0 * math.pi * wave * blade_pos / count
    scale = jnp.where(
        (harmonic == 0) | (harmonic == half_count), 1.0 / math.sqrt(count), math.sqrt(2.0 / count)
    )
    cyclic_tab = jnp.where(harmonic > half_count, jnp.sin(angle), jnp.cos(angle)) * scale
    onehot = (blade_order[:, None] == jnp.arange(count)[None, :]).astype(jnp.float32)
    return jnp.dot(onehot, cyclic_tab, precision=lax.Precision.HIGHEST)


def general_plan(phi, loads, harm_diam, mistuning, dyn_diag, blade_order):
    rows_dev = phi.shape[0]
    half_modes = phi.shape[1]
    local_diam = half_modes // MODES
    columns = loads.shape[1] // NHARM
    col_width = mistuning.shape[1]
    diam_index = lax.axis_index("diam")
    row_index = lax.axis_index("rows")
    first_diam = diam_index * local_diam
    diam_ids = first_diam + jnp.arange(local_diam, dtype=jnp.int32)
    select = (harm_diam[:, None] == diam_ids[None, :]).astype(jnp.bfloat16)
    combined = jnp.einsum(
        "rkc,kh->rhc",
        loads.reshape(rows_dev, NHARM, columns),
        select,
        preferred_element_type=jnp.float32,
    ).astype(jnp.bfloat16)
    shapes = phi.reshape(rows_dev, local_diam, MODES)
    force_part = jnp.einsum(
        "rhm,rhc->hmc", shapes, combined, preferred_element_type=jnp.float32
    ).reshape(half_modes, columns)
    half_start = diam_index * half_modes
    dyn_half = lax.dynamic_slice_in_dim(dyn_diag, half_start, half_modes, 0)[:, None]

    def row_total(partial_term):
        return lax.psum(partial_term, "rows")

    force_half = row_total(force_part)
    amp_half = force_half / dyn_half
    for sweep in range(ITERS):
        full_amp = lax.all_gather(amp_half, "diam", axis=0, tiled=True)
        col_part = lax.dynamic_slice_in_dim(full_amp, row_index * col_width, col_width, 0)
        amp_half = (
            force_half
            - row_total(
                jnp.dot(
                    mistuning,
                    col_part,
                    precision=lax.Precision.HIGHEST,
                    preferred_element_type=jnp.float32,
                )
            )
        ) / dyn_half
    amp_low = amp_half.astype(jnp.bfloat16).reshape(local_diam, MODES, columns)
    sector = jnp.einsum("rhm,hmc->hcr", shapes, amp_low, preferred_element_type=jnp.float32).astype(
        jnp.bfloat16
    )
    table = cyclic_rows(blade_order)
    table_cols = lax.dynamic_slice_in_dim(table, first_diam, local_diam, 1)
    partial_value = jnp.einsum(
        "sh,hcr->scr", table_cols, sector.astype(jnp.float32), precision=lax.Precision.HIGHEST
    )
    blades = lax.psum_scatter(
        partial_value.astype(jnp.bfloat16), "diam", scatter_dimension=0, tiled=True
    )
    return blades


VMEM = pl.BlockSpec(memory_space=pltpu.VMEM)
SMEM = pl.BlockSpec(memory_space=pltpu.SMEM)
HBM = pl.BlockSpec(memory_space=pltpu.HBM)
WIDE = pltpu.CompilerParams(vmem_limit_bytes=16 << 20)
LIMIT = pltpu.CompilerParams(vmem_limit_bytes=8 << 20)


def in_hbm(*values):
    return [pltpu.with_memory_space_constraint(value, pltpu.HBM) for value in values]


def pack(value):
    spare = jnp.zeros((value.shape[0], 2 * LANES - MODES), F32)
    tail = jnp.concatenate([value[:, LANES:], spare], axis=1)
    lane = lax.broadcasted_iota(jnp.int32, (8, LANES), 1)
    middle = []
    for row in (0, 8):
        late = pltpu.roll(tail[row + 16 : row + 24], HALF, 1)
        middle.append(jnp.where(lane < HALF, tail[row : row + 8], late))
    last = jnp.zeros((8, LANES), F32)
    for g in range(4):
        moved = pltpu.roll(tail[8 * g : 8 * g + 8], HALF + 8 * g, 1)
        last = jnp.where((lane >= 8 * g) & (lane < 8 * g + 8), moved, last)
    return jnp.concatenate([value[:, :LANES], *middle, last])


def unpack(packed):
    lane = lax.broadcasted_iota(jnp.int32, (8, LANES), 1)
    tail = []
    for g in range(4):
        row = 32 + 8 * (g % 2)
        middle = packed[row : row + 8]
        if g >= 2:
            middle = pltpu.roll(middle, HALF, 1)
        last = pltpu.roll(packed[48:56], HALF - 8 * g, 1)
        tail.append(jnp.where(lane < HALF, middle, last))
    return jnp.concatenate([packed[:32], jnp.concatenate(tail)], axis=1)[:, :MODES]


def pick(core, even, odd):
    return jnp.where(core == 0, even, odd)


def load_kernel(columns, core_ref, harm_hbm, loads_hbm, phi_hbm, send_ref, mine_ref, phi_send_ref, phi_mine_ref, harm_ref, loads_ref, sems):
    core = core_ref[0]
    pairs = phi_mine_ref.shape[0]
    harm_copy = pltpu.make_async_copy(harm_hbm, harm_ref, sems.at[0])
    harm_copy.start()
    load_copy = pltpu.make_async_copy(loads_hbm, loads_ref, sems.at[1])
    load_copy.start()
    copies = [
        pltpu.make_async_copy(phi_hbm.at[:, 1 - core], phi_send_ref, sems.at[2]),
        pltpu.make_async_copy(phi_hbm.at[:, core], phi_mine_ref, sems.at[3]),
    ]
    for copy in copies:
        copy.start()
    harm_copy.wait()
    wide = loads_ref.shape[1]
    col = lax.broadcasted_iota(jnp.int32, (8, wide), 1)
    key = jnp.full((8, wide), -1, jnp.int32)
    for k in range(NHARM):
        diam = harm_ref[k] - 2 * pairs * core
        place = pick((diam & 1) - core, pairs, 0) + (diam >> 1)
        place = jnp.where((diam >= 0) & (diam < 2 * pairs), place, 2 * pairs)
        inside = (col >= k * columns) & (col < (k + 1) * columns)
        key = jnp.where(inside, (place - k) * columns + col, key)
    shape = (2 * pairs * columns, wide)
    row = lax.broadcasted_iota(jnp.int32, shape, 0)
    spread = jnp.where(row == jnp.broadcast_to(key[0:1], shape), 1.0, 0.0).astype(BF16)
    load_copy.wait()
    combined = lax.dot_general(
        spread, loads_ref[...], (((1,), (1,)), ((), ())), preferred_element_type=F32
    ).astype(BF16)
    send_ref[...] = combined[: pairs * columns].reshape(send_ref.shape)
    mine_ref[...] = combined[pairs * columns :].reshape(mine_ref.shape)
    for copy in copies:
        copy.wait()


def assemble_kernel(core_ref, mine_ref, recv_ref, out_ref):
    core = core_ref[0]
    pairs = recv_ref.shape[0]
    for half, ref in ((core, mine_ref), (1 - core, recv_ref)):
        for k in range(pairs):
            out_ref[half * pairs + k] = pack(ref[k].astype(F32)).astype(BF16)


def pack_kernel(columns, row_ref, out_ref):
    row = jnp.broadcast_to(row_ref[...], (columns, MODES))
    out = pack(row)
    out_ref[...] = jnp.where(out == 0.0, 1.0, out)


def regroup_kernel(core_ref, stiff_hbm, keep_ref, send_ref, stiff_ref, sems):
    core = core_ref[0]
    pieces = [(chunk, first, last) for chunk in range(2) for first, last in ((0, 112), (112, MODES))]
    copies = []
    for at, (chunk, first, last) in enumerate(pieces):
        rows = pl.ds(chunk * MODES + first, last - first)
        copies.append(
            pltpu.make_async_copy(stiff_hbm.at[rows], stiff_ref.at[rows], sems.at[at])
        )
        copies[at].start()

    def split(parity, refs, chunk, first, last):
        stiff = stiff_ref[chunk * MODES + first : chunk * MODES + last].astype(BF16)
        for k in range(2 * keep_ref.shape[1]):
            odd = k % 2
            owner = parity if odd == parity else 1 - parity
            at = chunk if owner == 0 else 1 - chunk
            refs[odd][at, k // 2, first:last] = stiff[:, k * MODES : (k + 1) * MODES]

    for at, piece in enumerate(pieces):
        copies[at].wait()

        @pl.when(core == 0)
        def _():
            split(0, (keep_ref, send_ref), *piece)

        @pl.when(core == 1)
        def _():
            split(1, (send_ref, keep_ref), *piece)


def product_kernel(source, core_ref, amp_ref, keep_ref, recv_ref, *rest):
    prev_ref, out_ref = rest if len(rest) == 2 else (None, rest[0])
    core = core_ref[0]
    slots = keep_ref.shape[1]
    amp = unpack(amp_ref[...].astype(F32)).astype(BF16)
    for half, ref in ((core, keep_ref), (1 - core, recv_ref)):
        for k in range(slots):
            at = half * slots + k
            value = pack(jnp.dot(amp, ref[source, k], preferred_element_type=F32))
            if prev_ref is not None:
                value = value + prev_ref[at]
            out_ref[at] = value.astype(out_ref.dtype)


def parity_weights(odd, core, table_ref, amp_ref, weights_ref):
    local_diam = amp_ref.shape[0]
    columns = weights_ref.shape[1] // local_diam
    pairs = local_diam // 2
    for at_half, half in enumerate((core, 1 - core)):
        for k in range(pairs):
            at = half * pairs + k
            amp = unpack(amp_ref[at].astype(F32))
            for s in range(local_diam):
                value = table_ref[2 * at + odd, s : s + 1] * amp
                weights_ref[at_half * pairs + k, s * columns : (s + 1) * columns] = value.astype(BF16)


def parity_product(odd, weights_ref, own_ref, recv_ref, total, lanes):
    pairs = own_ref.shape[0] // 2
    for at_half, phi_ref in enumerate((own_ref, recv_ref)):
        for k in range(pairs):
            total = total + jnp.dot(
                weights_ref[at_half * pairs + k],
                phi_ref[2 * k + odd, :, lanes],
                preferred_element_type=F32,
            )
    return total


def same_kernel(core_ref, table_ref, amp_ref, own_ref, recv_ref, out_ref, weights_ref):
    core = core_ref[0]
    parity_weights(core, core, table_ref, amp_ref, weights_ref)
    out_ref[...] = parity_product(core, weights_ref, own_ref, recv_ref, 0.0, slice(None))


def crossed_kernel(core_ref, table_ref, amp_ref, own_ref, recv_ref, prev_ref, out_hbm, weights_ref, out_ref, sems):
    core = core_ref[0]
    parity_weights(1 - core, core, table_ref, amp_ref, weights_ref)
    tiles = sems.shape[0]
    wide = out_ref.shape[2] // tiles
    copies = []
    for tile in range(tiles):
        lanes = slice(tile * wide, (tile + 1) * wide)
        total = prev_ref[:, lanes]
        total = parity_product(1 - core, weights_ref, own_ref, recv_ref, total, lanes)
        out_ref[:, :, lanes] = total.astype(BF16).reshape(out_ref.shape[:2] + (wide,))
        copies.append(
            pltpu.make_async_copy(out_ref.at[:, :, lanes], out_hbm.at[:, :, lanes], sems.at[tile])
        )
        copies[tile].start()
    for copy in copies:
        copy.wait()


def chunk_plan(phi, loads, harm_diam, mistuning, dyn_diag, blade_order):
    rows_dev, half_modes = phi.shape
    local_diam = half_modes // MODES
    columns = loads.shape[1] // NHARM
    core = lax.axis_index("diam")
    own_diam = 2 * lax.axis_index("rows") + core
    first_diam = core * local_diam
    core_arg = core.reshape(1).astype(jnp.int32)
    pairs = local_diam // 2

    def other_core(value):
        return lax.ppermute(value, "diam", SWAP)

    def exchange(slots):
        return lax.all_to_all(slots, "rows", 0, 0, tiled=True)

    def row_total(got):
        return jnp.sum(got.astype(F32), axis=0)

    shapes = phi.T.reshape(local_diam, MODES, rows_dev)
    half_combined = jax.ShapeDtypeStruct((pairs, columns, rows_dev), BF16)
    half_shapes = jax.ShapeDtypeStruct((pairs, MODES, rows_dev), BF16)
    combined_send, combined_mine, shapes_send, shapes_mine = pl.pallas_call(
        functools.partial(load_kernel, columns),
        name="load",
        in_specs=[SMEM, HBM, HBM, HBM],
        out_specs=[VMEM] * 4,
        out_shape=[half_combined, half_combined, half_shapes, half_shapes],
        scratch_shapes=[
            pltpu.SMEM(harm_diam.shape, jnp.int32),
            pltpu.VMEM(loads.shape, BF16),
            pltpu.SemaphoreType.DMA((4,)),
        ],
        compiler_params=LIMIT,
    )(core_arg, *in_hbm(harm_diam, loads, shapes.reshape(pairs, 2, MODES, rows_dev)))

    def force_part(combined, near):
        return jnp.einsum("hcr,hmr->hcm", combined, near, preferred_element_type=F32).astype(BF16)

    force_recv = other_core(force_part(combined_send, shapes_send))
    slots_shape = (local_diam,) + PACKED
    force_slots = pl.pallas_call(
        assemble_kernel,
        name="assemble",
        in_specs=[SMEM, VMEM, VMEM],
        out_specs=VMEM,
        out_shape=jax.ShapeDtypeStruct(slots_shape, BF16),
        compiler_params=LIMIT,
    )(core_arg, force_part(combined_mine, shapes_mine), force_recv)
    force_slots, stiff, order, dyn_diag = lax.optimization_barrier(
        (force_slots, mistuning.T, blade_order, dyn_diag)
    )
    force_got = exchange(force_slots)

    group = jax.ShapeDtypeStruct((2, pairs, MODES, MODES), BF16)
    keep, sent = pl.pallas_call(
        regroup_kernel,
        name="regroup",
        in_specs=[SMEM, HBM],
        out_specs=[VMEM, VMEM],
        out_shape=[group, group],
        scratch_shapes=[
            pltpu.VMEM(stiff.shape, F32),
            pltpu.SemaphoreType.DMA((4,)),
        ],
        compiler_params=WIDE,
        cost_estimate=pl.CostEstimate(
            flops=2 * mistuning.size, bytes_accessed=8 * mistuning.size, transcendentals=0
        ),
    )(core_arg, *in_hbm(stiff))
    recv = other_core(sent)
    table = lax.dynamic_slice_in_dim(cyclic_rows(order), first_diam, local_diam, 0)
    table = jnp.broadcast_to(table.T[:, :, None], (NBLADE, local_diam, MODES))
    dyn_own = pl.pallas_call(
        functools.partial(pack_kernel, columns),
        name="pack",
        in_specs=[VMEM],
        out_specs=VMEM,
        out_shape=jax.ShapeDtypeStruct(PACKED, F32),
        compiler_params=LIMIT,
        cost_estimate=pl.CostEstimate(flops=1, bytes_accessed=1, transcendentals=0),
    )(lax.dynamic_slice_in_dim(dyn_diag, own_diam * MODES, MODES, 0)[None, :])
    force_got, keep, table, dyn_own = lax.optimization_barrier((force_got, keep, table, dyn_own))

    def product(source, *operands):
        return pl.pallas_call(
            functools.partial(product_kernel, source),
            name="product",
            in_specs=[SMEM] + [VMEM] * len(operands),
            out_specs=VMEM,
            out_shape=jax.ShapeDtypeStruct(slots_shape, BF16 if source else F32),
            compiler_params=LIMIT,
        )(core_arg, *operands)

    force = row_total(force_got)
    amp = force / dyn_own
    for sweep in range(ITERS):
        amp_low = amp.astype(BF16)
        amp_other = other_core(amp_low)
        part = product(0, amp_low, keep, recv)
        part, amp_other = lax.optimization_barrier((part, amp_other))
        if sweep == ITERS - 1:
            part, shapes_sent = lax.optimization_barrier((part, shapes))
            shapes_received = other_core(shapes_sent)
        part = product(1, amp_other, keep, recv, part)
        amp = (force - row_total(exchange(part))) / dyn_own
    same = exchange(jnp.broadcast_to(amp.astype(BF16)[None], slots_shape))
    crossed = other_core(same)

    half_cost = pl.CostEstimate(
        flops=2 * local_diam * columns * phi.size, bytes_accessed=2 * phi.size, transcendentals=0
    )
    weights = pltpu.VMEM((local_diam, local_diam * columns, MODES), BF16)
    part = pl.pallas_call(
        same_kernel,
        name="blades_same",
        in_specs=[SMEM] + [VMEM] * 4,
        out_specs=VMEM,
        out_shape=jax.ShapeDtypeStruct((local_diam * columns, rows_dev), F32),
        scratch_shapes=[weights],
        compiler_params=WIDE,
        cost_estimate=half_cost,
    )(core_arg, table, same, shapes_sent, shapes_received)
    part, crossed = lax.optimization_barrier((part, crossed))
    out_shape = (local_diam, columns, rows_dev)
    return pl.pallas_call(
        crossed_kernel,
        name="blades_crossed",
        in_specs=[SMEM] + [VMEM] * 5,
        out_specs=HBM,
        out_shape=jax.ShapeDtypeStruct(out_shape, BF16),
        scratch_shapes=[weights, pltpu.VMEM(out_shape, BF16), pltpu.SemaphoreType.DMA((4,))],
        compiler_params=WIDE,
        cost_estimate=half_cost,
    )(core_arg, table, crossed, shapes_sent, shapes_received, part)


def solution(mesh):
    placed = (P("rows", "diam"), P("rows", None), P(), P("diam", "rows"), P("grp"), P())
    one_each = mesh.shape["rows"] * 2 == NBLADE and mesh.shape["diam"] == 2
    return jax.shard_map(
        chunk_plan if one_each else general_plan,
        mesh=mesh,
        in_specs=placed,
        out_specs=P("diam", "grp", "rows"),
        check_vma=False,
    )
```

```python
import functools
import math

import jax
import jax.numpy as jnp
from jax import lax
from jax.experimental import pallas as pl
from jax.experimental.pallas import tpu as pltpu
from jax.sharding import PartitionSpec as P

NBLADE = 16
MODES = 200
NHARM = 16
ITERS = 4
SWAP = [(0, 1), (1, 0)]
LANES = 128
HALF = 64
HUB = 2
PACKED = (56, LANES)
F32 = jnp.float32
BF16 = jnp.bfloat16


def cyclic_rows(blade_order):
    count = NBLADE
    blade_pos = jnp.arange(count).astype(jnp.float32)[:, None]
    harmonic = jnp.arange(count)[None, :]
    half_count = count // 2
    wave = jnp.where(harmonic > half_count, harmonic - half_count, harmonic).astype(jnp.float32)
    angle = 2.0 * math.pi * wave * blade_pos / count
    scale = jnp.where(
        (harmonic == 0) | (harmonic == half_count), 1.0 / math.sqrt(count), math.sqrt(2.0 / count)
    )
    cyclic_tab = jnp.where(harmonic > half_count, jnp.sin(angle), jnp.cos(angle)) * scale
    onehot = (blade_order[:, None] == jnp.arange(count)[None, :]).astype(jnp.float32)
    return jnp.dot(onehot, cyclic_tab, precision=lax.Precision.HIGHEST)


def general_plan(phi, loads, harm_diam, mistuning, dyn_diag, blade_order):
    rows_dev = phi.shape[0]
    half_modes = phi.shape[1]
    local_diam = half_modes // MODES
    columns = loads.shape[1] // NHARM
    col_width = mistuning.shape[1]
    diam_index = lax.axis_index("diam")
    row_index = lax.axis_index("rows")
    first_diam = diam_index * local_diam
    diam_ids = first_diam + jnp.arange(local_diam, dtype=jnp.int32)
    select = (harm_diam[:, None] == diam_ids[None, :]).astype(jnp.bfloat16)
    combined = jnp.einsum(
        "rkc,kh->rhc",
        loads.reshape(rows_dev, NHARM, columns),
        select,
        preferred_element_type=jnp.float32,
    ).astype(jnp.bfloat16)
    shapes = phi.reshape(rows_dev, local_diam, MODES)
    force_part = jnp.einsum(
        "rhm,rhc->hmc", shapes, combined, preferred_element_type=jnp.float32
    ).reshape(half_modes, columns)
    half_start = diam_index * half_modes
    dyn_half = lax.dynamic_slice_in_dim(dyn_diag, half_start, half_modes, 0)[:, None]

    def row_total(partial_term):
        return lax.psum(partial_term, "rows")

    force_half = row_total(force_part)
    amp_half = force_half / dyn_half
    for sweep in range(ITERS):
        full_amp = lax.all_gather(amp_half, "diam", axis=0, tiled=True)
        col_part = lax.dynamic_slice_in_dim(full_amp, row_index * col_width, col_width, 0)
        amp_half = (
            force_half
            - row_total(
                jnp.dot(
                    mistuning,
                    col_part,
                    precision=lax.Precision.HIGHEST,
                    preferred_element_type=jnp.float32,
                )
            )
        ) / dyn_half
    amp_low = amp_half.astype(jnp.bfloat16).reshape(local_diam, MODES, columns)
    sector = jnp.einsum("rhm,hmc->hcr", shapes, amp_low, preferred_element_type=jnp.float32).astype(
        jnp.bfloat16
    )
    table = cyclic_rows(blade_order)
    table_cols = lax.dynamic_slice_in_dim(table, first_diam, local_diam, 1)
    partial_value = jnp.einsum(
        "sh,hcr->scr", table_cols, sector.astype(jnp.float32), precision=lax.Precision.HIGHEST
    )
    blades = lax.psum_scatter(
        partial_value.astype(jnp.bfloat16), "diam", scatter_dimension=0, tiled=True
    )
    return blades


VMEM = pl.BlockSpec(memory_space=pltpu.VMEM)
SMEM = pl.BlockSpec(memory_space=pltpu.SMEM)
HBM = pl.BlockSpec(memory_space=pltpu.HBM)
WIDE = pltpu.CompilerParams(vmem_limit_bytes=16 << 20)
LIMIT = pltpu.CompilerParams(vmem_limit_bytes=8 << 20)


def in_hbm(*values):
    return [pltpu.with_memory_space_constraint(value, pltpu.HBM) for value in values]


def pack(value):
    spare = jnp.zeros((value.shape[0], 2 * LANES - MODES), F32)
    tail = jnp.concatenate([value[:, LANES:], spare], axis=1)
    lane = lax.broadcasted_iota(jnp.int32, (8, LANES), 1)
    middle = []
    for row in (0, 8):
        late = pltpu.roll(tail[row + 16 : row + 24], HALF, 1)
        middle.append(jnp.where(lane < HALF, tail[row : row + 8], late))
    last = jnp.zeros((8, LANES), F32)
    for g in range(4):
        moved = pltpu.roll(tail[8 * g : 8 * g + 8], HALF + 8 * g, 1)
        last = jnp.where((lane >= 8 * g) & (lane < 8 * g + 8), moved, last)
    return jnp.concatenate([value[:, :LANES], *middle, last])


def unpack(packed):
    lane = lax.broadcasted_iota(jnp.int32, (8, LANES), 1)
    tail = []
    for g in range(4):
        row = 32 + 8 * (g % 2)
        middle = packed[row : row + 8]
        if g >= 2:
            middle = pltpu.roll(middle, HALF, 1)
        last = pltpu.roll(packed[48:56], HALF - 8 * g, 1)
        tail.append(jnp.where(lane < HALF, middle, last))
    return jnp.concatenate([packed[:32], jnp.concatenate(tail)], axis=1)[:, :MODES]


def pick(core, even, odd):
    return jnp.where(core == 0, even, odd)


def load_kernel(columns, core_ref, harm_hbm, loads_hbm, phi_hbm, send_ref, mine_ref, phi_send_ref, phi_mine_ref, harm_ref, loads_ref, sems):
    core = core_ref[0]
    pairs = phi_mine_ref.shape[0]
    harm_copy = pltpu.make_async_copy(harm_hbm, harm_ref, sems.at[0])
    harm_copy.start()
    load_copy = pltpu.make_async_copy(loads_hbm, loads_ref, sems.at[1])
    load_copy.start()
    copies = [
        pltpu.make_async_copy(phi_hbm.at[:, 1 - core], phi_send_ref, sems.at[2]),
        pltpu.make_async_copy(phi_hbm.at[:, core], phi_mine_ref, sems.at[3]),
    ]
    for copy in copies:
        copy.start()
    harm_copy.wait()
    wide = loads_ref.shape[1]
    col = lax.broadcasted_iota(jnp.int32, (8, wide), 1)
    key = jnp.full((8, wide), -1, jnp.int32)
    for k in range(NHARM):
        diam = harm_ref[k] - 2 * pairs * core
        place = pick((diam & 1) - core, pairs, 0) + (diam >> 1)
        place = jnp.where((diam >= 0) & (diam < 2 * pairs), place, 2 * pairs)
        inside = (col >= k * columns) & (col < (k + 1) * columns)
        key = jnp.where(inside, (place - k) * columns + col, key)
    shape = (2 * pairs * columns, wide)
    row = lax.broadcasted_iota(jnp.int32, shape, 0)
    spread = jnp.where(row == jnp.broadcast_to(key[0:1], shape), 1.0, 0.0).astype(BF16)
    load_copy.wait()
    combined = lax.dot_general(
        spread, loads_ref[...], (((1,), (1,)), ((), ())), preferred_element_type=F32
    ).astype(BF16)
    send_ref[...] = combined[: pairs * columns].reshape(send_ref.shape)
    mine_ref[...] = combined[pairs * columns :].reshape(mine_ref.shape)
    for copy in copies:
        copy.wait()


def assemble_kernel(core_ref, mine_ref, recv_ref, out_ref):
    core = core_ref[0]
    pairs = recv_ref.shape[0]
    for half, ref in ((core, mine_ref), (1 - core, recv_ref)):
        for k in range(pairs):
            out_ref[half * pairs + (k ^ HUB)] = pack(ref[k].astype(F32)).astype(BF16)


def pack_kernel(columns, row_ref, out_ref):
    row = jnp.broadcast_to(row_ref[...], (columns, MODES))
    out = pack(row)
    out_ref[...] = jnp.where(out == 0.0, 1.0, out)


def regroup_kernel(core_ref, stiff_hbm, keep_ref, send_ref, stiff_ref, sems):
    core = core_ref[0]
    pieces = [(chunk, first, last) for chunk in range(2) for first, last in ((0, 112), (112, MODES))]
    copies = []
    for at, (chunk, first, last) in enumerate(pieces):
        rows = pl.ds(chunk * MODES + first, last - first)
        copies.append(
            pltpu.make_async_copy(stiff_hbm.at[rows], stiff_ref.at[rows], sems.at[at])
        )
        copies[at].start()

    def split(parity, refs, chunk, first, last):
        stiff = stiff_ref[chunk * MODES + first : chunk * MODES + last].astype(BF16)
        for k in range(2 * keep_ref.shape[1]):
            odd = k % 2
            owner = parity if odd == parity else 1 - parity
            at = chunk if owner == 0 else 1 - chunk
            refs[odd][at, k // 2, first:last] = stiff[:, k * MODES : (k + 1) * MODES]

    for at, piece in enumerate(pieces):
        copies[at].wait()

        @pl.when(core == 0)
        def _():
            split(0, (keep_ref, send_ref), *piece)

        @pl.when(core == 1)
        def _():
            split(1, (send_ref, keep_ref), *piece)


def product_kernel(source, core_ref, amp_ref, keep_ref, recv_ref, *rest):
    prev_ref, out_ref = rest if len(rest) == 2 else (None, rest[0])
    core = core_ref[0]
    slots = keep_ref.shape[1]
    amp = unpack(amp_ref[...].astype(F32)).astype(BF16)
    for half, ref in ((core, keep_ref), (1 - core, recv_ref)):
        for k in range(slots):
            at = half * slots + (k ^ HUB)
            value = pack(jnp.dot(amp, ref[source, k], preferred_element_type=F32))
            if prev_ref is not None:
                value = value + prev_ref[at]
            out_ref[at] = value.astype(out_ref.dtype)


def parity_weights(odd, core, table_ref, amp_ref, weights_ref):
    local_diam = amp_ref.shape[0]
    columns = weights_ref.shape[1] // local_diam
    pairs = local_diam // 2
    for at_half, half in enumerate((core, 1 - core)):
        for k in range(pairs):
            at = half * pairs + k
            amp = unpack(amp_ref[half * pairs + (k ^ HUB)].astype(F32))
            for s in range(local_diam):
                value = table_ref[2 * at + odd, s : s + 1] * amp
                weights_ref[at_half * pairs + k, s * columns : (s + 1) * columns] = value.astype(BF16)


def parity_product(odd, weights_ref, own_ref, recv_ref, total, lanes):
    pairs = own_ref.shape[0] // 2
    for at_half, phi_ref in enumerate((own_ref, recv_ref)):
        for k in range(pairs):
            total = total + jnp.dot(
                weights_ref[at_half * pairs + k],
                phi_ref[2 * k + odd, :, lanes],
                preferred_element_type=F32,
            )
    return total


def same_kernel(core_ref, table_ref, amp_ref, own_ref, recv_ref, out_ref, weights_ref):
    core = core_ref[0]
    parity_weights(core, core, table_ref, amp_ref, weights_ref)
    out_ref[...] = parity_product(core, weights_ref, own_ref, recv_ref, 0.0, slice(None))


def crossed_kernel(core_ref, table_ref, amp_ref, own_ref, recv_ref, prev_ref, out_hbm, weights_ref, out_ref, sems):
    core = core_ref[0]
    parity_weights(1 - core, core, table_ref, amp_ref, weights_ref)
    tiles = sems.shape[0]
    wide = out_ref.shape[2] // tiles
    copies = []
    for tile in range(tiles):
        lanes = slice(tile * wide, (tile + 1) * wide)
        total = prev_ref[:, lanes]
        total = parity_product(1 - core, weights_ref, own_ref, recv_ref, total, lanes)
        out_ref[:, :, lanes] = total.astype(BF16).reshape(out_ref.shape[:2] + (wide,))
        copies.append(
            pltpu.make_async_copy(out_ref.at[:, :, lanes], out_hbm.at[:, :, lanes], sems.at[tile])
        )
        copies[tile].start()
    for copy in copies:
        copy.wait()


def chunk_plan(phi, loads, harm_diam, mistuning, dyn_diag, blade_order):
    rows_dev, half_modes = phi.shape
    local_diam = half_modes // MODES
    columns = loads.shape[1] // NHARM
    core = lax.axis_index("diam")
    own_diam = 2 * lax.axis_index("rows") + core
    first_diam = core * local_diam
    core_arg = core.reshape(1).astype(jnp.int32)
    pairs = local_diam // 2

    def other_core(value):
        return lax.ppermute(value, "diam", SWAP)

    def exchange(slots):
        order = [row ^ HUB for row in range(slots.shape[0])]
        return lax.all_to_all(slots, "rows", 0, 0, tiled=True, axis_index_groups=[order])

    def row_total(got):
        return jnp.sum(got.astype(F32), axis=0)

    shapes = phi.T.reshape(local_diam, MODES, rows_dev)
    half_combined = jax.ShapeDtypeStruct((pairs, columns, rows_dev), BF16)
    half_shapes = jax.ShapeDtypeStruct((pairs, MODES, rows_dev), BF16)
    combined_send, combined_mine, shapes_send, shapes_mine = pl.pallas_call(
        functools.partial(load_kernel, columns),
        name="load",
        in_specs=[SMEM, HBM, HBM, HBM],
        out_specs=[VMEM] * 4,
        out_shape=[half_combined, half_combined, half_shapes, half_shapes],
        scratch_shapes=[
            pltpu.SMEM(harm_diam.shape, jnp.int32),
            pltpu.VMEM(loads.shape, BF16),
            pltpu.SemaphoreType.DMA((4,)),
        ],
        compiler_params=LIMIT,
    )(core_arg, *in_hbm(harm_diam, loads, shapes.reshape(pairs, 2, MODES, rows_dev)))

    def force_part(combined, near):
        return jnp.einsum("hcr,hmr->hcm", combined, near, preferred_element_type=F32).astype(BF16)

    force_recv = other_core(force_part(combined_send, shapes_send))
    slots_shape = (local_diam,) + PACKED
    force_slots = pl.pallas_call(
        assemble_kernel,
        name="assemble",
        in_specs=[SMEM, VMEM, VMEM],
        out_specs=VMEM,
        out_shape=jax.ShapeDtypeStruct(slots_shape, BF16),
        compiler_params=LIMIT,
    )(core_arg, force_part(combined_mine, shapes_mine), force_recv)
    force_slots, stiff, order, dyn_diag = lax.optimization_barrier(
        (force_slots, mistuning.T, blade_order, dyn_diag)
    )
    force_got = exchange(force_slots)

    group = jax.ShapeDtypeStruct((2, pairs, MODES, MODES), BF16)
    keep, sent = pl.pallas_call(
        regroup_kernel,
        name="regroup",
        in_specs=[SMEM, HBM],
        out_specs=[VMEM, VMEM],
        out_shape=[group, group],
        scratch_shapes=[
            pltpu.VMEM(stiff.shape, F32),
            pltpu.SemaphoreType.DMA((4,)),
        ],
        compiler_params=WIDE,
        cost_estimate=pl.CostEstimate(
            flops=2 * mistuning.size, bytes_accessed=8 * mistuning.size, transcendentals=0
        ),
    )(core_arg, *in_hbm(stiff))
    recv = other_core(sent)
    table = lax.dynamic_slice_in_dim(cyclic_rows(order), first_diam, local_diam, 0)
    table = jnp.broadcast_to(table.T[:, :, None], (NBLADE, local_diam, MODES))
    dyn_own = pl.pallas_call(
        functools.partial(pack_kernel, columns),
        name="pack",
        in_specs=[VMEM],
        out_specs=VMEM,
        out_shape=jax.ShapeDtypeStruct(PACKED, F32),
        compiler_params=LIMIT,
        cost_estimate=pl.CostEstimate(flops=1, bytes_accessed=1, transcendentals=0),
    )(lax.dynamic_slice_in_dim(dyn_diag, own_diam * MODES, MODES, 0)[None, :])
    force_got, keep, table, dyn_own = lax.optimization_barrier((force_got, keep, table, dyn_own))

    def product(source, *operands):
        return pl.pallas_call(
            functools.partial(product_kernel, source),
            name="product",
            in_specs=[SMEM] + [VMEM] * len(operands),
            out_specs=VMEM,
            out_shape=jax.ShapeDtypeStruct(slots_shape, BF16 if source else F32),
            compiler_params=LIMIT,
        )(core_arg, *operands)

    force = row_total(force_got)
    amp = force / dyn_own
    for sweep in range(ITERS):
        amp_low = amp.astype(BF16)
        amp_other = other_core(amp_low)
        part = product(0, amp_low, keep, recv)
        part, amp_other = lax.optimization_barrier((part, amp_other))
        if sweep == ITERS - 1:
            part, shapes_sent = lax.optimization_barrier((part, shapes))
            shapes_received = other_core(shapes_sent)
        part = product(1, amp_other, keep, recv, part)
        amp = (force - row_total(exchange(part))) / dyn_own
    same = exchange(jnp.broadcast_to(amp.astype(BF16)[None], slots_shape))
    crossed = other_core(same)

    half_cost = pl.CostEstimate(
        flops=2 * local_diam * columns * phi.size, bytes_accessed=2 * phi.size, transcendentals=0
    )
    weights = pltpu.VMEM((local_diam, local_diam * columns, MODES), BF16)
    part = pl.pallas_call(
        same_kernel,
        name="blades_same",
        in_specs=[SMEM] + [VMEM] * 4,
        out_specs=VMEM,
        out_shape=jax.ShapeDtypeStruct((local_diam * columns, rows_dev), F32),
        scratch_shapes=[weights],
        compiler_params=WIDE,
        cost_estimate=half_cost,
    )(core_arg, table, same, shapes_sent, shapes_received)
    part, crossed = lax.optimization_barrier((part, crossed))
    out_shape = (local_diam, columns, rows_dev)
    return pl.pallas_call(
        crossed_kernel,
        name="blades_crossed",
        in_specs=[SMEM] + [VMEM] * 5,
        out_specs=HBM,
        out_shape=jax.ShapeDtypeStruct(out_shape, BF16),
        scratch_shapes=[weights, pltpu.VMEM(out_shape, BF16), pltpu.SemaphoreType.DMA((4,))],
        compiler_params=WIDE,
        cost_estimate=half_cost,
    )(core_arg, table, crossed, shapes_sent, shapes_received, part)


def solution(mesh):
    placed = (P("rows", "diam"), P("rows", None), P(), P("diam", "rows"), P("grp"), P())
    one_each = mesh.shape["rows"] * 2 == NBLADE and mesh.shape["diam"] == 2
    return jax.shard_map(
        chunk_plan if one_each else general_plan,
        mesh=mesh,
        in_specs=placed,
        out_specs=P("diam", "grp", "rows"),
        check_vma=False,
    )
```

```python
import functools
import math

import jax
import jax.numpy as jnp
from jax import lax
from jax.experimental import pallas as pl
from jax.experimental.pallas import tpu as pltpu
from jax.sharding import PartitionSpec as P

NBLADE = 16
MODES = 200
NHARM = 16
ITERS = 4
SWAP = [(0, 1), (1, 0)]
LANES = 128
HALF = 64
ORDER = [5, 4, 3, 2, 1, 0, 7, 6]
PACKED = (56, LANES)
F32 = jnp.float32
BF16 = jnp.bfloat16


def cyclic_rows(blade_order):
    count = NBLADE
    blade_pos = jnp.arange(count).astype(jnp.float32)[:, None]
    harmonic = jnp.arange(count)[None, :]
    half_count = count // 2
    wave = jnp.where(harmonic > half_count, harmonic - half_count, harmonic).astype(jnp.float32)
    angle = 2.0 * math.pi * wave * blade_pos / count
    scale = jnp.where(
        (harmonic == 0) | (harmonic == half_count), 1.0 / math.sqrt(count), math.sqrt(2.0 / count)
    )
    cyclic_tab = jnp.where(harmonic > half_count, jnp.sin(angle), jnp.cos(angle)) * scale
    onehot = (blade_order[:, None] == jnp.arange(count)[None, :]).astype(jnp.float32)
    return jnp.dot(onehot, cyclic_tab, precision=lax.Precision.HIGHEST)


def general_plan(phi, loads, harm_diam, mistuning, dyn_diag, blade_order):
    rows_dev = phi.shape[0]
    half_modes = phi.shape[1]
    local_diam = half_modes // MODES
    columns = loads.shape[1] // NHARM
    col_width = mistuning.shape[1]
    diam_index = lax.axis_index("diam")
    row_index = lax.axis_index("rows")
    first_diam = diam_index * local_diam
    diam_ids = first_diam + jnp.arange(local_diam, dtype=jnp.int32)
    select = (harm_diam[:, None] == diam_ids[None, :]).astype(jnp.bfloat16)
    combined = jnp.einsum(
        "rkc,kh->rhc",
        loads.reshape(rows_dev, NHARM, columns),
        select,
        preferred_element_type=jnp.float32,
    ).astype(jnp.bfloat16)
    shapes = phi.reshape(rows_dev, local_diam, MODES)
    force_part = jnp.einsum(
        "rhm,rhc->hmc", shapes, combined, preferred_element_type=jnp.float32
    ).reshape(half_modes, columns)
    half_start = diam_index * half_modes
    dyn_half = lax.dynamic_slice_in_dim(dyn_diag, half_start, half_modes, 0)[:, None]

    def row_total(partial_term):
        return lax.psum(partial_term, "rows")

    force_half = row_total(force_part)
    amp_half = force_half / dyn_half
    for sweep in range(ITERS):
        full_amp = lax.all_gather(amp_half, "diam", axis=0, tiled=True)
        col_part = lax.dynamic_slice_in_dim(full_amp, row_index * col_width, col_width, 0)
        amp_half = (
            force_half
            - row_total(
                jnp.dot(
                    mistuning,
                    col_part,
                    precision=lax.Precision.HIGHEST,
                    preferred_element_type=jnp.float32,
                )
            )
        ) / dyn_half
    amp_low = amp_half.astype(jnp.bfloat16).reshape(local_diam, MODES, columns)
    sector = jnp.einsum("rhm,hmc->hcr", shapes, amp_low, preferred_element_type=jnp.float32).astype(
        jnp.bfloat16
    )
    table = cyclic_rows(blade_order)
    table_cols = lax.dynamic_slice_in_dim(table, first_diam, local_diam, 1)
    partial_value = jnp.einsum(
        "sh,hcr->scr", table_cols, sector.astype(jnp.float32), precision=lax.Precision.HIGHEST
    )
    blades = lax.psum_scatter(
        partial_value.astype(jnp.bfloat16), "diam", scatter_dimension=0, tiled=True
    )
    return blades


VMEM = pl.BlockSpec(memory_space=pltpu.VMEM)
SMEM = pl.BlockSpec(memory_space=pltpu.SMEM)
HBM = pl.BlockSpec(memory_space=pltpu.HBM)
WIDE = pltpu.CompilerParams(vmem_limit_bytes=16 << 20)
LIMIT = pltpu.CompilerParams(vmem_limit_bytes=8 << 20)


def in_hbm(*values):
    return [pltpu.with_memory_space_constraint(value, pltpu.HBM) for value in values]


def pack(value):
    spare = jnp.zeros((value.shape[0], 2 * LANES - MODES), F32)
    tail = jnp.concatenate([value[:, LANES:], spare], axis=1)
    lane = lax.broadcasted_iota(jnp.int32, (8, LANES), 1)
    middle = []
    for row in (0, 8):
        late = pltpu.roll(tail[row + 16 : row + 24], HALF, 1)
        middle.append(jnp.where(lane < HALF, tail[row : row + 8], late))
    last = jnp.zeros((8, LANES), F32)
    for g in range(4):
        moved = pltpu.roll(tail[8 * g : 8 * g + 8], HALF + 8 * g, 1)
        last = jnp.where((lane >= 8 * g) & (lane < 8 * g + 8), moved, last)
    return jnp.concatenate([value[:, :LANES], *middle, last])


def unpack(packed):
    lane = lax.broadcasted_iota(jnp.int32, (8, LANES), 1)
    tail = []
    for g in range(4):
        row = 32 + 8 * (g % 2)
        middle = packed[row : row + 8]
        if g >= 2:
            middle = pltpu.roll(middle, HALF, 1)
        last = pltpu.roll(packed[48:56], HALF - 8 * g, 1)
        tail.append(jnp.where(lane < HALF, middle, last))
    return jnp.concatenate([packed[:32], jnp.concatenate(tail)], axis=1)[:, :MODES]


def slot_of(half, pairs, k):
    return jnp.where(half == 0, ORDER.index(k), ORDER.index(pairs + k))


def pick(core, even, odd):
    return jnp.where(core == 0, even, odd)


def load_kernel(columns, core_ref, harm_hbm, loads_hbm, phi_hbm, send_ref, mine_ref, phi_send_ref, phi_mine_ref, harm_ref, loads_ref, sems):
    core = core_ref[0]
    pairs = phi_mine_ref.shape[0]
    harm_copy = pltpu.make_async_copy(harm_hbm, harm_ref, sems.at[0])
    harm_copy.start()
    load_copy = pltpu.make_async_copy(loads_hbm, loads_ref, sems.at[1])
    load_copy.start()
    copies = [
        pltpu.make_async_copy(phi_hbm.at[:, 1 - core], phi_send_ref, sems.at[2]),
        pltpu.make_async_copy(phi_hbm.at[:, core], phi_mine_ref, sems.at[3]),
    ]
    for copy in copies:
        copy.start()
    harm_copy.wait()
    wide = loads_ref.shape[1]
    col = lax.broadcasted_iota(jnp.int32, (8, wide), 1)
    key = jnp.full((8, wide), -1, jnp.int32)
    for k in range(NHARM):
        diam = harm_ref[k] - 2 * pairs * core
        place = pick((diam & 1) - core, pairs, 0) + (diam >> 1)
        place = jnp.where((diam >= 0) & (diam < 2 * pairs), place, 2 * pairs)
        inside = (col >= k * columns) & (col < (k + 1) * columns)
        key = jnp.where(inside, (place - k) * columns + col, key)
    shape = (2 * pairs * columns, wide)
    row = lax.broadcasted_iota(jnp.int32, shape, 0)
    spread = jnp.where(row == jnp.broadcast_to(key[0:1], shape), 1.0, 0.0).astype(BF16)
    load_copy.wait()
    combined = lax.dot_general(
        spread, loads_ref[...], (((1,), (1,)), ((), ())), preferred_element_type=F32
    ).astype(BF16)
    send_ref[...] = combined[: pairs * columns].reshape(send_ref.shape)
    mine_ref[...] = combined[pairs * columns :].reshape(mine_ref.shape)
    for copy in copies:
        copy.wait()


def assemble_kernel(core_ref, mine_ref, recv_ref, out_ref):
    core = core_ref[0]
    pairs = recv_ref.shape[0]
    for half, ref in ((core, mine_ref), (1 - core, recv_ref)):
        for k in range(pairs):
            out_ref[slot_of(half, pairs, k)] = pack(ref[k].astype(F32)).astype(BF16)


def pack_kernel(columns, row_ref, out_ref):
    row = jnp.broadcast_to(row_ref[...], (columns, MODES))
    out = pack(row)
    out_ref[...] = jnp.where(out == 0.0, 1.0, out)


def regroup_kernel(core_ref, stiff_hbm, keep_ref, send_ref, stiff_ref, sems):
    core = core_ref[0]
    pieces = [(chunk, first, last) for chunk in range(2) for first, last in ((0, 112), (112, MODES))]
    copies = []
    for at, (chunk, first, last) in enumerate(pieces):
        rows = pl.ds(chunk * MODES + first, last - first)
        copies.append(
            pltpu.make_async_copy(stiff_hbm.at[rows], stiff_ref.at[rows], sems.at[at])
        )
        copies[at].start()

    def split(parity, refs, chunk, first, last):
        stiff = stiff_ref[chunk * MODES + first : chunk * MODES + last].astype(BF16)
        for k in range(2 * keep_ref.shape[1]):
            odd = k % 2
            owner = parity if odd == parity else 1 - parity
            at = chunk if owner == 0 else 1 - chunk
            refs[odd][at, k // 2, first:last] = stiff[:, k * MODES : (k + 1) * MODES]

    for at, piece in enumerate(pieces):
        copies[at].wait()

        @pl.when(core == 0)
        def _():
            split(0, (keep_ref, send_ref), *piece)

        @pl.when(core == 1)
        def _():
            split(1, (send_ref, keep_ref), *piece)


def product_kernel(source, core_ref, amp_ref, keep_ref, recv_ref, *rest):
    prev_ref, out_ref = rest if len(rest) == 2 else (None, rest[0])
    core = core_ref[0]
    slots = keep_ref.shape[1]
    amp = unpack(amp_ref[...].astype(F32)).astype(BF16)
    for half, ref in ((core, keep_ref), (1 - core, recv_ref)):
        for k in range(slots):
            at = slot_of(half, slots, k)
            value = pack(jnp.dot(amp, ref[source, k], preferred_element_type=F32))
            if prev_ref is not None:
                value = value + prev_ref[at]
            out_ref[at] = value.astype(out_ref.dtype)


def parity_weights(odd, core, table_ref, amp_ref, weights_ref):
    local_diam = amp_ref.shape[0]
    columns = weights_ref.shape[1] // local_diam
    pairs = local_diam // 2
    for at_half, half in enumerate((core, 1 - core)):
        for k in range(pairs):
            at = half * pairs + k
            amp = unpack(amp_ref[slot_of(half, pairs, k)].astype(F32))
            for s in range(local_diam):
                value = table_ref[2 * at + odd, s : s + 1] * amp
                weights_ref[at_half * pairs + k, s * columns : (s + 1) * columns] = value.astype(BF16)


def parity_product(odd, weights_ref, own_ref, recv_ref, total, lanes):
    pairs = own_ref.shape[0] // 2
    for at_half, phi_ref in enumerate((own_ref, recv_ref)):
        for k in range(pairs):
            total = total + jnp.dot(
                weights_ref[at_half * pairs + k],
                phi_ref[2 * k + odd, :, lanes],
                preferred_element_type=F32,
            )
    return total


def same_kernel(core_ref, table_ref, amp_ref, own_ref, recv_ref, out_ref, weights_ref):
    core = core_ref[0]
    parity_weights(core, core, table_ref, amp_ref, weights_ref)
    out_ref[...] = parity_product(core, weights_ref, own_ref, recv_ref, 0.0, slice(None))


def crossed_kernel(core_ref, table_ref, amp_ref, own_ref, recv_ref, prev_ref, out_hbm, weights_ref, out_ref, sems):
    core = core_ref[0]
    parity_weights(1 - core, core, table_ref, amp_ref, weights_ref)
    tiles = sems.shape[0]
    wide = out_ref.shape[2] // tiles
    copies = []
    for tile in range(tiles):
        lanes = slice(tile * wide, (tile + 1) * wide)
        total = prev_ref[:, lanes]
        total = parity_product(1 - core, weights_ref, own_ref, recv_ref, total, lanes)
        out_ref[:, :, lanes] = total.astype(BF16).reshape(out_ref.shape[:2] + (wide,))
        copies.append(
            pltpu.make_async_copy(out_ref.at[:, :, lanes], out_hbm.at[:, :, lanes], sems.at[tile])
        )
        copies[tile].start()
    for copy in copies:
        copy.wait()


def chunk_plan(phi, loads, harm_diam, mistuning, dyn_diag, blade_order):
    rows_dev, half_modes = phi.shape
    local_diam = half_modes // MODES
    columns = loads.shape[1] // NHARM
    core = lax.axis_index("diam")
    own_diam = 2 * lax.axis_index("rows") + core
    first_diam = core * local_diam
    core_arg = core.reshape(1).astype(jnp.int32)
    pairs = local_diam // 2

    def other_core(value):
        return lax.ppermute(value, "diam", SWAP)

    def exchange(slots):
        return lax.all_to_all(slots, "rows", 0, 0, tiled=True, axis_index_groups=[ORDER])

    def row_total(got):
        return jnp.sum(got.astype(F32), axis=0)

    shapes = phi.T.reshape(local_diam, MODES, rows_dev)
    half_combined = jax.ShapeDtypeStruct((pairs, columns, rows_dev), BF16)
    half_shapes = jax.ShapeDtypeStruct((pairs, MODES, rows_dev), BF16)
    combined_send, combined_mine, shapes_send, shapes_mine = pl.pallas_call(
        functools.partial(load_kernel, columns),
        name="load",
        in_specs=[SMEM, HBM, HBM, HBM],
        out_specs=[VMEM] * 4,
        out_shape=[half_combined, half_combined, half_shapes, half_shapes],
        scratch_shapes=[
            pltpu.SMEM(harm_diam.shape, jnp.int32),
            pltpu.VMEM(loads.shape, BF16),
            pltpu.SemaphoreType.DMA((4,)),
        ],
        compiler_params=LIMIT,
    )(core_arg, *in_hbm(harm_diam, loads, shapes.reshape(pairs, 2, MODES, rows_dev)))

    def force_part(combined, near):
        return jnp.einsum("hcr,hmr->hcm", combined, near, preferred_element_type=F32).astype(BF16)

    force_recv = other_core(force_part(combined_send, shapes_send))
    slots_shape = (local_diam,) + PACKED
    force_slots = pl.pallas_call(
        assemble_kernel,
        name="assemble",
        in_specs=[SMEM, VMEM, VMEM],
        out_specs=VMEM,
        out_shape=jax.ShapeDtypeStruct(slots_shape, BF16),
        compiler_params=LIMIT,
    )(core_arg, force_part(combined_mine, shapes_mine), force_recv)
    force_slots, stiff, order, dyn_diag = lax.optimization_barrier(
        (force_slots, mistuning.T, blade_order, dyn_diag)
    )
    force_got = exchange(force_slots)

    group = jax.ShapeDtypeStruct((2, pairs, MODES, MODES), BF16)
    keep, sent = pl.pallas_call(
        regroup_kernel,
        name="regroup",
        in_specs=[SMEM, HBM],
        out_specs=[VMEM, VMEM],
        out_shape=[group, group],
        scratch_shapes=[
            pltpu.VMEM(stiff.shape, F32),
            pltpu.SemaphoreType.DMA((4,)),
        ],
        compiler_params=WIDE,
        cost_estimate=pl.CostEstimate(
            flops=2 * mistuning.size, bytes_accessed=8 * mistuning.size, transcendentals=0
        ),
    )(core_arg, *in_hbm(stiff))
    recv = other_core(sent)
    table = lax.dynamic_slice_in_dim(cyclic_rows(order), first_diam, local_diam, 0)
    table = jnp.broadcast_to(table.T[:, :, None], (NBLADE, local_diam, MODES))
    dyn_own = pl.pallas_call(
        functools.partial(pack_kernel, columns),
        name="pack",
        in_specs=[VMEM],
        out_specs=VMEM,
        out_shape=jax.ShapeDtypeStruct(PACKED, F32),
        compiler_params=LIMIT,
        cost_estimate=pl.CostEstimate(flops=1, bytes_accessed=1, transcendentals=0),
    )(lax.dynamic_slice_in_dim(dyn_diag, own_diam * MODES, MODES, 0)[None, :])
    force_got, keep, table, dyn_own = lax.optimization_barrier((force_got, keep, table, dyn_own))

    def product(source, *operands):
        return pl.pallas_call(
            functools.partial(product_kernel, source),
            name="product",
            in_specs=[SMEM] + [VMEM] * len(operands),
            out_specs=VMEM,
            out_shape=jax.ShapeDtypeStruct(slots_shape, BF16 if source else F32),
            compiler_params=LIMIT,
        )(core_arg, *operands)

    force = row_total(force_got)
    amp = force / dyn_own
    for sweep in range(ITERS):
        amp_low = amp.astype(BF16)
        amp_other = other_core(amp_low)
        part = product(0, amp_low, keep, recv)
        part, amp_other = lax.optimization_barrier((part, amp_other))
        if sweep == ITERS - 1:
            part, shapes_sent = lax.optimization_barrier((part, shapes))
            shapes_received = other_core(shapes_sent)
        part = product(1, amp_other, keep, recv, part)
        amp = (force - row_total(exchange(part))) / dyn_own
    same = exchange(jnp.broadcast_to(amp.astype(BF16)[None], slots_shape))
    crossed = other_core(same)

    half_cost = pl.CostEstimate(
        flops=2 * local_diam * columns * phi.size, bytes_accessed=2 * phi.size, transcendentals=0
    )
    weights = pltpu.VMEM((local_diam, local_diam * columns, MODES), BF16)
    part = pl.pallas_call(
        same_kernel,
        name="blades_same",
        in_specs=[SMEM] + [VMEM] * 4,
        out_specs=VMEM,
        out_shape=jax.ShapeDtypeStruct((local_diam * columns, rows_dev), F32),
        scratch_shapes=[weights],
        compiler_params=WIDE,
        cost_estimate=half_cost,
    )(core_arg, table, same, shapes_sent, shapes_received)
    part, crossed = lax.optimization_barrier((part, crossed))
    out_shape = (local_diam, columns, rows_dev)
    return pl.pallas_call(
        crossed_kernel,
        name="blades_crossed",
        in_specs=[SMEM] + [VMEM] * 5,
        out_specs=HBM,
        out_shape=jax.ShapeDtypeStruct(out_shape, BF16),
        scratch_shapes=[weights, pltpu.VMEM(out_shape, BF16), pltpu.SemaphoreType.DMA((4,))],
        compiler_params=WIDE,
        cost_estimate=half_cost,
    )(core_arg, table, crossed, shapes_sent, shapes_received, part)


def solution(mesh):
    placed = (P("rows", "diam"), P("rows", None), P(), P("diam", "rows"), P("grp"), P())
    one_each = mesh.shape["rows"] * 2 == NBLADE and mesh.shape["diam"] == 2
    return jax.shard_map(
        chunk_plan if one_each else general_plan,
        mesh=mesh,
        in_specs=placed,
        out_specs=P("diam", "grp", "rows"),
        check_vma=False,
    )
```

```python
import functools
import math

import jax
import jax.numpy as jnp
from jax import lax
from jax.experimental import pallas as pl
from jax.experimental.pallas import tpu as pltpu
from jax.sharding import PartitionSpec as P

NBLADE = 16
MODES = 200
NHARM = 16
ITERS = 4
SWAP = [(0, 1), (1, 0)]
LANES = 128
HALF = 64
ORDER = [5, 4, 3, 2, 1, 0, 7, 6]
PACKED = (56, LANES)
F32 = jnp.float32
BF16 = jnp.bfloat16


def cyclic_rows(blade_order):
    count = NBLADE
    blade_pos = jnp.arange(count).astype(jnp.float32)[:, None]
    harmonic = jnp.arange(count)[None, :]
    half_count = count // 2
    wave = jnp.where(harmonic > half_count, harmonic - half_count, harmonic).astype(jnp.float32)
    angle = 2.0 * math.pi * wave * blade_pos / count
    scale = jnp.where(
        (harmonic == 0) | (harmonic == half_count), 1.0 / math.sqrt(count), math.sqrt(2.0 / count)
    )
    cyclic_tab = jnp.where(harmonic > half_count, jnp.sin(angle), jnp.cos(angle)) * scale
    onehot = (blade_order[:, None] == jnp.arange(count)[None, :]).astype(jnp.float32)
    return jnp.dot(onehot, cyclic_tab, precision=lax.Precision.HIGHEST)


def general_plan(phi, loads, harm_diam, mistuning, dyn_diag, blade_order):
    rows_dev = phi.shape[0]
    half_modes = phi.shape[1]
    local_diam = half_modes // MODES
    columns = loads.shape[1] // NHARM
    col_width = mistuning.shape[1]
    diam_index = lax.axis_index("diam")
    row_index = lax.axis_index("rows")
    first_diam = diam_index * local_diam
    diam_ids = first_diam + jnp.arange(local_diam, dtype=jnp.int32)
    select = (harm_diam[:, None] == diam_ids[None, :]).astype(jnp.bfloat16)
    combined = jnp.einsum(
        "rkc,kh->rhc",
        loads.reshape(rows_dev, NHARM, columns),
        select,
        preferred_element_type=jnp.float32,
    ).astype(jnp.bfloat16)
    shapes = phi.reshape(rows_dev, local_diam, MODES)
    force_part = jnp.einsum(
        "rhm,rhc->hmc", shapes, combined, preferred_element_type=jnp.float32
    ).reshape(half_modes, columns)
    half_start = diam_index * half_modes
    dyn_half = lax.dynamic_slice_in_dim(dyn_diag, half_start, half_modes, 0)[:, None]

    def row_total(partial_term):
        return lax.psum(partial_term, "rows")

    force_half = row_total(force_part)
    amp_half = force_half / dyn_half
    for sweep in range(ITERS):
        full_amp = lax.all_gather(amp_half, "diam", axis=0, tiled=True)
        col_part = lax.dynamic_slice_in_dim(full_amp, row_index * col_width, col_width, 0)
        amp_half = (
            force_half
            - row_total(
                jnp.dot(
                    mistuning,
                    col_part,
                    precision=lax.Precision.HIGHEST,
                    preferred_element_type=jnp.float32,
                )
            )
        ) / dyn_half
    amp_low = amp_half.astype(jnp.bfloat16).reshape(local_diam, MODES, columns)
    sector = jnp.einsum("rhm,hmc->hcr", shapes, amp_low, preferred_element_type=jnp.float32).astype(
        jnp.bfloat16
    )
    table = cyclic_rows(blade_order)
    table_cols = lax.dynamic_slice_in_dim(table, first_diam, local_diam, 1)
    partial_value = jnp.einsum(
        "sh,hcr->scr", table_cols, sector.astype(jnp.float32), precision=lax.Precision.HIGHEST
    )
    blades = lax.psum_scatter(
        partial_value.astype(jnp.bfloat16), "diam", scatter_dimension=0, tiled=True
    )
    return blades


VMEM = pl.BlockSpec(memory_space=pltpu.VMEM)
SMEM = pl.BlockSpec(memory_space=pltpu.SMEM)
HBM = pl.BlockSpec(memory_space=pltpu.HBM)
WIDE = pltpu.CompilerParams(vmem_limit_bytes=16 << 20)
LIMIT = pltpu.CompilerParams(vmem_limit_bytes=8 << 20)


def in_hbm(*values):
    return [pltpu.with_memory_space_constraint(value, pltpu.HBM) for value in values]


def pack(value):
    spare = jnp.zeros((value.shape[0], 2 * LANES - MODES), F32)
    tail = jnp.concatenate([value[:, LANES:], spare], axis=1)
    lane = lax.broadcasted_iota(jnp.int32, (8, LANES), 1)
    middle = []
    for row in (0, 8):
        late = pltpu.roll(tail[row + 16 : row + 24], HALF, 1)
        middle.append(jnp.where(lane < HALF, tail[row : row + 8], late))
    last = jnp.zeros((8, LANES), F32)
    for g in range(4):
        moved = pltpu.roll(tail[8 * g : 8 * g + 8], HALF + 8 * g, 1)
        last = jnp.where((lane >= 8 * g) & (lane < 8 * g + 8), moved, last)
    return jnp.concatenate([value[:, :LANES], *middle, last])


def unpack(packed):
    lane = lax.broadcasted_iota(jnp.int32, (8, LANES), 1)
    tail = []
    for g in range(4):
        row = 32 + 8 * (g % 2)
        middle = packed[row : row + 8]
        if g >= 2:
            middle = pltpu.roll(middle, HALF, 1)
        last = pltpu.roll(packed[48:56], HALF - 8 * g, 1)
        tail.append(jnp.where(lane < HALF, middle, last))
    return jnp.concatenate([packed[:32], jnp.concatenate(tail)], axis=1)[:, :MODES]


def slot_of(half, pairs, k):
    return jnp.where(half == 0, ORDER.index(k), ORDER.index(pairs + k))


def pick(core, even, odd):
    return jnp.where(core == 0, even, odd)


def load_kernel(columns, core_ref, harm_hbm, loads_hbm, phi_hbm, send_ref, mine_ref, phi_send_ref, phi_mine_ref, harm_ref, loads_ref, sems):
    core = core_ref[0]
    pairs = phi_mine_ref.shape[0]
    harm_copy = pltpu.make_async_copy(harm_hbm, harm_ref, sems.at[0])
    harm_copy.start()
    load_copy = pltpu.make_async_copy(loads_hbm, loads_ref, sems.at[1])
    load_copy.start()
    copies = [
        pltpu.make_async_copy(phi_hbm.at[:, 1 - core], phi_send_ref, sems.at[2]),
        pltpu.make_async_copy(phi_hbm.at[:, core], phi_mine_ref, sems.at[3]),
    ]
    for copy in copies:
        copy.start()
    harm_copy.wait()
    wide = loads_ref.shape[1]
    col = lax.broadcasted_iota(jnp.int32, (8, wide), 1)
    key = jnp.full((8, wide), -1, jnp.int32)
    for k in range(NHARM):
        diam = harm_ref[k] - 2 * pairs * core
        place = pick((diam & 1) - core, pairs, 0) + (diam >> 1)
        place = jnp.where((diam >= 0) & (diam < 2 * pairs), place, 2 * pairs)
        inside = (col >= k * columns) & (col < (k + 1) * columns)
        key = jnp.where(inside, (place - k) * columns + col, key)
    shape = (2 * pairs * columns, wide)
    row = lax.broadcasted_iota(jnp.int32, shape, 0)
    spread = jnp.where(row == jnp.broadcast_to(key[0:1], shape), 1.0, 0.0).astype(BF16)
    load_copy.wait()
    combined = lax.dot_general(
        spread, loads_ref[...], (((1,), (1,)), ((), ())), preferred_element_type=F32
    ).astype(BF16)
    send_ref[...] = combined[: pairs * columns].reshape(send_ref.shape)
    mine_ref[...] = combined[pairs * columns :].reshape(mine_ref.shape)
    for copy in copies:
        copy.wait()


def assemble_kernel(core_ref, mine_ref, recv_ref, out_ref):
    core = core_ref[0]
    pairs = recv_ref.shape[0]
    for half, ref in ((core, mine_ref), (1 - core, recv_ref)):
        for k in range(pairs):
            out_ref[slot_of(half, pairs, k)] = pack(ref[k].astype(F32)).astype(BF16)


def pack_kernel(columns, row_ref, out_ref):
    row = jnp.broadcast_to(row_ref[...], (columns, MODES))
    out = pack(row)
    out_ref[...] = jnp.where(out == 0.0, 1.0, out)


def regroup_kernel(core_ref, stiff_hbm, keep_ref, send_ref, stiff_ref, sems):
    core = core_ref[0]
    pieces = [(chunk, first, last) for chunk in range(2) for first, last in ((0, 112), (112, MODES))]
    copies = []
    for at, (chunk, first, last) in enumerate(pieces):
        rows = pl.ds(chunk * MODES + first, last - first)
        copies.append(
            pltpu.make_async_copy(stiff_hbm.at[rows], stiff_ref.at[rows], sems.at[at])
        )
        copies[at].start()

    def split(parity, refs, chunk, first, last):
        stiff = stiff_ref[chunk * MODES + first : chunk * MODES + last].astype(BF16)
        for k in range(2 * keep_ref.shape[1]):
            odd = k % 2
            owner = parity if odd == parity else 1 - parity
            at = chunk if owner == 0 else 1 - chunk
            refs[odd][at, k // 2, first:last] = stiff[:, k * MODES : (k + 1) * MODES]

    for at, piece in enumerate(pieces):
        copies[at].wait()

        @pl.when(core == 0)
        def _():
            split(0, (keep_ref, send_ref), *piece)

        @pl.when(core == 1)
        def _():
            split(1, (send_ref, keep_ref), *piece)


def product_kernel(source, core_ref, amp_ref, keep_ref, recv_ref, *rest):
    prev_ref, out_ref = rest if len(rest) == 2 else (None, rest[0])
    core = core_ref[0]
    slots = keep_ref.shape[1]
    amp = unpack(amp_ref[...].astype(F32)).astype(BF16)
    for half, ref in ((core, keep_ref), (1 - core, recv_ref)):
        for k in range(slots):
            at = slot_of(half, slots, k)
            value = pack(jnp.dot(amp, ref[source, k], preferred_element_type=F32))
            if prev_ref is not None:
                value = value + prev_ref[at]
            out_ref[at] = value.astype(out_ref.dtype)


def parity_weights(odd, core, table_ref, amp_ref, weights_ref):
    local_diam = amp_ref.shape[0]
    columns = weights_ref.shape[1] // local_diam
    pairs = local_diam // 2
    for at_half, half in enumerate((core, 1 - core)):
        for k in range(pairs):
            at = half * pairs + k
            amp = unpack(amp_ref[slot_of(half, pairs, k)].astype(F32))
            for s in range(local_diam):
                value = table_ref[2 * at + odd, s : s + 1] * amp
                weights_ref[at_half * pairs + k, s * columns : (s + 1) * columns] = value.astype(BF16)


def parity_product(odd, weights_ref, own_ref, recv_ref, total, lanes):
    pairs = own_ref.shape[0] // 2
    for at_half, phi_ref in enumerate((own_ref, recv_ref)):
        for k in range(pairs):
            total = total + jnp.dot(
                weights_ref[at_half * pairs + k],
                phi_ref[2 * k + odd, :, lanes],
                preferred_element_type=F32,
            )
    return total


def same_kernel(core_ref, table_ref, amp_ref, own_ref, recv_ref, out_ref, weights_ref):
    core = core_ref[0]
    parity_weights(core, core, table_ref, amp_ref, weights_ref)
    out_ref[...] = parity_product(core, weights_ref, own_ref, recv_ref, 0.0, slice(None))


def crossed_kernel(core_ref, table_ref, amp_ref, own_ref, recv_ref, prev_ref, out_hbm, weights_ref, out_ref, sems):
    core = core_ref[0]
    parity_weights(1 - core, core, table_ref, amp_ref, weights_ref)
    tiles = sems.shape[0]
    wide = out_ref.shape[2] // tiles
    copies = []
    for tile in range(tiles):
        lanes = slice(tile * wide, (tile + 1) * wide)
        total = prev_ref[:, lanes]
        total = parity_product(1 - core, weights_ref, own_ref, recv_ref, total, lanes)
        out_ref[:, :, lanes] = total.astype(BF16).reshape(out_ref.shape[:2] + (wide,))
        copies.append(
            pltpu.make_async_copy(out_ref.at[:, :, lanes], out_hbm.at[:, :, lanes], sems.at[tile])
        )
        copies[tile].start()
    for copy in copies:
        copy.wait()


def chunk_plan(phi, loads, harm_diam, mistuning, dyn_diag, blade_order):
    rows_dev, half_modes = phi.shape
    local_diam = half_modes // MODES
    columns = loads.shape[1] // NHARM
    core = lax.axis_index("diam")
    own_diam = 2 * lax.axis_index("rows") + core
    first_diam = core * local_diam
    core_arg = core.reshape(1).astype(jnp.int32)
    pairs = local_diam // 2

    def other_core(value):
        return lax.ppermute(value, "diam", SWAP)

    def exchange(slots):
        return lax.all_to_all(slots, "rows", 0, 0, tiled=True, axis_index_groups=[ORDER])

    def row_total(got):
        return jnp.sum(got.astype(F32), axis=0)

    shapes = phi.T.reshape(local_diam, MODES, rows_dev)
    half_combined = jax.ShapeDtypeStruct((pairs, columns, rows_dev), BF16)
    half_shapes = jax.ShapeDtypeStruct((pairs, MODES, rows_dev), BF16)
    combined_send, combined_mine, shapes_send, shapes_mine = pl.pallas_call(
        functools.partial(load_kernel, columns),
        name="load",
        in_specs=[SMEM, HBM, HBM, HBM],
        out_specs=[VMEM] * 4,
        out_shape=[half_combined, half_combined, half_shapes, half_shapes],
        scratch_shapes=[
            pltpu.SMEM(harm_diam.shape, jnp.int32),
            pltpu.VMEM(loads.shape, BF16),
            pltpu.SemaphoreType.DMA((4,)),
        ],
        compiler_params=LIMIT,
    )(core_arg, *in_hbm(harm_diam, loads, shapes.reshape(pairs, 2, MODES, rows_dev)))

    def force_part(combined, near):
        return jnp.einsum("hcr,hmr->hcm", combined, near, preferred_element_type=F32).astype(BF16)

    force_recv = other_core(force_part(combined_send, shapes_send))
    slots_shape = (local_diam,) + PACKED
    force_slots = pl.pallas_call(
        assemble_kernel,
        name="assemble",
        in_specs=[SMEM, VMEM, VMEM],
        out_specs=VMEM,
        out_shape=jax.ShapeDtypeStruct(slots_shape, BF16),
        compiler_params=LIMIT,
    )(core_arg, force_part(combined_mine, shapes_mine), force_recv)
    force_slots, stiff, order, dyn_diag = lax.optimization_barrier(
        (force_slots, mistuning.T, blade_order, dyn_diag)
    )
    force_got = exchange(force_slots)

    group = jax.ShapeDtypeStruct((2, pairs, MODES, MODES), BF16)
    keep, sent = pl.pallas_call(
        regroup_kernel,
        name="regroup",
        in_specs=[SMEM, HBM],
        out_specs=[VMEM, VMEM],
        out_shape=[group, group],
        scratch_shapes=[
            pltpu.VMEM(stiff.shape, F32),
            pltpu.SemaphoreType.DMA((4,)),
        ],
        compiler_params=WIDE,
        cost_estimate=pl.CostEstimate(
            flops=2 * mistuning.size, bytes_accessed=8 * mistuning.size, transcendentals=0
        ),
    )(core_arg, *in_hbm(stiff))
    recv = other_core(sent)
    table = lax.dynamic_slice_in_dim(cyclic_rows(order), first_diam, local_diam, 0)
    table = jnp.broadcast_to(table.T[:, :, None], (NBLADE, local_diam, MODES))
    dyn_own = pl.pallas_call(
        functools.partial(pack_kernel, columns),
        name="pack",
        in_specs=[VMEM],
        out_specs=VMEM,
        out_shape=jax.ShapeDtypeStruct(PACKED, F32),
        compiler_params=LIMIT,
        cost_estimate=pl.CostEstimate(flops=1, bytes_accessed=1, transcendentals=0),
    )(lax.dynamic_slice_in_dim(dyn_diag, own_diam * MODES, MODES, 0)[None, :])
    force_got, keep, table, dyn_own = lax.optimization_barrier((force_got, keep, table, dyn_own))

    def product(source, *operands):
        return pl.pallas_call(
            functools.partial(product_kernel, source),
            name="product",
            in_specs=[SMEM] + [VMEM] * len(operands),
            out_specs=VMEM,
            out_shape=jax.ShapeDtypeStruct(slots_shape, BF16 if source else F32),
            compiler_params=LIMIT,
        )(core_arg, *operands)

    force = row_total(force_got)
    amp = force / dyn_own
    for sweep in range(ITERS):
        amp_low = amp.astype(BF16)
        amp_other = other_core(amp_low)
        part = product(0, amp_low, keep, recv)
        part, amp_other = lax.optimization_barrier((part, amp_other))
        if sweep == ITERS - 1:
            part, shapes_sent = lax.optimization_barrier((part, shapes))
            shapes_received = other_core(shapes_sent)
        part = product(1, amp_other, keep, recv, part)
        amp = (force - row_total(exchange(part))) / dyn_own
    same = exchange(jnp.broadcast_to(amp.astype(BF16)[None], slots_shape))
    crossed = other_core(same)

    half_cost = pl.CostEstimate(
        flops=2 * local_diam * columns * phi.size, bytes_accessed=2 * phi.size, transcendentals=0
    )
    weights = pltpu.VMEM((local_diam, local_diam * columns, MODES), BF16)
    part = pl.pallas_call(
        same_kernel,
        name="blades_same",
        in_specs=[SMEM] + [VMEM] * 4,
        out_specs=VMEM,
        out_shape=jax.ShapeDtypeStruct((local_diam * columns, rows_dev), F32),
        scratch_shapes=[weights],
        compiler_params=WIDE,
        cost_estimate=half_cost,
    )(core_arg, table, same, shapes_sent, shapes_received)
    part, crossed = lax.optimization_barrier((part, crossed))
    out_shape = (local_diam, columns, rows_dev)
    return pl.pallas_call(
        crossed_kernel,
        name="blades_crossed",
        in_specs=[SMEM] + [VMEM] * 5,
        out_specs=HBM,
        out_shape=jax.ShapeDtypeStruct(out_shape, BF16),
        scratch_shapes=[weights, pltpu.VMEM(out_shape, BF16), pltpu.SemaphoreType.DMA((2,))],
        compiler_params=WIDE,
        cost_estimate=half_cost,
    )(core_arg, table, crossed, shapes_sent, shapes_received, part)


def solution(mesh):
    placed = (P("rows", "diam"), P("rows", None), P(), P("diam", "rows"), P("grp"), P())
    one_each = mesh.shape["rows"] * 2 == NBLADE and mesh.shape["diam"] == 2
    return jax.shard_map(
        chunk_plan if one_each else general_plan,
        mesh=mesh,
        in_specs=placed,
        out_specs=P("diam", "grp", "rows"),
        check_vma=False,
    )
```
